128 devices in a mesh: grp: 8 (over y, core), tok: 16 (over z, x).
Axes of the slice: x: 4, y: 4, z: 4, core: 2. Of those that a mesh axis runs over, the one named last changes fastest.
Arguments:
- pre_q: bfloat16 [8192, 4096], P(('grp', 'tok')), may hold values from -64 to 64
- pre_kv: bfloat16 [8192, 2048], P(('grp', 'tok')), may hold values from -8 to 8
- pre_segment: int32 [8, 1024], P('grp'), may hold values from 0 to 3, never falling along the last dimension, each value on 1 to 512 neighbouring positions
- dec_q: bfloat16 [128, 4096], P(('grp', 'tok')), may hold values from -64 to 64
- cache: bfloat16 [128, 512, 2048], P(('grp', 'tok')), may hold values from -8 to 8
- cache_len: int32 [128], P(('grp', 'tok')), may hold values from 1 to 512, 32768 in all
- slot_request: int32 [128], replicated, may hold values from 0 to 127, each once
- resid: bfloat16 [8320, 4096], P('grp', 'tok'), may hold values from -64 to 64
- wo: bfloat16 [4096, 4096], P(None, 'tok'), may hold values from -0.5 to 0.5
- tenant: int32 [8, 1040], P('grp'), may hold values from 0 to 3, never falling along the last dimension, each value on 1 to 520 neighbouring positions
- norm_gain: float32 [4, 4096], replicated, may hold values from 0.25 to 1.75
- w_gate: bfloat16 [4096, 12288], P(None, 'tok'), may hold values from -0.09375 to 0.09375
- w_up: bfloat16 [4096, 12288], P(None, 'tok'), may hold values from -0.09375 to 0.09375
- w_down: bfloat16 [12288, 4096], P('tok'), may hold values from -0.0546875 to 0.0546875
Outputs:
- out: bfloat16 [8320, 4096], P('grp', 'tok')
The draws below stay inside these ranges and needn't reach their ends.
All inputs are finite; a program needn't handle non-finite values. No bound on the sum of `cache_len` on one device may be relied on, other than what follows from the above.
Results may differ from the reference program's by a relative error of at most 0.011.
Values may be sent and summed in bfloat16 or wider, within the bound.
A program may use at most 128 MiB of HBM per device.

```python
import math
import jax
import jax.numpy as jnp
import numpy as np
from jax import lax

D = 4096
H = 32
KVH = 8
HD = 128
FFW = 12288
TENANTS = 4
PRE_DEV = 64
CMAX = 512
PB = 1024
GT = 1040
TOKENS = 8320
PRE = 8192
DEC = 128
SEG_CNT = 4
SEG_MOST = 512
N_GRP = 8
N_TOK = 16


def prefill_pair(key):
    query_key = jax.random.fold_in(key, 101)
    pair_key = jax.random.fold_in(key, 102)
    width = KVH * HD
    queries = jnp.clip(jax.random.normal(query_key, (PRE, D), jnp.float32), -6.0, 6.0)
    pairs = jnp.clip(jax.random.normal(pair_key, (PRE, 2 * width), jnp.float32), -6.0, 6.0)
    return (queries, pairs)


def draw_pre_q(key, part):
    return prefill_pair(key)[0].astype(jnp.bfloat16)


def draw_pre_kv(key, part):
    return prefill_pair(key)[1].astype(jnp.bfloat16)


def decode_pair(key):
    query_key = jax.random.fold_in(key, 201)
    cache_key = jax.random.fold_in(key, 202)
    width = KVH * HD
    queries = jnp.clip(jax.random.normal(query_key, (DEC, D), jnp.float32), -6.0, 6.0)
    entries = jnp.clip(jax.random.normal(cache_key, (DEC, CMAX, 2 * width), jnp.float32), -6.0, 6.0)
    return (queries, entries)


def draw_dec_q(key, part):
    return decode_pair(key)[0].astype(jnp.bfloat16)


def draw_cache(key, part):
    return decode_pair(key)[1].astype(jnp.bfloat16)


def draw_resid(key, part):
    base_key = jax.random.fold_in(key, 301)
    row_key = jax.random.fold_in(key, 302)
    column_key = jax.random.fold_in(key, 303)
    base = jnp.clip(jax.random.normal(base_key, (TOKENS, D), jnp.float32), -6.0, 6.0)
    row_scale = jnp.exp(jax.random.uniform(row_key, (TOKENS, 1), jnp.float32, 0.0, math.log(10.0)))
    rising = math.log(3.0) * jnp.arange(D).astype(jnp.float32)[None, :] / D
    column_scale = jnp.exp(jax.random.uniform(column_key, (1, D), jnp.float32, 0.0, math.log(4.0)) + rising)
    return (0.08 * base * row_scale * column_scale).astype(jnp.bfloat16)


def level_of(stream_key, extent, pieces, least, high):
    def one(axis_at, blocks):
        heights = jax.random.uniform(jax.random.fold_in(jax.random.fold_in(stream_key, 6), axis_at), (blocks,), jnp.float32, least / len(pieces), high / len(pieces))
        return jnp.repeat(jnp.exp(heights), extent[axis_at] // blocks).reshape((-1,) + (1,) * (len(extent) - axis_at - 1))

    loudness = one(*pieces[0])
    for cut in pieces[1:]:
        loudness = loudness * one(*cut)
    return loudness


def profile(amount, total, most, skew):
    loads = [(1 << 20) // math.isqrt(standing ** skew) + 1 for standing in range(2, amount + 1)]
    rest, counts = total - most - (amount - 1), [1] * (amount - 1)
    while rest > 0:
        free = [i for i in range(amount - 1) if counts[i] < most]
        whole, left = sum([loads[i] for i in free]), rest
        for i in free:
            more = min(most - counts[i], max(1, left * loads[i] // whole), rest)
            counts[i] = counts[i] + more
            rest = rest - more
    return np.array([most] + counts)


def uneven_parts(stream_key, amount, total, limit, skew):
    if amount == 2:
        one = jax.random.randint(stream_key, (), max(1, total - limit), min(limit, total - 1) + 1)
        return jnp.stack([one, total - one])
    sizes = jnp.asarray(profile(amount, total, limit, skew), jnp.int32)
    couples = (amount - 1) // 2
    source_of, taker = sizes[1:1 + 2 * couples:2], sizes[2:2 + 2 * couples:2]
    slack = jnp.minimum(source_of - 1, limit - taker)
    passed = jax.random.randint(jax.random.fold_in(stream_key, 1), (couples,), 0, 1 << 20) % (slack + 1)
    sizes = sizes.at[1:1 + 2 * couples:2].set(source_of - passed).at[2:2 + 2 * couples:2].set(taker + passed)
    return sizes[jax.random.permutation(jax.random.fold_in(stream_key, 2), amount)]


def noise(own_key, dims, spread, most, split=(), held_as=jnp.bfloat16):
    values = jax.random.normal(own_key, dims, jnp.float32) * spread
    if len(split) > 0:
        values = level_of(own_key, dims, split, -0.22, 0.18) * values
    return jnp.clip(values, min=-most, max=most).astype(held_as)


def setup_inputs(seed: int = 0) -> dict:
    arg_keys = jax.random.split(jax.random.key(seed), 15)
    pre_q = draw_pre_q(jax.random.fold_in(arg_keys[14], 71), 0)
    pre_kv = draw_pre_kv(jax.random.fold_in(arg_keys[14], 71), 0)
    pre_segment = jax.vmap(lambda own: jnp.searchsorted(jnp.cumsum(uneven_parts(own, SEG_CNT, PB, SEG_MOST, 0)), jnp.arange(PB), side="right"))(jax.random.split(arg_keys[2], N_GRP)).reshape((N_GRP, PB)).astype(jnp.int32)
    dec_q = draw_dec_q(jax.random.fold_in(arg_keys[14], 71), 0)
    cache = draw_cache(jax.random.fold_in(arg_keys[14], 71), 0)
    cache_len = uneven_parts(arg_keys[5], DEC, DEC * CMAX // 2, CMAX, 2).astype(jnp.int32)
    slot_request = jax.random.permutation(arg_keys[6], DEC).astype(jnp.int32)
    resid = draw_resid(jax.random.fold_in(arg_keys[14], 71), 0)
    wo = noise(arg_keys[8], (D, D), HD ** -0.5, 0.5, ((1, 16),))
    tenant = jax.vmap(lambda own: jnp.searchsorted(jnp.cumsum(uneven_parts(own, TENANTS, GT, GT // 2, 0)), jnp.arange(GT), side="right"))(jax.random.split(arg_keys[9], N_GRP)).reshape((N_GRP, GT)).astype(jnp.int32)
    norm_gain = jnp.clip(1.0 + 0.15 * jax.random.normal(arg_keys[10], (TENANTS, D), jnp.float32), 0.25, 1.75)
    w_gate = noise(arg_keys[11], (D, FFW), D ** -0.5, 0.09375, ((1, 16),))
    w_up = noise(arg_keys[12], (D, FFW), D ** -0.5, 0.09375, ((1, 16),))
    w_down = noise(arg_keys[13], (FFW, D), FFW ** -0.5, 0.0546875, ((0, 16),))
    return {"pre_q": pre_q, "pre_kv": pre_kv, "pre_segment": pre_segment, "dec_q": dec_q, "cache": cache, "cache_len": cache_len, "slot_request": slot_request, "resid": resid, "wo": wo, "tenant": tenant, "norm_gain": norm_gain, "w_gate": w_gate, "w_up": w_up, "w_down": w_down}


epsilon = 1e-05

def prefill_group(inputs):
    queries, pairs, segment = inputs
    group = H // KVH
    positions = jnp.arange(PB)
    allowed = (positions[None, :] <= positions[:, None]) & (segment[None, :] == segment[:, None])
    queries = queries.reshape(PB, KVH, group, HD).transpose(1, 0, 2, 3).astype(jnp.float32)
    keys = pairs[:, :KVH * HD].reshape(PB, KVH, HD).transpose(1, 0, 2).astype(jnp.float32)
    values = pairs[:, KVH * HD:].reshape(PB, KVH, HD).transpose(1, 0, 2).astype(jnp.float32)

    def one_head(head_inputs):
        query_head, key_head, value_head = head_inputs
        scores = jnp.einsum('qgd,nd->gqn', query_head, key_head) / math.sqrt(HD)
        masked = jnp.where(allowed[None], scores, -jnp.inf)
        highest = lax.optimization_barrier(jnp.max(masked, axis=-1, keepdims=True))
        weights = jnp.exp(masked - highest).astype(jnp.bfloat16)
        weights = lax.optimization_barrier(weights).astype(jnp.float32)
        totals = lax.optimization_barrier(jnp.sum(weights, axis=-1))
        mixed = jnp.einsum('gqn,nd->gqd', weights, value_head)
        return mixed / totals[..., None]
    heads_out = lax.map(one_head, (queries, keys, values))
    return heads_out.transpose(2, 0, 1, 3).reshape(PB, D).astype(jnp.bfloat16)

def decode_slot(inputs):
    query, entries, length = inputs
    group = H // KVH
    query = query.reshape(KVH, group, HD).astype(jnp.float32)
    keys = entries[:, :KVH * HD].reshape(CMAX, KVH, HD).astype(jnp.float32)
    values = entries[:, KVH * HD:].reshape(CMAX, KVH, HD).astype(jnp.float32)
    scores = jnp.einsum('kgd,pkd->kgp', query, keys) / math.sqrt(HD)
    visible = jnp.arange(CMAX) < length
    masked = jnp.where(visible, scores, -jnp.inf)
    highest = lax.optimization_barrier(jnp.max(masked, axis=-1, keepdims=True))
    weights = jnp.exp(masked - highest).astype(jnp.bfloat16)
    weights = lax.optimization_barrier(weights).astype(jnp.float32)
    totals = lax.optimization_barrier(jnp.sum(weights, axis=-1))
    mixed = jnp.einsum('kgp,pkd->kgd', weights, values)
    return (mixed / totals[..., None]).reshape(D).astype(jnp.bfloat16)

def reference(pre_q, pre_kv, pre_segment, dec_q, cache, cache_len, slot_request, resid, wo, tenant, norm_gain, w_gate, w_up, w_down):
    prefill_att = lax.map(prefill_group, (pre_q.reshape(N_GRP, PB, D), pre_kv.reshape(N_GRP, PB, 2 * KVH * HD), pre_segment))
    prefill_att = prefill_att.reshape(N_GRP, N_TOK, PRE_DEV, D)
    slot_queries = dec_q[slot_request.astype(jnp.int32)]
    decode_att = lax.map(decode_slot, (slot_queries, cache, cache_len)).reshape(N_GRP, N_TOK, 1, D)
    attention = jnp.concatenate([prefill_att, decode_att], axis=2).reshape(TOKENS, D)
    mixed_in = (resid.astype(jnp.float32) + jnp.dot(attention, wo, preferred_element_type=jnp.float32)).astype(jnp.bfloat16)

    def feed_group(inputs):
        rows_in, owners = inputs
        wide = rows_in.astype(jnp.float32)
        mean_square = lax.optimization_barrier(jnp.mean(wide * wide, axis=-1, keepdims=True))
        one_hot = (owners[:, None] == jnp.arange(TENANTS)[None, :]).astype(jnp.float32)
        gains = jnp.dot(one_hot, norm_gain, precision=lax.Precision.HIGHEST)
        normed = (wide * lax.rsqrt(mean_square + epsilon) * gains).astype(jnp.bfloat16)
        gate_part = jnp.dot(normed, w_gate, preferred_element_type=jnp.float32)
        lift_part = jnp.dot(normed, w_up, preferred_element_type=jnp.float32)
        hidden = (jax.nn.silu(gate_part) * lift_part).astype(jnp.bfloat16)
        return (wide + jnp.dot(hidden, w_down, preferred_element_type=jnp.float32)).astype(jnp.bfloat16)
    result = lax.map(feed_group, (mixed_in.reshape(N_GRP, GT, D), tenant))
    return result.reshape(TOKENS, D)
```

```python
import functools
import math

import jax
import jax.numpy as jnp
from jax import lax
from jax.experimental import pallas as pl
from jax.experimental.pallas import tpu as pltpu
from jax.sharding import PartitionSpec as P

D = 4096
H = 32
KVH = 8
HD = 128
SIDE = 4
PEERS = SIDE * SIDE
BLOCK = D // PEERS
HALF = BLOCK // 2
WIDE = D // 2
SUB = 16
SPLIT = 112
CHUNKS = 5

epsilon = 1e-05
MESH = pl.DeviceIdType.MESH


def ring_kernel(
    att_ref,
    dec_ref,
    resid_ref,
    tenant_ref,
    gain_ref,
    wo_hbm,
    wg_hbm,
    wu_hbm,
    wd_hbm,
    out_ref,
    abuf,
    dbuf,
    xbuf,
    pbuf,
    mixed,
    normed,
    hidden,
    r1,
    r2,
    r3,
    r4,
    wo_ref,
    wg_ref,
    wu_ref,
    wd_ref,
    w_sem,
    a_send,
    a_recv,
    d_send,
    d_recv,
    x_send,
    x_recv,
    p_send,
    p_recv,
):
    me = lax.axis_index("tok")
    z, x = me // SIDE, me % SIDE
    rows = resid_ref.shape[0] // CHUNKS
    tiles = rows // SUB
    att_chunks = att_ref.shape[0] // SUB
    ffw = wg_ref.shape[1]
    parts = ((0, SPLIT), (SPLIT, rows - SPLIT))

    def hop(value, step):
        return lax.rem(value + step + SIDE, SIDE)

    def neighbour(axis, step):
        if axis == 0:
            return z * SIDE + hop(x, step)
        return hop(z, step) * SIDE + x

    def send(src, dst, sends, recvs, chunk, index, peer):
        return pltpu.make_async_remote_copy(
            src_ref=src,
            dst_ref=dst,
            send_sem=sends.at[chunk, index],
            recv_sem=recvs.at[chunk, index],
            device_id={"tok": peer},
            device_id_type=MESH,
        )

    def slot(level, half, way):
        return level * 4 + half * 2 + way

    steps = (1, -1)

    def row_span(chunk, part=None):
        base = chunk * rows
        if part is None:
            return pl.ds(pl.multiple_of(base, SUB), rows)
        return pl.ds(pl.multiple_of(base + parts[part][0], SUB), parts[part][1])

    def lanes(base, size):
        return pl.ds(pl.multiple_of(base, HALF), size)

    def near_lanes(half, offset):
        if half == 0:
            return lanes(z * 4 * HALF + hop(x, offset) * HALF, HALF)
        return lanes(WIDE + x * 4 * HALF + hop(z, offset) * HALF, HALF)

    def far_lanes(half, offset):
        if half == 0:
            return lanes(hop(z, offset) * 4 * HALF, 4 * HALF)
        return lanes(WIDE + hop(x, offset) * 4 * HALF, 4 * HALF)

    def a_cols(half, part):
        if part is None:
            return pl.ds(half * WIDE, WIDE)
        return pl.ds(half * WIDE + part * (WIDE // 2), WIDE // 2)

    def a_near(chunk, half, offset, part=None):
        if half == 0:
            return abuf.at[chunk * SIDE + z, hop(x, offset), :, a_cols(half, part)]
        return abuf.at[chunk * SIDE + hop(z, offset), x, :, a_cols(half, part)]

    def a_far(chunk, half, offset, part=None):
        if half == 0:
            return abuf.at[chunk * SIDE + hop(z, offset), :, :, a_cols(half, part)]
        return abuf.at[pl.ds(chunk * SIDE, SIDE), hop(x, offset), :, a_cols(half, part)]

    def x_near(chunk, half, offset, part=None):
        return xbuf.at[row_span(chunk, part), near_lanes(half, offset)]

    def x_far(chunk, half, offset, part=None):
        return xbuf.at[row_span(chunk, part), far_lanes(half, offset)]

    def gather_copy(near, far, sends, recvs, chunk, level, half, way, arriving):
        step = steps[way]
        axis = half if level < 2 else 1 - half
        block = near if level < 2 else far
        if level % 2 == 0:
            ref = block(chunk, half, -step if arriving else 0)
        else:
            ref = block(chunk, half, -2 * step if arriving else -step, way)
        return send(ref, ref, sends, recvs, chunk, slot(level, half, way), neighbour(axis, step))

    def gather_start(near, far, sends, recvs, chunk, level):
        for half in (0, 1):
            for way in (0, 1):
                gather_copy(near, far, sends, recvs, chunk, level, half, way, False).start()

    def gather_wait(near, far, sends, recvs, chunk, level):
        for half in (0, 1):
            for way in (0, 1):
                gather_copy(near, far, sends, recvs, chunk, level, half, way, True).wait_recv()

    def gather_sent(near, far, sends, recvs, chunk, level):
        for half in (0, 1):
            for way in (0, 1):
                gather_copy(near, far, sends, recvs, chunk, level, half, way, False).wait_send()

    a_args = (a_near, a_far, a_send, a_recv)
    x_args = (x_near, x_far, x_send, x_recv)

    def gather_step(args, chunk, level):
        gather_wait(*args, chunk, level)
        if level < 3:
            gather_start(*args, chunk, level + 1)

    def part_rows(part):
        return pl.ds(parts[part][0], parts[part][1])

    def scatter_copy(chunk, level, half, way):
        step = steps[way]
        axis = 1 - half if level < 2 else half
        if level == 0:
            src = pbuf.at[row_span(chunk, way), far_lanes(half, 2)]
            dst = r1.at[chunk, half, part_rows(way), :]
        elif level == 1:
            src = pbuf.at[row_span(chunk), far_lanes(half, step)]
            dst = r2.at[chunk, half, way]
        elif level == 2:
            src = pbuf.at[row_span(chunk, way), near_lanes(half, 2)]
            dst = r3.at[chunk, half, part_rows(way), :]
        else:
            src = pbuf.at[row_span(chunk), near_lanes(half, step)]
            dst = r4.at[chunk, half, way]
        return send(src, dst, p_send, p_recv, chunk, slot(level, half, way), neighbour(axis, step))

    def scatter_start(chunk, level):
        for half in (0, 1):
            for way in (0, 1):
                scatter_copy(chunk, level, half, way).start()

    def wide(value):
        return value.astype(jnp.float32)

    def scatter_step(chunk, level):
        for half in (0, 1):
            for way in (0, 1):
                scatter_copy(chunk, level, half, way).wait_recv()
            if level % 2 == 0:
                for way in (0, 1):
                    cols = (far_lanes if level == 0 else near_lanes)(half, steps[way])
                    landed = (r1 if level == 0 else r3)[chunk, half, part_rows(way), :]
                    span = row_span(chunk, way)
                    pbuf[span, cols] = (wide(pbuf[span, cols]) + wide(landed)).astype(jnp.bfloat16)
                    scatter_copy(chunk, level + 1, half, way).start()
            elif level == 1:
                cols, span = far_lanes(half, 0), row_span(chunk)
                total = wide(pbuf[span, cols]) + wide(r2[chunk, half, 0]) + wide(r2[chunk, half, 1])
                pbuf[span, cols] = total.astype(jnp.bfloat16)
                for way in (0, 1):
                    scatter_copy(chunk, 2, half, way).start()
            else:
                span = row_span(chunk)
                own = pl.ds(half * HALF, HALF)
                total = (
                    wide(pbuf[span, near_lanes(half, 0)])
                    + wide(r4[chunk, half, 0])
                    + wide(r4[chunk, half, 1])
                )
                out_ref[span, own] = (wide(mixed[span, own]) + total).astype(jnp.bfloat16)

    def scatter_sent(chunk, level):
        for half in (0, 1):
            for way in (0, 1):
                scatter_copy(chunk, level, half, way).wait_send()

    def dec_copy(k, arriving):
        other = lax.rem(me + k, PEERS)
        return pltpu.make_async_remote_copy(
            src_ref=dec_ref,
            dst_ref=dbuf.at[lax.rem(me - k + PEERS, PEERS) if arriving else me],
            send_sem=d_send.at[k],
            recv_sem=d_recv.at[k],
            device_id={"tok": other},
            device_id_type=MESH,
        )

    def project(chunk):
        first = chunk * tiles
        piece = jnp.concatenate(
            [abuf[(first + t) // SIDE, (first + t) % SIDE] for t in range(tiles)], axis=0
        )
        span = row_span(chunk)
        total = jnp.dot(piece, wo_ref[...], preferred_element_type=jnp.float32)
        value = (wide(resid_ref[span, :]) + total).astype(jnp.bfloat16)
        mixed[span, :] = value
        xbuf[span, near_lanes(0, 0)] = value[:, :HALF]
        xbuf[span, near_lanes(1, 0)] = value[:, HALF:]

    def normalize(chunk):
        @pl.loop(0, tiles)
        def _(t):
            span = pl.ds(pl.multiple_of(chunk * rows + t * SUB, SUB), SUB)
            total = jnp.zeros((SUB, HALF), jnp.float32)
            for block in range(D // HALF):
                value = wide(xbuf[span, block * HALF : (block + 1) * HALF])
                total = total + value * value
            scale = lax.rsqrt(jnp.sum(total, axis=-1, keepdims=True) / D + epsilon)
            owner = tenant_ref[span, :]
            to = pl.ds(pl.multiple_of(t * SUB, SUB), SUB)
            for block in range(D // HALF):
                cols = slice(block * HALF, (block + 1) * HALF)
                gain = gain_ref[3:4, cols]
                for k in (2, 1, 0):
                    gain = jnp.where(owner == k, gain_ref[k : k + 1, cols], gain)
                normed[to, cols] = (wide(xbuf[span, cols]) * scale * gain).astype(jnp.bfloat16)

    def lift(tile, width):
        cols = slice(tile * width, (tile + 1) * width)
        gate = jnp.dot(normed[...], wg_ref[:, cols], preferred_element_type=jnp.float32)
        up = jnp.dot(normed[...], wu_ref[:, cols], preferred_element_type=jnp.float32)
        hidden[:, cols] = (gate / (1.0 + jnp.exp(-gate)) * up).astype(jnp.bfloat16)

    def lower(chunk, width):
        @pl.loop(0, D // width)
        def _(tile):
            cols = pl.ds(pl.multiple_of(tile * width, width), width)
            part = jnp.dot(hidden[...], wd_ref[:, cols], preferred_element_type=jnp.float32)
            pbuf[row_span(chunk), cols] = part.astype(jnp.bfloat16)

    barrier = pltpu.get_barrier_semaphore()

    @pl.loop(1, PEERS)
    def _(k):
        pl.semaphore_signal(
            barrier, inc=1, device_id={"tok": lax.rem(me + k, PEERS)}, device_id_type=MESH
        )

    fetch_wo = pltpu.make_async_copy(wo_hbm, wo_ref, w_sem.at[0])
    fetch_wo.start()

    @pl.loop(0, att_chunks)
    def _(chunk):
        abuf[chunk * SIDE + z, x] = att_ref[pl.ds(pl.multiple_of(chunk * SUB, SUB), SUB), :]

    dbuf[me] = dec_ref[...]
    pl.semaphore_wait(barrier, PEERS - 1)

    @pl.loop(0, att_chunks)
    def _(chunk):
        gather_start(*a_args, chunk, 0)

    @pl.loop(1, PEERS)
    def _(k):
        dec_copy(k, False).start()

    @pl.loop(0, PEERS)
    def _(t):
        for half in (0, 1):
            source = pl.ds(pl.multiple_of(t * BLOCK + half * HALF, HALF), HALF)
            if half == 0:
                place = t * HALF
            else:
                place = WIDE + (t % SIDE) * (SIDE * HALF) + (t // SIDE) * HALF
            target = pl.ds(pl.multiple_of(place, HALF), HALF)
            pltpu.make_async_copy(wg_hbm.at[source, :], wg_ref.at[target, :], w_sem.at[1]).start()
            pltpu.make_async_copy(wu_hbm.at[source, :], wu_ref.at[target, :], w_sem.at[2]).start()
            pltpu.make_async_copy(wd_hbm.at[:, source], wd_ref.at[:, target], w_sem.at[3]).start()

    width = 256

    @pl.loop(0, CHUNKS + 3)
    def _(s):
        att_on = s < att_chunks
        x_on = jnp.logical_and(s >= 1, s < CHUNKS + 1)
        f_on = jnp.logical_and(s >= 2, s < CHUNKS + 2)
        p_on = s >= 3

        def progress(level):
            @pl.when(att_on)
            def _():
                gather_step(a_args, s, level)

            @pl.when(x_on)
            def _():
                gather_step(x_args, s - 1, level)

            @pl.when(p_on)
            def _():
                scatter_step(s - 3, level)

        @pl.when(s == 2)
        def _():
            pltpu.make_async_copy(wg_ref, wg_ref, w_sem.at[1]).wait()
            pltpu.make_async_copy(wu_ref, wu_ref, w_sem.at[2]).wait()
            pltpu.make_async_copy(wd_ref, wd_ref, w_sem.at[3]).wait()

        @pl.when(f_on)
        def _():
            normalize(s - 2)

        progress(0)

        @pl.when(f_on)
        def _():
            lift(0, width)

        progress(1)

        @pl.when(f_on)
        def _():
            for tile in range(1, ffw // width):
                lift(tile, width)

        progress(2)

        @pl.when(f_on)
        def _():
            lower(s - 2, 512)
            scatter_start(s - 2, 0)

        progress(3)

        @pl.when(s == 0)
        def _():
            fetch_wo.wait()

        @pl.when(s == CHUNKS - 1)
        def _():
            @pl.loop(1, PEERS)
            def _(k):
                dec_copy(k, True).wait_recv()

            for head in range(H):
                abuf[att_chunks * SIDE, 0, :, head * HD : (head + 1) * HD] = dbuf[
                    :, head, :
                ].astype(jnp.bfloat16)

        @pl.when(s < CHUNKS)
        def _():
            project(s)
            gather_start(*x_args, s, 0)

    @pl.loop(1, PEERS)
    def _(k):
        dec_copy(k, False).wait_send()

    @pl.loop(0, att_chunks)
    def _(chunk):
        for level in range(4):
            gather_sent(*a_args, chunk, level)

    @pl.loop(0, CHUNKS)
    def _(chunk):
        for level in range(4):
            gather_sent(*x_args, chunk, level)
            scatter_sent(chunk, level)


def ring_call(att, dec, resid, owner, gains, wo, w_gate, w_up, w_down):
    tokens = resid.shape[0]
    rows = tokens // CHUNKS
    ffw = w_gate.shape[1]
    vmem = pl.BlockSpec(memory_space=pltpu.VMEM)
    hbm = pl.BlockSpec(memory_space=pl.ANY)
    bf16 = jnp.bfloat16
    dma = pltpu.SemaphoreType.DMA
    return pl.pallas_call(
        ring_kernel,
        out_shape=jax.ShapeDtypeStruct((tokens, BLOCK), bf16),
        in_specs=[vmem] * 5 + [hbm] * 4,
        out_specs=vmem,
        scratch_shapes=[
            pltpu.VMEM((SIDE * SIDE + 1, SIDE, SUB, D), bf16),
            pltpu.VMEM((PEERS, H, HD), jnp.float32),
            pltpu.VMEM((tokens, D), bf16),
            pltpu.VMEM((tokens, D), bf16),
            pltpu.VMEM((tokens, BLOCK), bf16),
            pltpu.VMEM((rows, D), bf16),
            pltpu.VMEM((rows, ffw), bf16),
            pltpu.VMEM((CHUNKS, 2, rows, 4 * HALF), bf16),
            pltpu.VMEM((CHUNKS, 2, 2, rows, 4 * HALF), bf16),
            pltpu.VMEM((CHUNKS, 2, rows, HALF), bf16),
            pltpu.VMEM((CHUNKS, 2, 2, rows, HALF), bf16),
            pltpu.VMEM(wo.shape, bf16),
            pltpu.VMEM(w_gate.shape, bf16),
            pltpu.VMEM(w_up.shape, bf16),
            pltpu.VMEM(w_down.shape, bf16),
            dma((4,)),
            dma((CHUNKS, 16)),
            dma((CHUNKS, 16)),
            dma((PEERS,)),
            dma((PEERS,)),
            dma((CHUNKS, 16)),
            dma((CHUNKS, 16)),
            dma((CHUNKS, 16)),
            dma((CHUNKS, 16)),
        ],
        compiler_params=pltpu.CompilerParams(
            collective_id=1, has_side_effects=True, vmem_limit_bytes=67000000
        ),
        name="ring_layer",
    )(att, dec, resid, owner, gains, wo, w_gate, w_up, w_down)


def grouped(rows, blocks):
    count = rows.shape[0] // blocks
    rest = rows.shape[1:]
    split = rows.reshape(blocks, count, *rest)
    main = split[:, : count - 1].reshape(blocks, (count - 1) // SUB, SUB, *rest)
    main = jnp.swapaxes(main, 0, 1).reshape(blocks * (count - 1), *rest)
    return jnp.concatenate([main, split[:, count - 1]], axis=0)


def ungrouped(rows, blocks):
    count = rows.shape[0] // blocks
    rest = rows.shape[1:]
    main = rows[: blocks * (count - 1)].reshape((count - 1) // SUB, blocks, SUB, *rest)
    main = jnp.swapaxes(main, 0, 1).reshape(blocks, count - 1, *rest)
    last = rows[blocks * (count - 1) :].reshape(blocks, 1, *rest)
    return jnp.concatenate([main, last], axis=1).reshape(blocks * count, *rest)


def shards(
    pre_q,
    pre_kv,
    pre_segment,
    dec_q,
    cache,
    cache_len,
    slot_request,
    resid,
    wo,
    tenant,
    norm_gain,
    w_gate,
    w_up,
    w_down,
):
    group = H // KVH
    width = KVH * HD
    tok_index = lax.axis_index("tok")
    local_rows = pre_q.shape[0]
    segment = pre_segment[0]
    query_pos = tok_index * local_rows + jnp.arange(local_rows)
    query_seg = lax.dynamic_slice_in_dim(segment, tok_index * local_rows, local_rows)
    queries = pre_q.reshape(local_rows, KVH, group, HD)
    piece = lax.all_gather(pre_kv, "tok", axis=0, tiled=True)
    count = piece.shape[0]
    keys = piece[:, :width].reshape(count, KVH, HD)
    values = piece[:, width:].reshape(count, KVH, HD)
    key_pos = jnp.arange(count)
    allowed = (key_pos[None, :] <= query_pos[:, None]) & (segment[None, :] == query_seg[:, None])
    scores = jnp.einsum(
        "qkgd,nkd->kgqn", queries, keys, preferred_element_type=jnp.float32
    ) / math.sqrt(HD)
    scores = jnp.where(allowed, scores, -jnp.inf)
    highest = jnp.max(scores, axis=-1, keepdims=True)
    weights = jnp.exp(scores - highest).astype(jnp.bfloat16)
    totals = jnp.sum(weights.astype(jnp.float32), axis=-1)
    summed = jnp.einsum("kgqn,nkd->kgqd", weights, values, preferred_element_type=jnp.float32)
    prefill_out = (
        (summed / totals[..., None])
        .transpose(2, 0, 1, 3)
        .reshape(local_rows, D)
        .astype(jnp.bfloat16)
    )
    all_queries = lax.all_gather(dec_q, ("grp", "tok"), axis=0, tiled=True)
    slot = lax.axis_index(("grp", "tok"))
    request = slot_request[slot]
    query_row = lax.dynamic_slice_in_dim(all_queries, request, 1, 0).reshape(KVH, group, HD)
    positions = cache.shape[1]
    entries = cache[0].reshape(positions, 2, KVH, HD)
    slot_scores = jnp.einsum(
        "kgd,pkd->kgp", query_row, entries[:, 0], preferred_element_type=jnp.float32
    ) / math.sqrt(HD)
    visible = jnp.arange(positions) < cache_len[0]
    slot_scores = jnp.where(visible, slot_scores, -jnp.inf)
    slot_top = jnp.max(slot_scores, axis=-1, keepdims=True)
    slot_weights = jnp.exp(slot_scores - slot_top).astype(jnp.bfloat16)
    slot_total = jnp.sum(slot_weights.astype(jnp.float32), axis=-1)
    slot_mixed = jnp.einsum(
        "kgp,pkd->kgd", slot_weights, entries[:, 1], preferred_element_type=jnp.float32
    )
    decode_out = (slot_mixed / slot_total[..., None]).reshape(H, HD)

    blocks = lax.axis_size("tok")
    owner = grouped(tenant[0], blocks)
    owner = jnp.broadcast_to(owner[:, None], (owner.shape[0], HALF))
    pieces = norm_gain.reshape(-1, SIDE, SIDE, 2, HALF)
    first = pieces[:, :, :, 0].reshape(-1, WIDE)
    second = jnp.swapaxes(pieces[:, :, :, 1], 1, 2).reshape(-1, WIDE)
    gains = jnp.concatenate([first, second], axis=1)
    result = ring_call(
        prefill_out,
        decode_out,
        grouped(resid, blocks),
        owner,
        gains,
        wo,
        w_gate,
        w_up,
        w_down,
    )
    return ungrouped(result, blocks)


def solution(mesh):
    in_specs = (
        P(("grp", "tok"), None),
        P(("grp", "tok"), None),
        P("grp", None),
        P(("grp", "tok"), None),
        P(("grp", "tok"), None, None),
        P(("grp", "tok")),
        P(),
        P("grp", "tok"),
        P(None, "tok"),
        P("grp", None),
        P(),
        P(None, "tok"),
        P(None, "tok"),
        P("tok", None),
    )
    out_specs = P("grp", "tok")
    return jax.shard_map(shards, mesh=mesh, in_specs=in_specs, out_specs=out_specs, check_vma=False)
```

```python
import functools
import math

import jax
import jax.numpy as jnp
from jax import lax
from jax.experimental import pallas as pl
from jax.experimental.pallas import tpu as pltpu
from jax.sharding import PartitionSpec as P

D = 4096
H = 32
KVH = 8
HD = 128
SIDE = 4
PEERS = SIDE * SIDE
BLOCK = D // PEERS
HALF = BLOCK // 2
WIDE = D // 2
SUB = 16
SPLIT = 112
CHUNKS = 5

epsilon = 1e-05
MESH = pl.DeviceIdType.MESH


def ring_kernel(
    att_ref,
    dec_ref,
    resid_ref,
    tenant_ref,
    gain_ref,
    wo_hbm,
    wg_hbm,
    wu_hbm,
    wd_hbm,
    out_ref,
    abuf,
    dbuf,
    xbuf,
    pbuf,
    mixed,
    normed,
    hidden,
    r1,
    r2,
    r3,
    r4,
    wo_ref,
    wg_ref,
    wu_ref,
    wd_ref,
    w_sem,
    a_send,
    a_recv,
    d_send,
    d_recv,
    x_send,
    x_recv,
    p_send,
    p_recv,
):
    me = lax.axis_index("tok")
    z, x = me // SIDE, me % SIDE
    rows = resid_ref.shape[0] // CHUNKS
    tiles = rows // SUB
    att_chunks = att_ref.shape[0] // SUB
    ffw = wg_ref.shape[1]
    parts = ((0, SPLIT), (SPLIT, rows - SPLIT))

    def hop(value, step):
        return lax.rem(value + step + SIDE, SIDE)

    def neighbour(axis, step):
        if axis == 0:
            return z * SIDE + hop(x, step)
        return hop(z, step) * SIDE + x

    def send(src, dst, sends, recvs, chunk, index, peer):
        return pltpu.make_async_remote_copy(
            src_ref=src,
            dst_ref=dst,
            send_sem=sends.at[chunk, index],
            recv_sem=recvs.at[chunk, index],
            device_id={"tok": peer},
            device_id_type=MESH,
        )

    def slot(level, half, way):
        return level * 4 + half * 2 + way

    steps = (1, -1)

    def row_span(chunk, part=None):
        base = chunk * rows
        if part is None:
            return pl.ds(pl.multiple_of(base, SUB), rows)
        return pl.ds(pl.multiple_of(base + parts[part][0], SUB), parts[part][1])

    def lanes(base, size):
        return pl.ds(pl.multiple_of(base, HALF), size)

    def near_lanes(half, offset):
        if half == 0:
            return lanes(z * 4 * HALF + hop(x, offset) * HALF, HALF)
        return lanes(WIDE + x * 4 * HALF + hop(z, offset) * HALF, HALF)

    def far_lanes(half, offset):
        if half == 0:
            return lanes(hop(z, offset) * 4 * HALF, 4 * HALF)
        return lanes(WIDE + hop(x, offset) * 4 * HALF, 4 * HALF)

    def a_cols(half, part):
        if part is None:
            return pl.ds(half * WIDE, WIDE)
        return pl.ds(half * WIDE + part * (WIDE // 2), WIDE // 2)

    def a_near(chunk, half, offset, part=None):
        if half == 0:
            return abuf.at[chunk * SIDE + z, hop(x, offset), :, a_cols(half, part)]
        return abuf.at[chunk * SIDE + hop(z, offset), x, :, a_cols(half, part)]

    def a_far(chunk, half, offset, part=None):
        if half == 0:
            return abuf.at[chunk * SIDE + hop(z, offset), :, :, a_cols(half, part)]
        return abuf.at[pl.ds(chunk * SIDE, SIDE), hop(x, offset), :, a_cols(half, part)]

    def x_near(chunk, half, offset, part=None):
        return xbuf.at[row_span(chunk, part), near_lanes(half, offset)]

    def x_far(chunk, half, offset, part=None):
        return xbuf.at[row_span(chunk, part), far_lanes(half, offset)]

    def gather_copy(near, far, sends, recvs, chunk, level, half, way, arriving):
        step = steps[way]
        axis = half if level < 2 else 1 - half
        block = near if level < 2 else far
        if level % 2 == 0:
            ref = block(chunk, half, -step if arriving else 0)
        else:
            ref = block(chunk, half, -2 * step if arriving else -step, way)
        return send(ref, ref, sends, recvs, chunk, slot(level, half, way), neighbour(axis, step))

    def gather_start(near, far, sends, recvs, chunk, level):
        for half in (0, 1):
            for way in (0, 1):
                gather_copy(near, far, sends, recvs, chunk, level, half, way, False).start()

    def gather_wait(near, far, sends, recvs, chunk, level):
        for half in (0, 1):
            for way in (0, 1):
                gather_copy(near, far, sends, recvs, chunk, level, half, way, True).wait_recv()

    def gather_sent(near, far, sends, recvs, chunk, level):
        for half in (0, 1):
            for way in (0, 1):
                gather_copy(near, far, sends, recvs, chunk, level, half, way, False).wait_send()

    a_args = (a_near, a_far, a_send, a_recv)
    x_args = (x_near, x_far, x_send, x_recv)

    def gather_step(args, chunk, level):
        gather_wait(*args, chunk, level)
        if level < 3:
            gather_start(*args, chunk, level + 1)

    def part_rows(part):
        return pl.ds(parts[part][0], parts[part][1])

    def scatter_copy(chunk, level, half, way):
        step = steps[way]
        axis = 1 - half if level < 2 else half
        if level == 0:
            src = pbuf.at[row_span(chunk, way), far_lanes(half, 2)]
            dst = r1.at[chunk, half, part_rows(way), :]
        elif level == 1:
            src = pbuf.at[row_span(chunk), far_lanes(half, step)]
            dst = r2.at[chunk, half, way]
        elif level == 2:
            src = pbuf.at[row_span(chunk, way), near_lanes(half, 2)]
            dst = r3.at[chunk, half, part_rows(way), :]
        else:
            src = pbuf.at[row_span(chunk), near_lanes(half, step)]
            dst = r4.at[chunk, half, way]
        return send(src, dst, p_send, p_recv, chunk, slot(level, half, way), neighbour(axis, step))

    def scatter_start(chunk, level):
        for half in (0, 1):
            for way in (0, 1):
                scatter_copy(chunk, level, half, way).start()

    def wide(value):
        return value.astype(jnp.float32)

    def scatter_step(chunk, level):
        for half in (0, 1):
            for way in (0, 1):
                scatter_copy(chunk, level, half, way).wait_recv()
            if level % 2 == 0:
                for way in (0, 1):
                    cols = (far_lanes if level == 0 else near_lanes)(half, steps[way])
                    landed = (r1 if level == 0 else r3)[chunk, half, part_rows(way), :]
                    span = row_span(chunk, way)
                    pbuf[span, cols] = (wide(pbuf[span, cols]) + wide(landed)).astype(jnp.bfloat16)
                    scatter_copy(chunk, level + 1, half, way).start()
            elif level == 1:
                cols, span = far_lanes(half, 0), row_span(chunk)
                total = wide(pbuf[span, cols]) + wide(r2[chunk, half, 0]) + wide(r2[chunk, half, 1])
                pbuf[span, cols] = total.astype(jnp.bfloat16)
                for way in (0, 1):
                    scatter_copy(chunk, 2, half, way).start()
            else:
                span = row_span(chunk)
                own = pl.ds(half * HALF, HALF)
                total = (
                    wide(pbuf[span, near_lanes(half, 0)])
                    + wide(r4[chunk, half, 0])
                    + wide(r4[chunk, half, 1])
                )
                out_ref[span, own] = (wide(mixed[span, own]) + total).astype(jnp.bfloat16)

    def scatter_sent(chunk, level):
        for half in (0, 1):
            for way in (0, 1):
                scatter_copy(chunk, level, half, way).wait_send()

    def dec_copy(k, arriving):
        other = lax.rem(me + k, PEERS)
        return pltpu.make_async_remote_copy(
            src_ref=dec_ref,
            dst_ref=dbuf.at[lax.rem(me - k + PEERS, PEERS) if arriving else me],
            send_sem=d_send.at[k],
            recv_sem=d_recv.at[k],
            device_id={"tok": other},
            device_id_type=MESH,
        )

    def project(chunk):
        first = chunk * tiles
        piece = jnp.concatenate(
            [abuf[(first + t) // SIDE, (first + t) % SIDE] for t in range(tiles)], axis=0
        )
        span = row_span(chunk)
        total = jnp.dot(piece, wo_ref[...], preferred_element_type=jnp.float32)
        value = (wide(resid_ref[span, :]) + total).astype(jnp.bfloat16)
        mixed[span, :] = value
        xbuf[span, near_lanes(0, 0)] = value[:, :HALF]
        xbuf[span, near_lanes(1, 0)] = value[:, HALF:]

    def normalize(chunk):
        @pl.loop(0, tiles)
        def _(t):
            span = pl.ds(pl.multiple_of(chunk * rows + t * SUB, SUB), SUB)
            total = jnp.zeros((SUB, HALF), jnp.float32)
            for block in range(D // HALF):
                value = wide(xbuf[span, block * HALF : (block + 1) * HALF])
                total = total + value * value
            scale = lax.rsqrt(jnp.sum(total, axis=-1, keepdims=True) / D + epsilon)
            owner = tenant_ref[span, :]
            to = pl.ds(pl.multiple_of(t * SUB, SUB), SUB)
            for block in range(D // HALF):
                cols = slice(block * HALF, (block + 1) * HALF)
                gain = gain_ref[3:4, cols]
                for k in (2, 1, 0):
                    gain = jnp.where(owner == k, gain_ref[k : k + 1, cols], gain)
                normed[to, cols] = (wide(xbuf[span, cols]) * scale * gain).astype(jnp.bfloat16)

    def lift(tile, width):
        cols = slice(tile * width, (tile + 1) * width)
        gate = jnp.dot(normed[...], wg_ref[:, cols], preferred_element_type=jnp.float32)
        up = jnp.dot(normed[...], wu_ref[:, cols], preferred_element_type=jnp.float32)
        hidden[:, cols] = (gate / (1.0 + jnp.exp(-gate)) * up).astype(jnp.bfloat16)

    def lower(chunk, width):
        @pl.loop(0, D // width)
        def _(tile):
            cols = pl.ds(pl.multiple_of(tile * width, width), width)
            part = jnp.dot(hidden[...], wd_ref[:, cols], preferred_element_type=jnp.float32)
            pbuf[row_span(chunk), cols] = part.astype(jnp.bfloat16)

    barrier = pltpu.get_barrier_semaphore()

    @pl.loop(1, PEERS)
    def _(k):
        pl.semaphore_signal(
            barrier, inc=1, device_id={"tok": lax.rem(me + k, PEERS)}, device_id_type=MESH
        )

    fetch_wo = pltpu.make_async_copy(wo_hbm, wo_ref, w_sem.at[0])
    fetch_wo.start()

    @pl.loop(0, att_chunks)
    def _(chunk):
        abuf[chunk * SIDE + z, x] = att_ref[pl.ds(pl.multiple_of(chunk * SUB, SUB), SUB), :]

    dbuf[me] = dec_ref[...]
    pl.semaphore_wait(barrier, PEERS - 1)

    @pl.loop(0, att_chunks)
    def _(chunk):
        gather_start(*a_args, chunk, 0)

    @pl.loop(1, PEERS)
    def _(k):
        dec_copy(k, False).start()

    @pl.loop(0, PEERS)
    def _(t):
        for half in (0, 1):
            source = pl.ds(pl.multiple_of(t * BLOCK + half * HALF, HALF), HALF)
            if half == 0:
                place = t * HALF
            else:
                place = WIDE + (t % SIDE) * (SIDE * HALF) + (t // SIDE) * HALF
            target = pl.ds(pl.multiple_of(place, HALF), HALF)
            pltpu.make_async_copy(wg_hbm.at[source, :], wg_ref.at[target, :], w_sem.at[1]).start()
            pltpu.make_async_copy(wu_hbm.at[source, :], wu_ref.at[target, :], w_sem.at[2]).start()
            pltpu.make_async_copy(wd_hbm.at[:, source], wd_ref.at[:, target], w_sem.at[3]).start()

    width = 256

    @pl.loop(0, CHUNKS + 3)
    def _(s):
        att_on = s < att_chunks
        x_on = jnp.logical_and(s >= 1, s < CHUNKS + 1)
        f_on = jnp.logical_and(s >= 2, s < CHUNKS + 2)
        p_on = s >= 3

        def progress(level):
            @pl.when(att_on)
            def _():
                gather_step(a_args, s, level)

            @pl.when(x_on)
            def _():
                gather_step(x_args, s - 1, level)

            @pl.when(p_on)
            def _():
                scatter_step(s - 3, level)

        @pl.when(s == 2)
        def _():
            pltpu.make_async_copy(wg_ref, wg_ref, w_sem.at[1]).wait()
            pltpu.make_async_copy(wu_ref, wu_ref, w_sem.at[2]).wait()
            pltpu.make_async_copy(wd_ref, wd_ref, w_sem.at[3]).wait()

        @pl.when(f_on)
        def _():
            normalize(s - 2)

        progress(0)

        @pl.when(f_on)
        def _():
            lift(0, width)

        progress(1)

        @pl.when(f_on)
        def _():
            for tile in range(1, ffw // width):
                lift(tile, width)

        progress(2)

        @pl.when(f_on)
        def _():
            lower(s - 2, 512)
            scatter_start(s - 2, 0)

        progress(3)

        @pl.when(s == 0)
        def _():
            fetch_wo.wait()

        @pl.when(s == CHUNKS - 1)
        def _():
            @pl.loop(1, PEERS)
            def _(k):
                dec_copy(k, True).wait_recv()

            for head in range(H):
                abuf[att_chunks * SIDE, 0, :, head * HD : (head + 1) * HD] = dbuf[
                    :, head, :
                ].astype(jnp.bfloat16)

        @pl.when(s < CHUNKS)
        def _():
            project(s)
            gather_start(*x_args, s, 0)

    @pl.loop(1, PEERS)
    def _(k):
        dec_copy(k, False).wait_send()

    @pl.loop(0, att_chunks)
    def _(chunk):
        for level in range(4):
            gather_sent(*a_args, chunk, level)

    @pl.loop(0, CHUNKS)
    def _(chunk):
        for level in range(4):
            gather_sent(*x_args, chunk, level)
            scatter_sent(chunk, level)


def ring_call(att, dec, resid, owner, gains, wo, w_gate, w_up, w_down):
    tokens = resid.shape[0]
    rows = tokens // CHUNKS
    ffw = w_gate.shape[1]
    vmem = pl.BlockSpec(memory_space=pltpu.VMEM)
    hbm = pl.BlockSpec(memory_space=pl.ANY)
    bf16 = jnp.bfloat16
    dma = pltpu.SemaphoreType.DMA
    return pl.pallas_call(
        ring_kernel,
        out_shape=jax.ShapeDtypeStruct((tokens, BLOCK), bf16),
        in_specs=[vmem] * 5 + [hbm] * 4,
        out_specs=vmem,
        scratch_shapes=[
            pltpu.VMEM((SIDE * SIDE + 1, SIDE, SUB, D), bf16),
            pltpu.VMEM((PEERS, H, HD), jnp.float32),
            pltpu.VMEM((tokens, D), bf16),
            pltpu.VMEM((tokens, D), bf16),
            pltpu.VMEM((tokens, BLOCK), bf16),
            pltpu.VMEM((rows, D), bf16),
            pltpu.VMEM((rows, ffw), bf16),
            pltpu.VMEM((CHUNKS, 2, rows, 4 * HALF), bf16),
            pltpu.VMEM((CHUNKS, 2, 2, rows, 4 * HALF), bf16),
            pltpu.VMEM((CHUNKS, 2, rows, HALF), bf16),
            pltpu.VMEM((CHUNKS, 2, 2, rows, HALF), bf16),
            pltpu.VMEM(wo.shape, bf16),
            pltpu.VMEM(w_gate.shape, bf16),
            pltpu.VMEM(w_up.shape, bf16),
            pltpu.VMEM(w_down.shape, bf16),
            dma((4,)),
            dma((CHUNKS, 16)),
            dma((CHUNKS, 16)),
            dma((PEERS,)),
            dma((PEERS,)),
            dma((CHUNKS, 16)),
            dma((CHUNKS, 16)),
            dma((CHUNKS, 16)),
            dma((CHUNKS, 16)),
        ],
        compiler_params=pltpu.CompilerParams(
            collective_id=1, has_side_effects=True, vmem_limit_bytes=67000000
        ),
        name="ring_layer",
    )(att, dec, resid, owner, gains, wo, w_gate, w_up, w_down)


def attend_kernel(
    length_ref,
    request_ref,
    query_ref,
    pair_ref,
    segment_ref,
    dec_ref,
    cache_hbm,
    att_ref,
    own_ref,
    kbuf,
    cbuf,
    column,
    outgoing,
    incoming,
    bias,
    c_sem,
    k_send,
    k_recv,
    g_send,
    g_recv,
    q_send,
    q_recv,
):
    me = lax.axis_index("tok")
    grp = lax.axis_index("grp")
    groups = column.shape[0]
    z, x = me // SIDE, me % SIDE
    rows = query_ref.shape[0]
    width = KVH * HD
    group = H // KVH
    pieces = k_send.shape[0]
    heads = KVH // pieces
    steps = (1, -1)

    def hop(value, step):
        return lax.rem(value + step + SIDE, SIDE)

    def neighbour(axis, step):
        if axis == 0:
            return z * SIDE + hop(x, step)
        return hop(z, step) * SIDE + x

    def block(piece, half, offset, level, part):
        cols = pl.ds(half * width + piece * heads * HD, heads * HD)
        span = pl.ds(0, rows) if part is None else pl.ds(part * (rows // 2), rows // 2)
        if level < 2:
            if half == 0:
                return kbuf.at[z, hop(x, offset), span, cols]
            return kbuf.at[hop(z, offset), x, span, cols]
        if half == 0:
            return kbuf.at[hop(z, offset), :, span, cols]
        return kbuf.at[:, hop(x, offset), span, cols]

    def copy(piece, level, half, way, arriving):
        step = steps[way]
        axis = half if level < 2 else 1 - half
        if level % 2 == 0:
            ref = block(piece, half, -step if arriving else 0, level, None)
        else:
            ref = block(piece, half, -2 * step if arriving else -step, level, way)
        index = level * 4 + half * 2 + way
        return pltpu.make_async_remote_copy(
            src_ref=ref,
            dst_ref=ref,
            send_sem=k_send.at[piece, index],
            recv_sem=k_recv.at[piece, index],
            device_id={"tok": neighbour(axis, step)},
            device_id_type=MESH,
        )

    def start(piece, level):
        for half in (0, 1):
            for way in (0, 1):
                copy(piece, level, half, way, False).start()

    def step(piece, level):
        for half in (0, 1):
            for way in (0, 1):
                copy(piece, level, half, way, True).wait_recv()
        if level < 3:
            start(piece, level + 1)

    def group_copy(k, arriving):
        source = lax.rem(grp - k + groups, groups) if arriving else grp
        return pltpu.make_async_remote_copy(
            src_ref=dec_ref,
            dst_ref=column.at[source],
            send_sem=g_send.at[k],
            recv_sem=g_recv.at[k],
            device_id={"grp": lax.rem(grp + k, groups)},
            device_id_type=MESH,
        )

    def query_copy(k, arriving):
        other = lax.rem(me + k, PEERS)
        source = lax.rem(me - k + PEERS, PEERS) if arriving else me
        return pltpu.make_async_remote_copy(
            src_ref=outgoing.at[other],
            dst_ref=incoming.at[source],
            send_sem=q_send.at[k],
            recv_sem=q_recv.at[k],
            device_id={"tok": other},
            device_id_type=MESH,
        )

    barrier = pltpu.get_barrier_semaphore()
    fetch = pltpu.make_async_copy(cache_hbm, cbuf, c_sem)
    fetch.start()

    @pl.loop(1, PEERS)
    def _(k):
        pl.semaphore_signal(
            barrier, inc=1, device_id={"tok": lax.rem(me + k, PEERS)}, device_id_type=MESH
        )

    @pl.loop(1, groups)
    def _(k):
        pl.semaphore_signal(
            barrier, inc=1, device_id={"grp": lax.rem(grp + k, groups)}, device_id_type=MESH
        )

    kbuf[z, x] = pair_ref[...]
    column[grp] = dec_ref[...]
    pl.semaphore_wait(barrier, PEERS + groups - 2)

    @pl.loop(1, groups)
    def _(k):
        group_copy(k, False).start()

    for piece in range(pieces):
        start(piece, 0)

    window = 10
    first = 2 * (jnp.maximum(me - 8, 0) // 2)
    span = window * rows
    near = pl.ds(pl.multiple_of((me // 2) * (2 * rows), 2 * rows), 2 * rows)
    mine = segment_ref[:, near].astype(jnp.float32)
    turned = jnp.transpose(jnp.broadcast_to(mine, (2 * rows, 2 * rows)))
    query_seg = jnp.where(me % 2 == 1, turned[rows:], turned[:rows])[:, :1]
    seen = pl.ds(pl.multiple_of(first * rows, 2 * rows), span)
    key_seg = segment_ref[:, seen].astype(jnp.float32)
    query_pos = me * rows + lax.broadcasted_iota(jnp.int32, (rows, span), 0)
    key_pos = first * rows + lax.broadcasted_iota(jnp.int32, (rows, span), 1)
    allowed = (key_pos <= query_pos) & (query_seg == key_seg)
    bias[...] = jnp.where(allowed, 0.0, -jnp.inf)

    @pl.loop(1, groups)
    def _(k):
        group_copy(k, True).wait_recv()

    @pl.loop(0, PEERS)
    def _(t):
        request = request_ref[grp * PEERS + t]
        row = column[request // PEERS]
        held = request % PEERS == me
        outgoing[t] = jnp.where(held, row.astype(jnp.float32), 0.0).astype(jnp.bfloat16)

    @pl.loop(1, PEERS)
    def _(k):
        query_copy(k, False).start()

    incoming[me] = outgoing[me]
    scale = 1.0 / math.sqrt(HD)

    def prefill(piece):
        @pl.loop(0, heads)
        def _(i):
            head = piece * heads + i

            def joined(base):
                cols = pl.ds(pl.multiple_of(base + head * HD, HD), HD)
                return jnp.concatenate(
                    [
                        kbuf[(first + b) // SIDE, (first + b) % SIDE, :, cols]
                        for b in range(window)
                    ],
                    axis=0,
                )

            keys, values = joined(0), joined(width)
            for j in range(group):
                cols = pl.ds(pl.multiple_of((head * group + j) * HD, HD), HD)
                scores = lax.dot_general(
                    query_ref[:, cols],
                    keys,
                    (((1,), (1,)), ((), ())),
                    preferred_element_type=jnp.float32,
                )
                scores = scores * scale + bias[...]
                top = jnp.max(scores, axis=-1, keepdims=True)
                weights = jnp.exp(scores - top).astype(jnp.bfloat16)
                total = jnp.sum(weights.astype(jnp.float32), axis=-1, keepdims=True)
                summed = jnp.dot(weights, values, preferred_element_type=jnp.float32)
                att_ref[:, cols] = (summed / total).astype(jnp.bfloat16)

    def decode():
        query = incoming[0].astype(jnp.float32)
        for t in range(1, PEERS):
            query = query + incoming[t].astype(jnp.float32)
        query = query.astype(jnp.bfloat16)
        count = cbuf.shape[0]
        owner = lax.broadcasted_iota(jnp.int32, (H, count), 0) // group
        scores = jnp.zeros((H, count), jnp.float32)
        for head in range(KVH):
            part = lax.dot_general(
                query,
                cbuf[:, head * HD : (head + 1) * HD],
                (((1,), (1,)), ((), ())),
                preferred_element_type=jnp.float32,
            )
            scores = jnp.where(owner == head, part, scores)
        visible = lax.broadcasted_iota(jnp.int32, (H, count), 1) < length_ref[0]
        scores = jnp.where(visible, scores * scale, -jnp.inf)
        top = jnp.max(scores, axis=-1, keepdims=True)
        weights = jnp.exp(scores - top).astype(jnp.bfloat16)
        total = jnp.sum(weights.astype(jnp.float32), axis=-1, keepdims=True)
        owner = lax.broadcasted_iota(jnp.int32, (H, HD), 0) // group
        summed = jnp.zeros((H, HD), jnp.float32)
        for head in range(KVH):
            base = width + head * HD
            part = jnp.dot(
                weights, cbuf[:, base : base + HD], preferred_element_type=jnp.float32
            )
            summed = jnp.where(owner == head, part, summed)
        own_ref[...] = summed / total

    for wave in range(pieces + 3):
        for level in range(4):
            piece = wave - level
            if 0 <= piece < pieces:
                step(piece, level)
        if wave == 2:
            fetch.wait()

            @pl.loop(1, PEERS)
            def _(k):
                query_copy(k, True).wait_recv()

            decode()
        if wave >= 3:
            prefill(wave - 3)

    @pl.loop(1, groups)
    def _(k):
        group_copy(k, False).wait_send()

    @pl.loop(1, PEERS)
    def _(k):
        query_copy(k, False).wait_send()

    @pl.loop(0, pieces)
    def _(piece):
        for level in range(4):
            for half in (0, 1):
                for way in (0, 1):
                    copy(piece, level, half, way, False).wait_send()


def attend_call(length, request, queries, pairs, segment, dec, cache):
    rows = queries.shape[0]
    groups = lax.axis_size("grp")
    pieces = 4
    vmem = pl.BlockSpec(memory_space=pltpu.VMEM)
    smem = pl.BlockSpec(memory_space=pltpu.SMEM)
    bf16 = jnp.bfloat16
    dma = pltpu.SemaphoreType.DMA
    return pl.pallas_call(
        attend_kernel,
        out_shape=(
            jax.ShapeDtypeStruct((rows, D), bf16),
            jax.ShapeDtypeStruct((H, HD), jnp.float32),
        ),
        in_specs=[smem, smem, vmem, vmem, vmem, vmem, pl.BlockSpec(memory_space=pl.ANY)],
        out_specs=(vmem, vmem),
        scratch_shapes=[
            pltpu.VMEM((SIDE, SIDE, rows, pairs.shape[1]), bf16),
            pltpu.VMEM(cache.shape, bf16),
            pltpu.VMEM((groups, H, HD), bf16),
            pltpu.VMEM((PEERS, H, HD), bf16),
            pltpu.VMEM((PEERS, H, HD), bf16),
            pltpu.VMEM((rows, 10 * rows), jnp.float32),
            dma,
            dma((pieces, 16)),
            dma((pieces, 16)),
            dma((groups,)),
            dma((groups,)),
            dma((PEERS,)),
            dma((PEERS,)),
        ],
        compiler_params=pltpu.CompilerParams(
            collective_id=2, has_side_effects=True, vmem_limit_bytes=40000000
        ),
        name="attend",
    )(length, request, queries, pairs, segment, dec, cache)


def grouped(rows, blocks):
    count = rows.shape[0] // blocks
    rest = rows.shape[1:]
    split = rows.reshape(blocks, count, *rest)
    main = split[:, : count - 1].reshape(blocks, (count - 1) // SUB, SUB, *rest)
    main = jnp.swapaxes(main, 0, 1).reshape(blocks * (count - 1), *rest)
    return jnp.concatenate([main, split[:, count - 1]], axis=0)


def ungrouped(rows, blocks):
    count = rows.shape[0] // blocks
    rest = rows.shape[1:]
    main = rows[: blocks * (count - 1)].reshape((count - 1) // SUB, blocks, SUB, *rest)
    main = jnp.swapaxes(main, 0, 1).reshape(blocks, count - 1, *rest)
    last = rows[blocks * (count - 1) :].reshape(blocks, 1, *rest)
    return jnp.concatenate([main, last], axis=1).reshape(blocks * count, *rest)


def shards(
    pre_q,
    pre_kv,
    pre_segment,
    dec_q,
    cache,
    cache_len,
    slot_request,
    resid,
    wo,
    tenant,
    norm_gain,
    w_gate,
    w_up,
    w_down,
):
    prefill_out, decode_out = attend_call(
        cache_len,
        slot_request,
        pre_q,
        pre_kv,
        pre_segment,
        dec_q.reshape(H, HD),
        cache[0],
    )
    blocks = lax.axis_size("tok")
    owner = grouped(tenant[0], blocks)
    owner = jnp.broadcast_to(owner[:, None], (owner.shape[0], HALF))
    pieces = norm_gain.reshape(-1, SIDE, SIDE, 2, HALF)
    first = pieces[:, :, :, 0].reshape(-1, WIDE)
    second = jnp.swapaxes(pieces[:, :, :, 1], 1, 2).reshape(-1, WIDE)
    gains = jnp.concatenate([first, second], axis=1)
    result = ring_call(
        prefill_out,
        decode_out,
        grouped(resid, blocks),
        owner,
        gains,
        wo,
        w_gate,
        w_up,
        w_down,
    )
    return ungrouped(result, blocks)


def solution(mesh):
    in_specs = (
        P(("grp", "tok"), None),
        P(("grp", "tok"), None),
        P("grp", None),
        P(("grp", "tok"), None),
        P(("grp", "tok"), None, None),
        P(("grp", "tok")),
        P(),
        P("grp", "tok"),
        P(None, "tok"),
        P("grp", None),
        P(),
        P(None, "tok"),
        P(None, "tok"),
        P("tok", None),
    )
    out_specs = P("grp", "tok")
    return jax.shard_map(shards, mesh=mesh, in_specs=in_specs, out_specs=out_specs, check_vma=False)
```

```python
import functools
import math

import jax
import jax.numpy as jnp
from jax import lax
from jax.experimental import pallas as pl
from jax.experimental.pallas import tpu as pltpu
from jax.sharding import PartitionSpec as P

D = 4096
H = 32
KVH = 8
HD = 128
SIDE = 4
PEERS = SIDE * SIDE
BLOCK = D // PEERS
HALF = BLOCK // 2
WIDE = D // 2
QUAD = SIDE * HALF
SUB = 16
PIECES = 4
WINDOW = 10
CORES = 2

epsilon = 1e-05
MESH = pl.DeviceIdType.MESH
WAYS = (1, -1)


def layer_kernel(
    length_ref,
    request_ref,
    query_ref,
    pair_ref,
    segment_ref,
    dec_ref,
    cache_hbm,
    resid_ref,
    tenant_ref,
    gain_ref,
    wo_hbm,
    wg_hbm,
    wu_hbm,
    wd_hbm,
    out_ref,
    abuf,
    wbuf,
    xbuf,
    pbuf,
    normed,
    hidden,
    r1,
    r2,
    r3,
    r4,
    wg_ref,
    wu_ref,
    wd_ref,
    bias,
    column,
    outgoing,
    incoming,
    own,
    dbuf,
    rbuf,
    xdec,
    pdec,
    rdec,
    w_sem,
    k_send,
    k_recv,
    g_send,
    g_recv,
    q_send,
    q_recv,
    d_send,
    d_recv,
    a_send,
    a_recv,
    wz_send,
    wz_recv,
    wy_send,
    wy_recv,
    wc_send,
    wc_recv,
    b_send,
    b_recv,
    e_send,
    e_recv,
    x_send,
    x_recv,
    p_send,
    p_recv,
    f_send,
    f_recv,
):
    me = lax.axis_index("tok")
    grp = lax.axis_index("grp")
    groups = column.shape[0]
    z, x = me // SIDE, me % SIDE
    y, core = grp // CORES, grp % CORES
    rows = query_ref.shape[0]
    tall = SIDE * rows
    width = KVH * HD
    group = H // KVH
    heads = KVH // PIECES
    ffw = wg_ref.shape[1]
    slab = D // groups
    scale = 1.0 / math.sqrt(HD)

    def hop(value, step):
        return lax.rem(value + step + SIDE, SIDE)

    def neighbour(axis, step):
        if axis == 0:
            return {"tok": z * SIDE + hop(x, step)}
        if axis == 1:
            return {"tok": hop(z, step) * SIDE + x}
        return {"grp": hop(y, step) * CORES + core}

    def remote(src, dst, sent, landed, peer):
        return pltpu.make_async_remote_copy(
            src_ref=src,
            dst_ref=dst,
            send_sem=sent,
            recv_sem=landed,
            device_id=peer,
            device_id_type=MESH,
        )

    def lanes(base, size):
        return pl.ds(pl.multiple_of(base, HALF), size)

    def wide(value):
        return value.astype(jnp.float32)

    def inner(part):
        if part is None:
            return pl.ds(0, rows)
        return pl.ds(part * (rows // 2), rows // 2)

    def k_block(piece, half, offset, level, part):
        cols = pl.ds(half * width + piece * heads * HD, heads * HD)
        span = inner(part)
        if level < 2:
            if half == 0:
                return pbuf.at[z, hop(x, offset), span, cols]
            return pbuf.at[hop(z, offset), x, span, cols]
        if half == 0:
            return pbuf.at[hop(z, offset), :, span, cols]
        return pbuf.at[:, hop(x, offset), span, cols]

    def x_block(chunk, half, offset, level, part):
        span = inner(part)
        if level < 2:
            if half == 0:
                return xbuf.at[chunk, z, span, lanes(hop(x, offset) * QUAD, QUAD)]
            return xbuf.at[chunk, hop(z, offset), span, lanes(WIDE + x * QUAD, QUAD)]
        if half == 0:
            return xbuf.at[chunk, hop(z, offset), span, pl.ds(0, WIDE)]
        return xbuf.at[chunk, :, span, lanes(WIDE + hop(x, offset) * QUAD, QUAD)]

    def gather_copy(block, sends, recvs, chunk, level, half, way, arriving):
        step = WAYS[way]
        axis = half if level < 2 else 1 - half
        if level % 2 == 0:
            ref = block(chunk, half, -step if arriving else 0, level, None)
        else:
            ref = block(chunk, half, -2 * step if arriving else -step, level, way)
        index = level * 4 + half * 2 + way
        return remote(
            ref, ref, sends.at[chunk, index], recvs.at[chunk, index], neighbour(axis, step)
        )

    def each(make):
        for half in (0, 1):
            for way in (0, 1):
                make(half, way)

    def gather_start(args, chunk, level):
        each(lambda half, way: gather_copy(*args, chunk, level, half, way, False).start())

    def gather_step(args, chunk, level):
        each(lambda half, way: gather_copy(*args, chunk, level, half, way, True).wait_recv())
        if level < 3:
            gather_start(args, chunk, level + 1)

    def gather_sent(args, chunk, level):
        each(lambda half, way: gather_copy(*args, chunk, level, half, way, False).wait_send())

    k_args = (k_block, k_send, k_recv)
    x_args = (x_block, x_send, x_recv)

    def a_copy(piece, level, way, arriving):
        step = WAYS[way]
        offset = -step * (level + 1) if arriving else -step * level
        base = hop(x, offset) * rows
        count = rows
        if level == 1:
            base = base + way * (rows // 2)
            count = rows // 2
        cols = pl.ds(piece * (D // PIECES), D // PIECES)
        ref = abuf.at[pl.ds(pl.multiple_of(base, SUB), count), cols]
        index = level * 2 + way
        return remote(
            ref, ref, a_send.at[piece, index], a_recv.at[piece, index], neighbour(0, step)
        )

    def slab_rows(offset, part=None):
        base = (hop(y, offset) * CORES + core) * slab
        if part is None:
            return pl.ds(pl.multiple_of(base, slab // 2), slab)
        return pl.ds(pl.multiple_of(base + part * (slab // 2), slab // 2), slab // 2)

    def wz_copy(level, way, arriving):
        step = WAYS[way]
        offset = -step * (level + 1) if arriving else -step * level
        span = slab_rows(0, way if level == 1 else None)
        dst = wbuf.at[hop(z, offset), span, :]
        src = wo_hbm.at[span, :] if level == 0 and not arriving else dst
        index = level * 2 + way
        return remote(src, dst, wz_send.at[index], wz_recv.at[index], neighbour(1, step))

    def wy_copy(other, level, way, arriving):
        step = WAYS[way]
        offset = -step * (level + 1) if arriving else -step * level
        span = slab_rows(offset, way if level == 1 else None)
        ref = wbuf.at[hop(z, other), span, :]
        index = (other - 1) * 4 + level * 2 + way
        return remote(ref, ref, wy_send.at[index], wy_recv.at[index], neighbour(2, step))

    def wc_copy(other, offset, arriving):
        base = hop(y, offset) * CORES + (1 - core if arriving else core)
        ref = wbuf.at[hop(z, other), pl.ds(pl.multiple_of(base * slab, slab), slab), :]
        index = (other - 1) * 4 + offset + 1
        peer = {"grp": y * CORES + 1 - core}
        return remote(ref, ref, wc_send.at[index], wc_recv.at[index], peer)

    def group_copy(k, arriving):
        source = lax.rem(grp - k + groups, groups) if arriving else grp
        peer = {"grp": lax.rem(grp + k, groups)}
        return remote(dec_ref, column.at[source], g_send.at[k], g_recv.at[k], peer)

    def ahead(k):
        return lax.rem(me + k, PEERS)

    def behind(k):
        return lax.rem(me - k + PEERS, PEERS)

    def query_copy(k, arriving):
        dst = incoming.at[behind(k) if arriving else me]
        return remote(outgoing.at[ahead(k)], dst, q_send.at[k], q_recv.at[k], {"tok": ahead(k)})

    def dec_copy(k, arriving):
        dst = dbuf.at[behind(k) if arriving else me]
        return remote(own, dst, d_send.at[k], d_recv.at[k], {"tok": ahead(k)})

    def fdec_copy(k, arriving):
        dst = rdec.at[behind(k) if arriving else me]
        return remote(pdec.at[ahead(k)], dst, f_send.at[k], f_recv.at[k], {"tok": ahead(k)})

    def base_copies(k, arriving):
        to = hop(z, k)
        slot = hop(z, -k) if arriving else z
        start = pl.ds(pl.multiple_of(to * tall, tall), tall)
        peer = {"tok": to * SIDE + x}
        last = pl.ds(PEERS * rows, PEERS)
        return (
            remote(
                resid_ref.at[start, :],
                rbuf.at[slot, pl.ds(0, tall), :],
                b_send.at[2 * k],
                b_recv.at[2 * k],
                peer,
            ),
            remote(
                resid_ref.at[last, :],
                rbuf.at[slot, pl.ds(tall, PEERS), :],
                b_send.at[2 * k + 1],
                b_recv.at[2 * k + 1],
                peer,
            ),
        )

    def xdec_copies(k, arriving):
        owner = hop(x, -k) if arriving else x
        peer = {"tok": z * SIDE + hop(x, k)}
        copies = []
        for half in (0, 1):
            ref = xdec.at[:, lanes(half * WIDE + owner * QUAD, QUAD)]
            index = 2 * k + half
            copies.append(remote(ref, ref, e_send.at[index], e_recv.at[index], peer))
        return copies

    def near_lanes(half, offset):
        if half == 0:
            return lanes(z * QUAD + hop(x, offset) * HALF, HALF)
        return lanes(WIDE + x * QUAD + hop(z, offset) * HALF, HALF)

    def far_lanes(half, offset):
        if half == 0:
            return lanes(hop(z, offset) * QUAD, QUAD)
        return lanes(WIDE + hop(x, offset) * QUAD, QUAD)

    def scatter_copy(chunk, level, half, way):
        step = WAYS[way]
        axis = 1 - half if level < 2 else half
        if level == 0:
            src = pbuf.at[chunk, :, inner(way), far_lanes(half, 2)]
            dst = r1.at[chunk, half, :, inner(way), :]
        elif level == 1:
            src = pbuf.at[chunk, :, :, far_lanes(half, step)]
            dst = r2.at[chunk, half, way]
        elif level == 2:
            src = pbuf.at[chunk, :, inner(way), near_lanes(half, 2)]
            dst = r3.at[chunk, half, :, inner(way), :]
        else:
            src = pbuf.at[chunk, :, :, near_lanes(half, step)]
            dst = r4.at[chunk, half, way]
        index = level * 4 + half * 2 + way
        return remote(
            src, dst, p_send.at[chunk, index], p_recv.at[chunk, index], neighbour(axis, step)
        )

    def scatter_start(chunk, level):
        each(lambda half, way: scatter_copy(chunk, level, half, way).start())

    def mine(half):
        return lanes(half * WIDE + x * QUAD + z * HALF, HALF)

    def scatter_step(chunk, level):
        for half in (0, 1):
            for way in (0, 1):
                scatter_copy(chunk, level, half, way).wait_recv()
            if level % 2 == 0:
                for way in (0, 1):
                    cols = (far_lanes if level == 0 else near_lanes)(half, WAYS[way])
                    span = inner(way)
                    landed = (r1 if level == 0 else r3)[chunk, half, :, span, :]
                    total = wide(pbuf[chunk, :, span, cols]) + wide(landed)
                    pbuf[chunk, :, span, cols] = total.astype(jnp.bfloat16)
                    scatter_copy(chunk, level + 1, half, way).start()
            elif level == 1:
                cols = far_lanes(half, 0)
                total = (
                    wide(pbuf[chunk, :, :, cols])
                    + wide(r2[chunk, half, 0])
                    + wide(r2[chunk, half, 1])
                )
                pbuf[chunk, :, :, cols] = total.astype(jnp.bfloat16)
                for way in (0, 1):
                    scatter_copy(chunk, 2, half, way).start()
            else:
                total = (
                    wide(pbuf[chunk, :, :, near_lanes(half, 0)])
                    + wide(r4[chunk, half, 0])
                    + wide(r4[chunk, half, 1])
                )
                total = wide(xbuf[chunk, :, :, mine(half)]) + total
                span = pl.ds(pl.multiple_of(chunk * tall, tall), tall)
                out_ref[span, half * HALF : (half + 1) * HALF] = total.astype(
                    jnp.bfloat16
                ).reshape(tall, HALF)

    def scatter_sent(chunk, level):
        each(lambda half, way: scatter_copy(chunk, level, half, way).wait_send())

    first = 2 * (jnp.maximum(me - 8, 0) // 2)

    def mask():
        span = WINDOW * rows
        near = lanes((me // 2) * (2 * rows), 2 * rows)
        part = segment_ref[:, near].astype(jnp.float32)
        turned = jnp.transpose(jnp.broadcast_to(part, (2 * rows, 2 * rows)))
        query_seg = jnp.where(me % 2 == 1, turned[rows:], turned[:rows])[:, :1]
        key_seg = segment_ref[:, lanes(first * rows, span)].astype(jnp.float32)
        query_pos = me * rows + lax.broadcasted_iota(jnp.int32, (rows, span), 0)
        key_pos = first * rows + lax.broadcasted_iota(jnp.int32, (rows, span), 1)
        allowed = (key_pos <= query_pos) & (query_seg == key_seg)
        bias[...] = jnp.where(allowed, 0.0, -jnp.inf)

    def prefill(piece):
        @pl.loop(0, heads)
        def _(i):
            head = piece * heads + i

            def joined(base):
                cols = lanes(base + head * HD, HD)
                return jnp.concatenate(
                    [
                        pbuf[(first + b) // SIDE, (first + b) % SIDE, :, cols]
                        for b in range(WINDOW)
                    ],
                    axis=0,
                )

            keys, values = joined(0), joined(width)
            for j in range(group):
                cols = lanes((head * group + j) * HD, HD)
                scores = lax.dot_general(
                    query_ref[:, cols],
                    keys,
                    (((1,), (1,)), ((), ())),
                    preferred_element_type=jnp.float32,
                )
                scores = scores * scale + bias[...]
                top = jnp.max(scores, axis=-1, keepdims=True)
                weights = jnp.exp(scores - top).astype(jnp.bfloat16)
                total = jnp.sum(wide(weights), axis=-1, keepdims=True)
                summed = jnp.dot(weights, values, preferred_element_type=jnp.float32)
                to = pl.ds(pl.multiple_of(x * rows, rows), rows)
                abuf[to, cols] = (summed / total).astype(jnp.bfloat16)

    def decode():
        query = wide(incoming[0])
        for t in range(1, PEERS):
            query = query + wide(incoming[t])
        query = query.astype(jnp.bfloat16)
        count = 2 * tall

        def cached(base):
            return pbuf[0:2, :, :, WIDE + base : WIDE + base + HD].reshape(count, HD)

        owner = lax.broadcasted_iota(jnp.int32, (H, count), 0) // group
        scores = jnp.zeros((H, count), jnp.float32)
        for head in range(KVH):
            part = lax.dot_general(
                query,
                cached(head * HD),
                (((1,), (1,)), ((), ())),
                preferred_element_type=jnp.float32,
            )
            scores = jnp.where(owner == head, part, scores)
        visible = lax.broadcasted_iota(jnp.int32, (H, count), 1) < length_ref[0]
        scores = jnp.where(visible, scores * scale, -jnp.inf)
        top = jnp.max(scores, axis=-1, keepdims=True)
        weights = jnp.exp(scores - top).astype(jnp.bfloat16)
        total = jnp.sum(wide(weights), axis=-1, keepdims=True)
        owner = lax.broadcasted_iota(jnp.int32, (H, HD), 0) // group
        summed = jnp.zeros((H, HD), jnp.float32)
        for head in range(KVH):
            part = jnp.dot(
                weights, cached(width + head * HD), preferred_element_type=jnp.float32
            )
            summed = jnp.where(owner == head, part, summed)
        own[...] = summed / total

    def project(other):
        total = wide(rbuf[other]) + jnp.dot(
            abuf[...], wbuf[other], preferred_element_type=jnp.float32
        )
        value = total.astype(jnp.bfloat16)
        for half in (0, 1):
            to = lanes(half * WIDE + x * QUAD + other * HALF, HALF)
            part = value[:, half * HALF : (half + 1) * HALF]
            for chunk in range(SIDE):
                xbuf[chunk, z, :, to] = part[chunk * rows : (chunk + 1) * rows]
            xdec[:, to] = part[tall:]

    def scaled(read, owner, write):
        total = jnp.zeros((SUB, HALF), jnp.float32)
        for block in range(D // HALF):
            value = wide(read(slice(block * HALF, (block + 1) * HALF)))
            total = total + value * value
        inverse = lax.rsqrt(jnp.sum(total, axis=-1, keepdims=True) / D + epsilon)
        for block in range(D // HALF):
            cols = slice(block * HALF, (block + 1) * HALF)
            gain = gain_ref[3:4, cols]
            for k in (2, 1, 0):
                gain = jnp.where(owner == k, gain_ref[k : k + 1, cols], gain)
            write(cols, (wide(read(cols)) * inverse * gain).astype(jnp.bfloat16))

    def normalize(chunk):
        @pl.loop(0, tall // SUB)
        def _(t):
            per = rows // SUB
            span = pl.ds(pl.multiple_of((t % per) * SUB, SUB), SUB)
            to = pl.ds(pl.multiple_of(t * SUB, SUB), SUB)
            owner = tenant_ref[pl.ds(pl.multiple_of(chunk * tall + t * SUB, SUB), SUB), :]

            def write(cols, value):
                normed[to, cols] = value

            scaled(lambda cols: xbuf[chunk, t // per, span, cols], owner, write)

    def normalize_dec():
        def write(cols, value):
            normed[tall : tall + SUB, cols] = value

        owner = tenant_ref[PEERS * rows : PEERS * rows + SUB, :]
        scaled(lambda cols: xdec[:, cols], owner, write)

    def lift(tile, size):
        cols = slice(tile * size, (tile + 1) * size)
        gate = jnp.dot(normed[...], wg_ref[:, cols], preferred_element_type=jnp.float32)
        up = jnp.dot(normed[...], wu_ref[:, cols], preferred_element_type=jnp.float32)
        hidden[:, cols] = (gate / (1.0 + jnp.exp(-gate)) * up).astype(jnp.bfloat16)

    def lower(chunk):
        @pl.loop(0, D // QUAD)
        def _(tile):
            cols = lanes(tile * QUAD, QUAD)
            part = jnp.dot(hidden[...], wd_ref[:, cols], preferred_element_type=jnp.float32)
            part = part.astype(jnp.bfloat16)
            pbuf[chunk, :, :, cols] = part[:tall].reshape(SIDE, rows, QUAD)

            @pl.when(chunk == 0)
            def _():
                for i in range(SIDE):
                    @pl.when(tile < SIDE)
                    def _():
                        pdec[tile * SIDE + i, :, :HALF] = part[tall:, i * HALF : (i + 1) * HALF]

                    @pl.when(tile >= SIDE)
                    def _():
                        pdec[i * SIDE + tile - SIDE, :, HALF:] = part[
                            tall:, i * HALF : (i + 1) * HALF
                        ]

    barrier = pltpu.get_barrier_semaphore()

    @pl.loop(1, PEERS)
    def _(k):
        pl.semaphore_signal(barrier, inc=1, device_id={"tok": ahead(k)}, device_id_type=MESH)

    @pl.loop(1, groups)
    def _(k):
        pl.semaphore_signal(
            barrier, inc=1, device_id={"grp": lax.rem(grp + k, groups)}, device_id_type=MESH
        )

    fetch = pltpu.make_async_copy(cache_hbm, pbuf.at[0:2, :, :, pl.ds(WIDE, WIDE)], w_sem.at[0])
    fetch.start()
    fetch_wo = pltpu.make_async_copy(wo_hbm, wbuf.at[z], w_sem.at[4])
    fetch_wo.start()
    pbuf[z, x, :, 0:WIDE] = pair_ref[...]
    column[grp] = dec_ref[...]
    rbuf[z, 0:tall, :] = resid_ref[pl.ds(pl.multiple_of(z * tall, tall), tall), :]
    rbuf[z, tall : tall + SUB, :] = resid_ref[PEERS * rows : PEERS * rows + SUB, :]
    pl.semaphore_wait(barrier, PEERS + groups - 2)

    @pl.loop(1, groups)
    def _(k):
        group_copy(k, False).start()

    gather_start(k_args, 0, 0)
    for way in (0, 1):
        wz_copy(0, way, False).start()
    for piece in range(1, PIECES):
        gather_start(k_args, piece, 0)

    @pl.loop(0, PEERS)
    def _(t):
        tz, tx = t // SIDE, t % SIDE
        for half in (0, 1):
            source = lanes(t * BLOCK + half * HALF, HALF)
            inside = lanes(half * WIDE + tx * QUAD + tz * HALF, HALF)
            place = t * HALF if half == 0 else WIDE + tx * QUAD + tz * HALF
            target = lanes(place, HALF)
            pltpu.make_async_copy(wg_hbm.at[source, :], wg_ref.at[inside, :], w_sem.at[1]).start()
            pltpu.make_async_copy(wu_hbm.at[source, :], wu_ref.at[inside, :], w_sem.at[2]).start()
            pltpu.make_async_copy(wd_hbm.at[:, source], wd_ref.at[:, target], w_sem.at[3]).start()

    mask()

    @pl.loop(1, groups)
    def _(k):
        group_copy(k, True).wait_recv()

    @pl.loop(0, PEERS)
    def _(t):
        request = request_ref[grp * PEERS + t]
        row = column[request // PEERS]
        held = request % PEERS == me
        outgoing[t] = jnp.where(held, wide(row), 0.0).astype(jnp.bfloat16)

    @pl.loop(1, PEERS)
    def _(k):
        query_copy(k, False).start()

    incoming[me] = outgoing[me]

    for wave in range(PIECES + 3):
        for level in range(4):
            piece = wave - level
            if 0 <= piece < PIECES:
                gather_step(k_args, piece, level)
        if wave == 0:
            for way in (0, 1):
                wz_copy(0, way, True).wait_recv()
            for way in (0, 1):
                wz_copy(1, way, False).start()
            for other in (1, 3):
                for way in (0, 1):
                    wy_copy(other, 0, way, False).start()
                wc_copy(other, 0, False).start()
            for k in (1, 2, 3):
                for copy in base_copies(k, False):
                    copy.start()
        if wave == 1:
            for way in (0, 1):
                wz_copy(1, way, True).wait_recv()
            for way in (0, 1):
                wy_copy(2, 0, way, False).start()
            wc_copy(2, 0, False).start()
        if wave == 2:
            fetch.wait()

            @pl.loop(1, PEERS)
            def _(k):
                query_copy(k, True).wait_recv()

            decode()

            @pl.loop(1, PEERS)
            def _(k):
                dec_copy(k, False).start()

            dbuf[me] = own[...]
        if wave >= 3:
            prefill(wave - 3)
            for way in (0, 1):
                a_copy(wave - 3, 0, way, False).start()
        if wave >= 4:
            for way in (0, 1):
                a_copy(wave - 4, 0, way, True).wait_recv()
                a_copy(wave - 4, 1, way, False).start()
        if wave == 4:
            for other in (1, 3, 2):
                for way in (0, 1):
                    wy_copy(other, 0, way, True).wait_recv()
                    wy_copy(other, 1, way, False).start()
                    wc_copy(other, -WAYS[way], False).start()

    for way in (0, 1):
        a_copy(PIECES - 1, 0, way, True).wait_recv()
        a_copy(PIECES - 1, 1, way, False).start()

    @pl.loop(1, PEERS)
    def _(k):
        dec_copy(k, True).wait_recv()

    for head in range(H):
        abuf[tall : tall + SUB, head * HD : (head + 1) * HD] = dbuf[:, head, :].astype(
            jnp.bfloat16
        )
    for other in (1, 3, 2):
        for way in (0, 1):
            wy_copy(other, 1, way, True).wait_recv()
        wc_copy(other, 2, False).start()
    for k in (1, 2, 3):
        for copy in base_copies(k, True):
            copy.wait_recv()
    for piece in range(PIECES):
        for way in (0, 1):
            a_copy(piece, 1, way, True).wait_recv()
    for other in (1, 2, 3):
        for offset in (-1, 0, 1, 2):
            wc_copy(other, offset, True).wait_recv()
    fetch_wo.wait()

    @pl.loop(0, SIDE)
    def _(other):
        project(other)

    for k in (1, 2, 3):
        for copy in xdec_copies(k, False):
            copy.start()

    @pl.loop(0, SIDE)
    def _(chunk):
        gather_start(x_args, chunk, 0)

    @pl.loop(0, PIECES)
    def _(piece):
        for level in range(4):
            gather_sent(k_args, piece, level)

    gather_step(x_args, 0, 0)
    gather_step(x_args, 0, 1)
    size = 256

    @pl.loop(0, SIDE + 2)
    def _(s):
        x_on = s < SIDE
        next_on = s < SIDE - 1
        f_on = jnp.logical_and(s >= 1, s < SIDE + 1)
        p_on = s >= 2

        @pl.when(s == 1)
        def _():
            pltpu.make_async_copy(wg_ref, wg_ref, w_sem.at[1]).wait()
            pltpu.make_async_copy(wu_ref, wu_ref, w_sem.at[2]).wait()
            pltpu.make_async_copy(wd_ref, wd_ref, w_sem.at[3]).wait()
            for k in (1, 2, 3):
                for copy in xdec_copies(k, True):
                    copy.wait_recv()
            normalize_dec()

        @pl.when(f_on)
        def _():
            normalize(s - 1)

        @pl.when(x_on)
        def _():
            gather_step(x_args, s, 2)

        @pl.when(next_on)
        def _():
            gather_step(x_args, s + 1, 0)

        @pl.when(p_on)
        def _():
            scatter_step(s - 2, 0)

        @pl.when(f_on)
        def _():
            lift(0, size)

        @pl.when(next_on)
        def _():
            gather_step(x_args, s + 1, 1)

        @pl.when(p_on)
        def _():
            scatter_step(s - 2, 1)

        @pl.when(f_on)
        def _():
            for tile in range(1, ffw // size):
                lift(tile, size)

        @pl.when(p_on)
        def _():
            scatter_step(s - 2, 2)

        @pl.when(f_on)
        def _():
            lower(s - 1)
            scatter_start(s - 1, 0)

        @pl.when(s == 1)
        def _():
            @pl.loop(1, PEERS)
            def _(k):
                fdec_copy(k, False).start()

        @pl.when(x_on)
        def _():
            gather_step(x_args, s, 3)

        @pl.when(p_on)
        def _():
            scatter_step(s - 2, 3)

    @pl.loop(1, PEERS)
    def _(k):
        fdec_copy(k, True).wait_recv()

    rdec[me] = pdec[me]
    total = wide(rdec[0])
    for t in range(1, PEERS):
        total = total + wide(rdec[t])
    for half in (0, 1):
        part = wide(xdec[:, mine(half)]) + total[:, half * HALF : (half + 1) * HALF]
        out_ref[PEERS * rows : PEERS * rows + SUB, half * HALF : (half + 1) * HALF] = part.astype(
            jnp.bfloat16
        )

    @pl.loop(1, groups)
    def _(k):
        group_copy(k, False).wait_send()

    @pl.loop(1, PEERS)
    def _(k):
        query_copy(k, False).wait_send()
        dec_copy(k, False).wait_send()
        fdec_copy(k, False).wait_send()

    for way in (0, 1):
        for level in (0, 1):
            wz_copy(level, way, False).wait_send()
            for other in (1, 2, 3):
                wy_copy(other, level, way, False).wait_send()
            for piece in range(PIECES):
                a_copy(piece, level, way, False).wait_send()
    for other in (1, 2, 3):
        for offset in (-1, 0, 1, 2):
            wc_copy(other, offset, False).wait_send()
        for copy in base_copies(other, False) + tuple(xdec_copies(other, False)):
            copy.wait_send()

    @pl.loop(0, SIDE)
    def _(chunk):
        for level in range(4):
            gather_sent(x_args, chunk, level)
            scatter_sent(chunk, level)


def layer_call(length, request, queries, pairs, segment, dec, cache, resid, owner, gains, *weights):
    wo, w_gate, w_up, w_down = weights
    rows = queries.shape[0]
    tall = SIDE * rows
    ffw = w_gate.shape[1]
    groups = lax.axis_size("grp")
    vmem = pl.BlockSpec(memory_space=pltpu.VMEM)
    smem = pl.BlockSpec(memory_space=pltpu.SMEM)
    hbm = pl.BlockSpec(memory_space=pl.ANY)
    bf16 = jnp.bfloat16
    dma = pltpu.SemaphoreType.DMA
    pairs_of = lambda *shape: [dma(shape), dma(shape)]
    return pl.pallas_call(
        layer_kernel,
        out_shape=jax.ShapeDtypeStruct(resid.shape, bf16),
        in_specs=[smem, smem, vmem, vmem, vmem, vmem, hbm, vmem, vmem, vmem] + [hbm] * 4,
        out_specs=vmem,
        scratch_shapes=[
            pltpu.VMEM((tall + SUB, D), bf16),
            pltpu.VMEM((SIDE, D, BLOCK), bf16),
            pltpu.VMEM((SIDE, SIDE, rows, D), bf16),
            pltpu.VMEM((SIDE, SIDE, rows, D), bf16),
            pltpu.VMEM((tall + SUB, D), bf16),
            pltpu.VMEM((tall + SUB, ffw), bf16),
            pltpu.VMEM((SIDE, 2, SIDE, rows, QUAD), bf16),
            pltpu.VMEM((SIDE, 2, 2, SIDE, rows, QUAD), bf16),
            pltpu.VMEM((SIDE, 2, SIDE, rows, HALF), bf16),
            pltpu.VMEM((SIDE, 2, 2, SIDE, rows, HALF), bf16),
            pltpu.VMEM(w_gate.shape, bf16),
            pltpu.VMEM(w_up.shape, bf16),
            pltpu.VMEM(w_down.shape, bf16),
            pltpu.VMEM((rows, WINDOW * rows), jnp.float32),
            pltpu.VMEM((groups, H, HD), bf16),
            pltpu.VMEM((PEERS, H, HD), bf16),
            pltpu.VMEM((PEERS, H, HD), bf16),
            pltpu.VMEM((H, HD), jnp.float32),
            pltpu.VMEM((PEERS, H, HD), jnp.float32),
            pltpu.VMEM((SIDE, tall + SUB, BLOCK), bf16),
            pltpu.VMEM((SUB, D), bf16),
            pltpu.VMEM((PEERS, SUB, BLOCK), bf16),
            pltpu.VMEM((PEERS, SUB, BLOCK), bf16),
            dma((5,)),
            *pairs_of(PIECES, 16),
            *pairs_of(groups),
            *pairs_of(PEERS),
            *pairs_of(PEERS),
            *pairs_of(PIECES, 4),
            *pairs_of(4),
            *pairs_of(12),
            *pairs_of(12),
            *pairs_of(8),
            *pairs_of(8),
            *pairs_of(SIDE, 16),
            *pairs_of(SIDE, 16),
            *pairs_of(PEERS),
        ],
        compiler_params=pltpu.CompilerParams(
            collective_id=1, has_side_effects=True, vmem_limit_bytes=67043328
        ),
        name="layer",
    )(length, request, queries, pairs, segment, dec, cache, resid, owner, gains, *weights)


def shards(
    pre_q,
    pre_kv,
    pre_segment,
    dec_q,
    cache,
    cache_len,
    slot_request,
    resid,
    wo,
    tenant,
    norm_gain,
    w_gate,
    w_up,
    w_down,
):
    rows = pre_q.shape[0]
    tokens, cols = resid.shape
    split = resid.reshape(PEERS, rows + 1, cols)
    natural = jnp.concatenate([split[:, :rows].reshape(PEERS * rows, cols), split[:, rows]], axis=0)
    owner = tenant[0].reshape(PEERS, rows + 1)
    main = jnp.swapaxes(owner[:, :rows].reshape(SIDE, SIDE, rows), 0, 1).reshape(PEERS * rows)
    owner = jnp.concatenate([main, owner[:, rows]], axis=0)
    owner = jnp.broadcast_to(owner[:, None], (tokens, HALF))
    gains = norm_gain.reshape(-1, SIDE, SIDE, 2, HALF).transpose(0, 3, 2, 1, 4).reshape(-1, D)
    result = layer_call(
        cache_len,
        slot_request,
        pre_q,
        pre_kv,
        pre_segment,
        dec_q.reshape(H, HD),
        cache.reshape(2, SIDE, -1, cache.shape[2]),
        natural,
        owner,
        gains,
        wo,
        w_gate,
        w_up,
        w_down,
    )
    main = result[: PEERS * rows].reshape(SIDE, SIDE, rows, cols)
    main = jnp.swapaxes(main, 0, 1).reshape(PEERS, rows, cols)
    last = result[PEERS * rows :].reshape(PEERS, 1, cols)
    return jnp.concatenate([main, last], axis=1).reshape(tokens, cols)


def solution(mesh):
    in_specs = (
        P(("grp", "tok"), None),
        P(("grp", "tok"), None),
        P("grp", None),
        P(("grp", "tok"), None),
        P(("grp", "tok"), None, None),
        P(("grp", "tok")),
        P(),
        P("grp", "tok"),
        P(None, "tok"),
        P("grp", None),
        P(),
        P(None, "tok"),
        P(None, "tok"),
        P("tok", None),
    )
    out_specs = P("grp", "tok")
    return jax.shard_map(shards, mesh=mesh, in_specs=in_specs, out_specs=out_specs, check_vma=False)
```

```python
import functools
import math

import jax
import jax.numpy as jnp
from jax import lax
from jax.experimental import pallas as pl
from jax.experimental.pallas import tpu as pltpu
from jax.sharding import PartitionSpec as P

D = 4096
H = 32
KVH = 8
HD = 128
SIDE = 4
PEERS = SIDE * SIDE
BLOCK = D // PEERS
HALF = BLOCK // 2
WIDE = D // 2
QUAD = SIDE * HALF
SUB = 16
PIECES = 4
CHUNKS = 8
PARTS = CHUNKS // SIDE
WINDOW = 10
CORES = 2

epsilon = 1e-05
MESH = pl.DeviceIdType.MESH
WAYS = (1, -1)


def layer_kernel(
    length_ref,
    request_ref,
    query_hbm,
    pair_hbm,
    segment_ref,
    dec_ref,
    cache_hbm,
    resid_hbm,
    tenant_ref,
    gain_hbm,
    wo_hbm,
    wg_hbm,
    wu_hbm,
    wd_hbm,
    out_hbm,
    qbuf,
    gbuf,
    obuf,
    abuf,
    wbuf,
    xbuf,
    pbuf,
    normed,
    hidden,
    r1,
    r2,
    r3,
    r4,
    wg_ref,
    wu_ref,
    wd_ref,
    bias,
    tbuf,
    column,
    outgoing,
    incoming,
    own,
    dbuf,
    rbuf,
    xdec,
    pdec,
    rdec,
    w_sem,
    o_sem,
    k_send,
    k_recv,
    g_send,
    g_recv,
    q_send,
    q_recv,
    d_send,
    d_recv,
    a_send,
    a_recv,
    wz_send,
    wz_recv,
    wy_send,
    wy_recv,
    wc_send,
    wc_recv,
    b_send,
    b_recv,
    e_send,
    e_recv,
    x_send,
    x_recv,
    p_send,
    p_recv,
    f_send,
    f_recv,
):
    me = lax.axis_index("tok")
    grp = lax.axis_index("grp")
    groups = column.shape[0]
    z, x = me // SIDE, me % SIDE
    y, core = grp // CORES, grp % CORES
    rows = query_hbm.shape[0]
    tall = SIDE * rows
    part_rows = rows // PARTS
    high = SIDE * part_rows
    width = KVH * HD
    group = H // KVH
    heads = KVH // PIECES
    ffw = wg_ref.shape[1]
    slab = D // groups
    scale = 1.0 / math.sqrt(HD)

    def hop(value, step):
        return lax.rem(value + step + SIDE, SIDE)

    def neighbour(axis, step):
        if axis == 0:
            return {"tok": z * SIDE + hop(x, step)}
        if axis == 1:
            return {"tok": hop(z, step) * SIDE + x}
        return {"grp": hop(y, step) * CORES + core}

    def remote(src, dst, sent, landed, peer):
        return pltpu.make_async_remote_copy(
            src_ref=src,
            dst_ref=dst,
            send_sem=sent,
            recv_sem=landed,
            device_id=peer,
            device_id_type=MESH,
        )

    def lanes(base, size):
        return pl.ds(pl.multiple_of(base, HALF), size)

    def wide(value):
        return value.astype(jnp.float32)

    def inner(part):
        if part is None:
            return pl.ds(0, rows)
        return pl.ds(part * (rows // 2), rows // 2)

    def k_block(piece, half, offset, level, part):
        cols = pl.ds(half * width + piece * heads * HD, heads * HD)
        span = inner(part)
        if level < 2:
            if half == 0:
                return pbuf.at[z, hop(x, offset), span, cols]
            return pbuf.at[hop(z, offset), x, span, cols]
        if half == 0:
            return pbuf.at[hop(z, offset), :, span, cols]
        return pbuf.at[:, hop(x, offset), span, cols]

    def within(chunk, part=None):
        base = (chunk % PARTS) * part_rows
        if part is None:
            return pl.ds(pl.multiple_of(base, SUB), part_rows)
        count = part_rows // 2
        return pl.ds(pl.multiple_of(base + part * count, SUB), count)

    def half_of(part):
        return pl.ds(part * (part_rows // 2), part_rows // 2)

    def x_block(number, half, offset, level, part):
        span = within(number, part)
        chunk = number // PARTS
        if level < 2:
            if half == 0:
                return xbuf.at[chunk, z, span, lanes(hop(x, offset) * QUAD, QUAD)]
            return xbuf.at[chunk, hop(z, offset), span, lanes(WIDE + x * QUAD, QUAD)]
        if half == 0:
            return xbuf.at[chunk, hop(z, offset), span, pl.ds(0, WIDE)]
        return xbuf.at[chunk, :, span, lanes(WIDE + hop(x, offset) * QUAD, QUAD)]

    def gather_copy(block, sends, recvs, chunk, level, half, way, arriving):
        step = WAYS[way]
        axis = half if level < 2 else 1 - half
        if level % 2 == 0:
            ref = block(chunk, half, -step if arriving else 0, level, None)
        else:
            ref = block(chunk, half, -2 * step if arriving else -step, level, way)
        index = level * 4 + half * 2 + way
        return remote(
            ref, ref, sends.at[chunk, index], recvs.at[chunk, index], neighbour(axis, step)
        )

    def each(make):
        for half in (0, 1):
            for way in (0, 1):
                make(half, way)

    def gather_start(args, chunk, level):
        each(lambda half, way: gather_copy(*args, chunk, level, half, way, False).start())

    def gather_step(args, chunk, level):
        each(lambda half, way: gather_copy(*args, chunk, level, half, way, True).wait_recv())
        if level < 3:
            gather_start(args, chunk, level + 1)

    def gather_sent(args, chunk, level):
        each(lambda half, way: gather_copy(*args, chunk, level, half, way, False).wait_send())

    k_args = (k_block, k_send, k_recv)
    x_args = (x_block, x_send, x_recv)

    def a_copy(piece, level, way, arriving):
        step = WAYS[way]
        offset = -step * (level + 1) if arriving else -step * level
        base = hop(x, offset) * rows
        count = rows
        if level == 1:
            base = base + way * (rows // 2)
            count = rows // 2
        cols = pl.ds(piece * (D // PIECES), D // PIECES)
        ref = abuf.at[pl.ds(pl.multiple_of(base, SUB), count), cols]
        index = level * 2 + way
        return remote(
            ref, ref, a_send.at[piece, index], a_recv.at[piece, index], neighbour(0, step)
        )

    def slab_rows(offset, part=None):
        base = (hop(y, offset) * CORES + core) * slab
        if part is None:
            return pl.ds(pl.multiple_of(base, slab // 2), slab)
        return pl.ds(pl.multiple_of(base + part * (slab // 2), slab // 2), slab // 2)

    def wz_copy(level, way, arriving):
        step = WAYS[way]
        offset = -step * (level + 1) if arriving else -step * level
        span = slab_rows(0, way if level == 1 else None)
        dst = wbuf.at[hop(z, offset), span, :]
        src = wo_hbm.at[span, :] if level == 0 and not arriving else dst
        index = level * 2 + way
        return remote(src, dst, wz_send.at[index], wz_recv.at[index], neighbour(1, step))

    def wy_copy(other, level, way, arriving):
        step = WAYS[way]
        offset = -step * (level + 1) if arriving else -step * level
        span = slab_rows(offset, way if level == 1 else None)
        ref = wbuf.at[hop(z, other), span, :]
        index = (other - 1) * 4 + level * 2 + way
        return remote(ref, ref, wy_send.at[index], wy_recv.at[index], neighbour(2, step))

    def wc_copy(other, offset, arriving):
        base = hop(y, offset) * CORES + (1 - core if arriving else core)
        ref = wbuf.at[hop(z, other), pl.ds(pl.multiple_of(base * slab, slab), slab), :]
        index = (other - 1) * 4 + offset + 1
        peer = {"grp": y * CORES + 1 - core}
        return remote(ref, ref, wc_send.at[index], wc_recv.at[index], peer)

    def group_copy(k, arriving):
        source = lax.rem(grp - k + groups, groups) if arriving else grp
        peer = {"grp": lax.rem(grp + k, groups)}
        return remote(column.at[grp], column.at[source], g_send.at[k], g_recv.at[k], peer)

    def ahead(k):
        return lax.rem(me + k, PEERS)

    def behind(k):
        return lax.rem(me - k + PEERS, PEERS)

    def query_copy(k, arriving):
        dst = incoming.at[behind(k) if arriving else me]
        return remote(outgoing.at[ahead(k)], dst, q_send.at[k], q_recv.at[k], {"tok": ahead(k)})

    def dec_copy(k, arriving):
        dst = dbuf.at[behind(k) if arriving else me]
        return remote(own, dst, d_send.at[k], d_recv.at[k], {"tok": ahead(k)})

    def fdec_copy(k, arriving):
        dst = rdec.at[behind(k) if arriving else me]
        return remote(pdec.at[ahead(k)], dst, f_send.at[k], f_recv.at[k], {"tok": ahead(k)})

    def base_copies(k, arriving):
        to = hop(z, k)
        slot = hop(z, -k) if arriving else z
        start = pl.ds(pl.multiple_of(to * tall, tall), tall)
        peer = {"tok": to * SIDE + x}
        last = pl.ds(PEERS * rows, PEERS)
        return (
            remote(
                resid_hbm.at[start, :],
                rbuf.at[slot, pl.ds(0, tall), :],
                b_send.at[2 * k],
                b_recv.at[2 * k],
                peer,
            ),
            remote(
                resid_hbm.at[last, :],
                rbuf.at[slot, pl.ds(tall, PEERS), :],
                b_send.at[2 * k + 1],
                b_recv.at[2 * k + 1],
                peer,
            ),
        )

    def xdec_copies(k, arriving):
        owner = hop(x, -k) if arriving else x
        peer = {"tok": z * SIDE + hop(x, k)}
        copies = []
        for half in (0, 1):
            ref = xdec.at[:, lanes(half * WIDE + owner * QUAD, QUAD)]
            index = 2 * k + half
            copies.append(remote(ref, ref, e_send.at[index], e_recv.at[index], peer))
        return copies

    def near_lanes(half, offset):
        if half == 0:
            return lanes(z * QUAD + hop(x, offset) * HALF, HALF)
        return lanes(WIDE + x * QUAD + hop(z, offset) * HALF, HALF)

    def far_lanes(half, offset):
        if half == 0:
            return lanes(hop(z, offset) * QUAD, QUAD)
        return lanes(WIDE + hop(x, offset) * QUAD, QUAD)

    def scatter_copy(number, level, half, way):
        step = WAYS[way]
        axis = 1 - half if level < 2 else half
        chunk, span = number // PARTS, within(number)
        if level == 0:
            src = pbuf.at[chunk, :, within(number, way), far_lanes(half, 2)]
            dst = r1.at[number, half, :, half_of(way), :]
        elif level == 1:
            src = pbuf.at[chunk, :, span, far_lanes(half, step)]
            dst = r2.at[number, half, way]
        elif level == 2:
            src = pbuf.at[chunk, :, within(number, way), near_lanes(half, 2)]
            dst = r3.at[number, half, :, half_of(way), :]
        else:
            src = pbuf.at[chunk, :, span, near_lanes(half, step)]
            dst = r4.at[number, half, way]
        index = level * 4 + half * 2 + way
        return remote(
            src, dst, p_send.at[number, index], p_recv.at[number, index], neighbour(axis, step)
        )

    def scatter_start(chunk, level):
        each(lambda half, way: scatter_copy(chunk, level, half, way).start())

    def mine(half):
        return lanes(half * WIDE + x * QUAD + z * HALF, HALF)

    def out_copy(number):
        span = pl.ds(pl.multiple_of(number * high, high), high)
        return pltpu.make_async_copy(obuf.at[span, :], out_hbm.at[span, :], o_sem.at[number])

    def scatter_step(number, level):
        chunk, span = number // PARTS, within(number)
        for half in (0, 1):
            for way in (0, 1):
                scatter_copy(number, level, half, way).wait_recv()
            if level % 2 == 0:
                for way in (0, 1):
                    cols = (far_lanes if level == 0 else near_lanes)(half, WAYS[way])
                    some = within(number, way)
                    landed = (r1 if level == 0 else r3)[number, half, :, half_of(way), :]
                    total = wide(pbuf[chunk, :, some, cols]) + wide(landed)
                    pbuf[chunk, :, some, cols] = total.astype(jnp.bfloat16)
                    scatter_copy(number, level + 1, half, way).start()
            elif level == 1:
                cols = far_lanes(half, 0)
                total = (
                    wide(pbuf[chunk, :, span, cols])
                    + wide(r2[number, half, 0])
                    + wide(r2[number, half, 1])
                )
                pbuf[chunk, :, span, cols] = total.astype(jnp.bfloat16)
                for way in (0, 1):
                    scatter_copy(number, 2, half, way).start()
            else:
                total = (
                    wide(pbuf[chunk, :, span, near_lanes(half, 0)])
                    + wide(r4[number, half, 0])
                    + wide(r4[number, half, 1])
                )
                total = wide(xbuf[chunk, :, span, mine(half)]) + total
                to = pl.ds(pl.multiple_of(number * high, high), high)
                obuf[to, half * HALF : (half + 1) * HALF] = total.astype(jnp.bfloat16).reshape(
                    high, HALF
                )
        if level == 3:
            out_copy(number).start()

    def scatter_sent(chunk, level):
        each(lambda half, way: scatter_copy(chunk, level, half, way).wait_send())

    first = 2 * (jnp.maximum(me - 8, 0) // 2)

    def mask():
        span = WINDOW * rows
        near = lanes((me // 2) * (2 * rows), 2 * rows)
        part = segment_ref[:, near].astype(jnp.float32)
        turned = jnp.transpose(jnp.broadcast_to(part, (2 * rows, 2 * rows)))
        query_seg = jnp.where(me % 2 == 1, turned[rows:], turned[:rows])[:, :1]
        key_seg = segment_ref[:, lanes(first * rows, span)].astype(jnp.float32)
        query_pos = me * rows + lax.broadcasted_iota(jnp.int32, (rows, span), 0)
        key_pos = first * rows + lax.broadcasted_iota(jnp.int32, (rows, span), 1)
        allowed = (key_pos <= query_pos) & (query_seg == key_seg)
        bias[...] = jnp.where(allowed, 0.0, -jnp.inf)

    def prefill(piece):
        @pl.loop(0, heads)
        def _(i):
            head = piece * heads + i

            def joined(base):
                cols = lanes(base + head * HD, HD)
                return jnp.concatenate(
                    [
                        pbuf[(first + b) // SIDE, (first + b) % SIDE, :, cols]
                        for b in range(WINDOW)
                    ],
                    axis=0,
                )

            keys, values = joined(0), joined(width)
            for j in range(group):
                cols = lanes((head * group + j) * HD, HD)
                scores = lax.dot_general(
                    qbuf[:, cols],
                    keys,
                    (((1,), (1,)), ((), ())),
                    preferred_element_type=jnp.float32,
                )
                scores = scores * scale + bias[...]
                top = jnp.max(scores, axis=-1, keepdims=True)
                weights = jnp.exp(scores - top).astype(jnp.bfloat16)
                total = jnp.sum(wide(weights), axis=-1, keepdims=True)
                summed = jnp.dot(weights, values, preferred_element_type=jnp.float32)
                to = pl.ds(pl.multiple_of(x * rows, rows), rows)
                abuf[to, cols] = (summed / total).astype(jnp.bfloat16)

    def decode():
        query = wide(incoming[0])
        for t in range(1, PEERS):
            query = query + wide(incoming[t])
        query = query.astype(jnp.bfloat16)
        count = 2 * tall

        def cached(base):
            return pbuf[0:2, :, :, WIDE + base : WIDE + base + HD].reshape(count, HD)

        owner = lax.broadcasted_iota(jnp.int32, (H, count), 0) // group
        scores = jnp.zeros((H, count), jnp.float32)
        for head in range(KVH):
            part = lax.dot_general(
                query,
                cached(head * HD),
                (((1,), (1,)), ((), ())),
                preferred_element_type=jnp.float32,
            )
            scores = jnp.where(owner == head, part, scores)
        visible = lax.broadcasted_iota(jnp.int32, (H, count), 1) < length_ref[0]
        scores = jnp.where(visible, scores * scale, -jnp.inf)
        top = jnp.max(scores, axis=-1, keepdims=True)
        weights = jnp.exp(scores - top).astype(jnp.bfloat16)
        total = jnp.sum(wide(weights), axis=-1, keepdims=True)
        owner = lax.broadcasted_iota(jnp.int32, (H, HD), 0) // group
        summed = jnp.zeros((H, HD), jnp.float32)
        for head in range(KVH):
            part = jnp.dot(
                weights, cached(width + head * HD), preferred_element_type=jnp.float32
            )
            summed = jnp.where(owner == head, part, summed)
        own[...] = summed / total

    def project(other):
        total = wide(rbuf[other]) + jnp.dot(
            abuf[...], wbuf[other], preferred_element_type=jnp.float32
        )
        value = total.astype(jnp.bfloat16)
        for half in (0, 1):
            to = lanes(half * WIDE + x * QUAD + other * HALF, HALF)
            part = value[:, half * HALF : (half + 1) * HALF]
            for chunk in range(SIDE):
                xbuf[chunk, z, :, to] = part[chunk * rows : (chunk + 1) * rows]
            xdec[:, to] = part[tall:]

    def scaled(read, owner, write):
        total = jnp.zeros((SUB, HALF), jnp.float32)
        for block in range(D // HALF):
            value = wide(read(slice(block * HALF, (block + 1) * HALF)))
            total = total + value * value
        inverse = lax.rsqrt(jnp.sum(total, axis=-1, keepdims=True) / D + epsilon)
        for block in range(D // HALF):
            cols = slice(block * HALF, (block + 1) * HALF)
            gain = gbuf[3:4, cols]
            for k in (2, 1, 0):
                gain = jnp.where(owner == k, gbuf[k : k + 1, cols], gain)
            write(cols, (wide(read(cols)) * inverse * gain).astype(jnp.bfloat16))

    def owners(base):
        part = tenant_ref[:, lanes(base, HALF)].astype(jnp.float32)
        return jnp.transpose(jnp.broadcast_to(part, (HALF, HALF)))

    def normalize(number):
        chunk = number // PARTS
        tbuf[...] = owners(number * high)

        @pl.loop(0, high // SUB)
        def _(t):
            per = part_rows // SUB
            base = (number % PARTS) * part_rows + (t % per) * SUB
            span = pl.ds(pl.multiple_of(base, SUB), SUB)
            to = pl.ds(pl.multiple_of(t * SUB, SUB), SUB)

            def write(cols, value):
                normed[to, cols] = value

            scaled(lambda cols: xbuf[chunk, t // per, span, cols], tbuf[to, :], write)

    def normalize_dec():
        def write(cols, value):
            normed[high : high + SUB, cols] = value

        scaled(lambda cols: xdec[:, cols], owners(PEERS * rows)[:SUB], write)

    def lift(tile, size):
        cols = slice(tile * size, (tile + 1) * size)
        gate = jnp.dot(normed[...], wg_ref[:, cols], preferred_element_type=jnp.float32)
        up = jnp.dot(normed[...], wu_ref[:, cols], preferred_element_type=jnp.float32)
        hidden[:, cols] = (gate / (1.0 + jnp.exp(-gate)) * up).astype(jnp.bfloat16)

    def lower(number):
        @pl.loop(0, D // QUAD)
        def _(tile):
            cols = lanes(tile * QUAD, QUAD)
            part = jnp.dot(hidden[...], wd_ref[:, cols], preferred_element_type=jnp.float32)
            part = part.astype(jnp.bfloat16)
            pbuf[number // PARTS, :, within(number), cols] = part[:high].reshape(
                SIDE, part_rows, QUAD
            )

            @pl.when(number == 0)
            def _():
                for i in range(SIDE):
                    piece = part[high:, i * HALF : (i + 1) * HALF]

                    @pl.when(tile < SIDE)
                    def _():
                        pdec[tile * SIDE + i, :, :HALF] = piece

                    @pl.when(tile >= SIDE)
                    def _():
                        pdec[i * SIDE + tile - SIDE, :, HALF:] = piece

    barrier = pltpu.get_barrier_semaphore()

    @pl.loop(1, PEERS)
    def _(k):
        pl.semaphore_signal(barrier, inc=1, device_id={"tok": ahead(k)}, device_id_type=MESH)

    @pl.loop(1, groups)
    def _(k):
        pl.semaphore_signal(
            barrier, inc=1, device_id={"grp": lax.rem(grp + k, groups)}, device_id_type=MESH
        )

    def local(src, dst, index):
        copy = pltpu.make_async_copy(src, dst, w_sem.at[index])
        copy.start()
        return copy

    fetch_pair = local(pair_hbm, pbuf.at[z, x, :, pl.ds(0, WIDE)], 5)
    fetch_query = local(query_hbm, qbuf, 6)
    fetch = local(cache_hbm, pbuf.at[0:2, :, :, pl.ds(WIDE, WIDE)], 0)
    for head in range(H):
        own[head : head + 1, :] = wide(dec_ref[:, head * HD : (head + 1) * HD])
    column[grp] = own[...].astype(jnp.bfloat16)
    fetch_pair.wait()
    pl.semaphore_wait(barrier, PEERS + groups - 2)

    @pl.loop(1, groups)
    def _(k):
        group_copy(k, False).start()

    for piece in range(PIECES):
        gather_start(k_args, piece, 0)
    for way in (0, 1):
        wz_copy(0, way, False).start()
    fetch_wo = local(wo_hbm, wbuf.at[z], 4)
    fetch_gain = local(gain_hbm, gbuf, 7)
    tall_at = pl.ds(pl.multiple_of(z * tall, tall), tall)
    last_at = pl.ds(PEERS * rows, PEERS)
    fetch_base = local(resid_hbm.at[tall_at, :], rbuf.at[z, pl.ds(0, tall), :], 8)
    fetch_last = local(resid_hbm.at[last_at, :], rbuf.at[z, pl.ds(tall, PEERS), :], 9)
    mask()
    near_order = ((0, 0), (1, 0), (0, 1), (2, 0), (1, 1), (3, 0), (2, 1), (3, 1))
    for piece, level in near_order:
        gather_step(k_args, piece, level)

    @pl.loop(1, groups)
    def _(k):
        group_copy(k, True).wait_recv()

    @pl.loop(0, PEERS)
    def _(t):
        request = request_ref[grp * PEERS + t]
        row = column[request // PEERS]
        held = request % PEERS == me
        outgoing[t] = jnp.where(held, wide(row), 0.0).astype(jnp.bfloat16)

    @pl.loop(1, PEERS)
    def _(k):
        query_copy(k, False).start()

    incoming[me] = outgoing[me]
    fetch_query.wait()

    def attend(piece):
        gather_step(k_args, piece, 3)
        prefill(piece)
        for way in (0, 1):
            a_copy(piece, 0, way, False).start()

    def pass_on(piece):
        for way in (0, 1):
            a_copy(piece, 0, way, True).wait_recv()
            a_copy(piece, 1, way, False).start()

    gather_step(k_args, 0, 2)
    for way in (0, 1):
        wz_copy(0, way, True).wait_recv()
    for way in (0, 1):
        wz_copy(1, way, False).start()
    for other in (1, 3):
        for way in (0, 1):
            wy_copy(other, 0, way, False).start()
        wc_copy(other, 0, False).start()
    gather_step(k_args, 1, 2)
    attend(0)
    for way in (0, 1):
        wz_copy(1, way, True).wait_recv()
    for way in (0, 1):
        wy_copy(2, 0, way, False).start()
    wc_copy(2, 0, False).start()
    gather_step(k_args, 2, 2)
    attend(1)
    pass_on(0)
    gather_step(k_args, 3, 2)
    for k in (1, 2, 3):
        for copy in base_copies(k, False):
            copy.start()
    attend(2)
    pass_on(1)
    fetch.wait()

    @pl.loop(1, PEERS)
    def _(k):
        query_copy(k, True).wait_recv()

    decode()

    @pl.loop(1, PEERS)
    def _(k):
        dec_copy(k, False).start()

    dbuf[me] = own[...]
    attend(3)
    pass_on(2)

    @pl.loop(0, PEERS)
    def _(t):
        tz, tx = t // SIDE, t % SIDE
        for half in (0, 1):
            source = lanes(t * BLOCK + half * HALF, HALF)
            inside = lanes(half * WIDE + tx * QUAD + tz * HALF, HALF)
            place = t * HALF if half == 0 else WIDE + tx * QUAD + tz * HALF
            target = lanes(place, HALF)
            pltpu.make_async_copy(wg_hbm.at[source, :], wg_ref.at[inside, :], w_sem.at[1]).start()
            pltpu.make_async_copy(wu_hbm.at[source, :], wu_ref.at[inside, :], w_sem.at[2]).start()
            pltpu.make_async_copy(wd_hbm.at[:, source], wd_ref.at[:, target], w_sem.at[3]).start()

    pass_on(3)
    for other in (1, 3, 2):
        for way in (0, 1):
            wy_copy(other, 0, way, True).wait_recv()
            wy_copy(other, 1, way, False).start()
            wc_copy(other, -WAYS[way], False).start()

    @pl.loop(1, PEERS)
    def _(k):
        dec_copy(k, True).wait_recv()

    for head in range(H):
        abuf[tall : tall + SUB, head * HD : (head + 1) * HD] = dbuf[:, head, :].astype(
            jnp.bfloat16
        )
    for other in (1, 3, 2):
        for way in (0, 1):
            wy_copy(other, 1, way, True).wait_recv()
        wc_copy(other, 2, False).start()
    for k in (1, 2, 3):
        for copy in base_copies(k, True):
            copy.wait_recv()
    for piece in range(PIECES):
        for way in (0, 1):
            a_copy(piece, 1, way, True).wait_recv()
    for other in (1, 2, 3):
        for offset in (-1, 0, 1, 2):
            wc_copy(other, offset, True).wait_recv()
    fetch_wo.wait()
    fetch_base.wait()
    fetch_last.wait()
    fetch_gain.wait()

    @pl.loop(0, SIDE)
    def _(other):
        project(other)

    for k in (1, 2, 3):
        for copy in xdec_copies(k, False):
            copy.start()

    @pl.loop(0, CHUNKS)
    def _(number):
        gather_start(x_args, number, 0)

    @pl.loop(0, PIECES)
    def _(piece):
        for level in range(4):
            gather_sent(k_args, piece, level)

    size = 256

    @pl.loop(0, CHUNKS + 6)
    def _(turn):
        s = turn - 3
        f_on = jnp.logical_and(s >= 1, s < CHUNKS + 1)

        def guarded(number, step, level, args=()):
            @pl.when(jnp.logical_and(number >= 0, number < CHUNKS))
            def _():
                step(*args, number, level)

        def gather(number, level):
            guarded(number, gather_step, level, (x_args,))

        def scatter(number, level):
            guarded(number, scatter_step, level)

        @pl.when(s == 1)
        def _():
            pltpu.make_async_copy(wg_ref, wg_ref, w_sem.at[1]).wait()
            pltpu.make_async_copy(wu_ref, wu_ref, w_sem.at[2]).wait()
            pltpu.make_async_copy(wd_ref, wd_ref, w_sem.at[3]).wait()
            for k in (1, 2, 3):
                for copy in xdec_copies(k, True):
                    copy.wait_recv()
            normalize_dec()

        @pl.when(f_on)
        def _():
            normalize(s - 1)

        scatter(s - 2, 0)
        gather(s + 3, 0)
        gather(s + 2, 1)

        @pl.when(f_on)
        def _():
            lift(0, size)

        scatter(s - 3, 2)
        gather(s + 1, 2)

        @pl.when(f_on)
        def _():
            lift(1, size)

        scatter(s - 2, 1)

        @pl.when(f_on)
        def _():
            for tile in range(2, ffw // size):
                lift(tile, size)

        scatter(s - 3, 3)

        @pl.when(f_on)
        def _():
            lower(s - 1)
            scatter_start(s - 1, 0)

        @pl.when(s == 1)
        def _():
            @pl.loop(1, PEERS)
            def _(k):
                fdec_copy(k, False).start()

        gather(s, 3)

    @pl.loop(1, PEERS)
    def _(k):
        fdec_copy(k, True).wait_recv()

    rdec[me] = pdec[me]
    total = wide(rdec[0])
    for t in range(1, PEERS):
        total = total + wide(rdec[t])
    for half in (0, 1):
        part = wide(xdec[:, mine(half)]) + total[:, half * HALF : (half + 1) * HALF]
        obuf[PEERS * rows : PEERS * rows + SUB, half * HALF : (half + 1) * HALF] = part.astype(
            jnp.bfloat16
        )
    ending = pl.ds(PEERS * rows, SUB)
    out_last = pltpu.make_async_copy(
        obuf.at[ending, :], out_hbm.at[ending, :], o_sem.at[CHUNKS]
    )
    out_last.start()

    @pl.loop(1, groups)
    def _(k):
        group_copy(k, False).wait_send()

    @pl.loop(1, PEERS)
    def _(k):
        query_copy(k, False).wait_send()
        dec_copy(k, False).wait_send()
        fdec_copy(k, False).wait_send()

    for way in (0, 1):
        for level in (0, 1):
            wz_copy(level, way, False).wait_send()
            for other in (1, 2, 3):
                wy_copy(other, level, way, False).wait_send()
            for piece in range(PIECES):
                a_copy(piece, level, way, False).wait_send()
    for other in (1, 2, 3):
        for offset in (-1, 0, 1, 2):
            wc_copy(other, offset, False).wait_send()
        for copy in base_copies(other, False) + tuple(xdec_copies(other, False)):
            copy.wait_send()

    @pl.loop(0, CHUNKS)
    def _(number):
        for level in range(4):
            gather_sent(x_args, number, level)
            scatter_sent(number, level)
        out_copy(number).wait()

    out_last.wait()


def layer_call(length, request, queries, pairs, segment, dec, cache, resid, owner, gains, *weights):
    wo, w_gate, w_up, w_down = weights
    rows = queries.shape[0]
    tall = SIDE * rows
    inner = rows // PARTS
    high = SIDE * inner
    ffw = w_gate.shape[1]
    groups = lax.axis_size("grp")
    vmem = pl.BlockSpec(memory_space=pltpu.VMEM)
    smem = pl.BlockSpec(memory_space=pltpu.SMEM)
    hbm = pl.BlockSpec(memory_space=pl.ANY)
    bf16 = jnp.bfloat16
    dma = pltpu.SemaphoreType.DMA
    pairs_of = lambda *shape: [dma(shape), dma(shape)]
    return pl.pallas_call(
        layer_kernel,
        out_shape=jax.ShapeDtypeStruct(resid.shape, bf16),
        in_specs=[smem, smem, hbm, hbm, vmem, vmem, hbm, hbm, vmem] + [hbm] * 5,
        out_specs=hbm,
        scratch_shapes=[
            pltpu.VMEM(queries.shape, bf16),
            pltpu.VMEM(gains.shape, jnp.float32),
            pltpu.VMEM(resid.shape, bf16),
            pltpu.VMEM((tall + SUB, D), bf16),
            pltpu.VMEM((SIDE, D, BLOCK), bf16),
            pltpu.VMEM((SIDE, SIDE, rows, D), bf16),
            pltpu.VMEM((SIDE, SIDE, rows, D), bf16),
            pltpu.VMEM((high + SUB, D), bf16),
            pltpu.VMEM((high + SUB, ffw), bf16),
            pltpu.VMEM((CHUNKS, 2, SIDE, inner, QUAD), bf16),
            pltpu.VMEM((CHUNKS, 2, 2, SIDE, inner, QUAD), bf16),
            pltpu.VMEM((CHUNKS, 2, SIDE, inner, HALF), bf16),
            pltpu.VMEM((CHUNKS, 2, 2, SIDE, inner, HALF), bf16),
            pltpu.VMEM(w_gate.shape, bf16),
            pltpu.VMEM(w_up.shape, bf16),
            pltpu.VMEM(w_down.shape, bf16),
            pltpu.VMEM((rows, WINDOW * rows), jnp.float32),
            pltpu.VMEM((HALF, HALF), jnp.float32),
            pltpu.VMEM((groups, H, HD), bf16),
            pltpu.VMEM((PEERS, H, HD), bf16),
            pltpu.VMEM((PEERS, H, HD), bf16),
            pltpu.VMEM((H, HD), jnp.float32),
            pltpu.VMEM((PEERS, H, HD), jnp.float32),
            pltpu.VMEM((SIDE, tall + SUB, BLOCK), bf16),
            pltpu.VMEM((SUB, D), bf16),
            pltpu.VMEM((PEERS, SUB, BLOCK), bf16),
            pltpu.VMEM((PEERS, SUB, BLOCK), bf16),
            dma((10,)),
            dma((CHUNKS + 1,)),
            *pairs_of(PIECES, 16),
            *pairs_of(groups),
            *pairs_of(PEERS),
            *pairs_of(PEERS),
            *pairs_of(PIECES, 4),
            *pairs_of(4),
            *pairs_of(12),
            *pairs_of(12),
            *pairs_of(8),
            *pairs_of(8),
            *pairs_of(CHUNKS, 16),
            *pairs_of(CHUNKS, 16),
            *pairs_of(PEERS),
        ],
        compiler_params=pltpu.CompilerParams(
            collective_id=1, has_side_effects=True, vmem_limit_bytes=67043328
        ),
        name="layer",
    )(length, request, queries, pairs, segment, dec, cache, resid, owner, gains, *weights)


def shards(
    pre_q,
    pre_kv,
    pre_segment,
    dec_q,
    cache,
    cache_len,
    slot_request,
    resid,
    wo,
    tenant,
    norm_gain,
    w_gate,
    w_up,
    w_down,
):
    rows = pre_q.shape[0]
    tokens, cols = resid.shape
    split = resid.reshape(PEERS, rows + 1, cols)
    natural = jnp.concatenate([split[:, :rows].reshape(PEERS * rows, cols), split[:, rows]], axis=0)
    owner = tenant[0].reshape(PEERS, rows + 1)
    main = owner[:, :rows].reshape(SIDE, CHUNKS, -1)
    owner = jnp.concatenate([jnp.swapaxes(main, 0, 1).reshape(-1), owner[:, rows]], axis=0)
    owner = jnp.pad(owner, (0, HALF - SUB)).reshape(1, -1)
    gains = norm_gain.reshape(-1, SIDE, SIDE, 2, HALF).transpose(0, 3, 2, 1, 4).reshape(-1, D)
    result = layer_call(
        cache_len,
        slot_request,
        pre_q,
        pre_kv,
        pre_segment,
        dec_q,
        cache.reshape(2, SIDE, -1, cache.shape[2]),
        natural,
        owner,
        gains,
        wo,
        w_gate,
        w_up,
        w_down,
    )
    main = result[: PEERS * rows].reshape(CHUNKS, SIDE, -1, cols)
    main = jnp.swapaxes(main, 0, 1).reshape(PEERS, rows, cols)
    last = result[PEERS * rows :].reshape(PEERS, 1, cols)
    return jnp.concatenate([main, last], axis=1).reshape(tokens, cols)


def solution(mesh):
    in_specs = (
        P(("grp", "tok"), None),
        P(("grp", "tok"), None),
        P("grp", None),
        P(("grp", "tok"), None),
        P(("grp", "tok"), None, None),
        P(("grp", "tok")),
        P(),
        P("grp", "tok"),
        P(None, "tok"),
        P("grp", None),
        P(),
        P(None, "tok"),
        P(None, "tok"),
        P("tok", None),
    )
    out_specs = P("grp", "tok")
    return jax.shard_map(shards, mesh=mesh, in_specs=in_specs, out_specs=out_specs, check_vma=False)
```

```python
import functools
import math

import jax
import jax.numpy as jnp
from jax import lax
from jax.experimental import pallas as pl
from jax.experimental.pallas import tpu as pltpu
from jax.sharding import PartitionSpec as P

D = 4096
H = 32
KVH = 8
HD = 128
SIDE = 4
PEERS = SIDE * SIDE
BLOCK = D // PEERS
HALF = BLOCK // 2
WIDE = D // 2
QUAD = SIDE * HALF
SUB = 16
PIECES = 4
CHUNKS = 4
PARTS = CHUNKS // SIDE
WINDOW = 10
CORES = 2

epsilon = 1e-05
MESH = pl.DeviceIdType.MESH
WAYS = (1, -1)


def layer_kernel(
    length_ref,
    request_ref,
    query_hbm,
    pair_hbm,
    segment_ref,
    dec_ref,
    cache_hbm,
    resid_hbm,
    tenant_ref,
    gain_hbm,
    wo_hbm,
    wg_hbm,
    wu_hbm,
    wd_hbm,
    out_hbm,
    qbuf,
    gbuf,
    obuf,
    abuf,
    wbuf,
    xbuf,
    pbuf,
    normed,
    hidden,
    r1,
    r2,
    r3,
    r4,
    wg_ref,
    wu_ref,
    wd_ref,
    bias,
    tbuf,
    column,
    outgoing,
    incoming,
    own,
    dbuf,
    rbuf,
    xdec,
    pdec,
    rdec,
    w_sem,
    o_sem,
    k_send,
    k_recv,
    g_send,
    g_recv,
    q_send,
    q_recv,
    d_send,
    d_recv,
    a_send,
    a_recv,
    wz_send,
    wz_recv,
    wy_send,
    wy_recv,
    wc_send,
    wc_recv,
    b_send,
    b_recv,
    e_send,
    e_recv,
    x_send,
    x_recv,
    p_send,
    p_recv,
    f_send,
    f_recv,
):
    me = lax.axis_index("tok")
    grp = lax.axis_index("grp")
    groups = column.shape[0]
    z, x = me // SIDE, me % SIDE
    y, core = grp // CORES, grp % CORES
    rows = query_hbm.shape[0]
    tall = SIDE * rows
    part_rows = rows // PARTS
    high = SIDE * part_rows
    width = KVH * HD
    group = H // KVH
    heads = KVH // PIECES
    ffw = wg_ref.shape[1]
    slab = D // groups
    scale = 1.0 / math.sqrt(HD)

    def hop(value, step):
        return lax.rem(value + step + SIDE, SIDE)

    def neighbour(axis, step):
        if axis == 0:
            return {"tok": z * SIDE + hop(x, step)}
        if axis == 1:
            return {"tok": hop(z, step) * SIDE + x}
        return {"grp": hop(y, step) * CORES + core}

    def remote(src, dst, sent, landed, peer):
        return pltpu.make_async_remote_copy(
            src_ref=src,
            dst_ref=dst,
            send_sem=sent,
            recv_sem=landed,
            device_id=peer,
            device_id_type=MESH,
        )

    def lanes(base, size):
        return pl.ds(pl.multiple_of(base, HALF), size)

    def wide(value):
        return value.astype(jnp.float32)

    def inner(part):
        if part is None:
            return pl.ds(0, rows)
        return pl.ds(part * (rows // 2), rows // 2)

    def k_block(piece, half, offset, level, part):
        cols = pl.ds(half * width + piece * heads * HD, heads * HD)
        span = inner(part)
        if level < 2:
            if half == 0:
                return pbuf.at[z, hop(x, offset), span, cols]
            return pbuf.at[hop(z, offset), x, span, cols]
        if half == 0:
            return pbuf.at[hop(z, offset), :, span, cols]
        return pbuf.at[:, hop(x, offset), span, cols]

    def within(chunk, part=None):
        base = (chunk % PARTS) * part_rows
        if part is None:
            return pl.ds(pl.multiple_of(base, SUB), part_rows)
        count = part_rows // 2
        return pl.ds(pl.multiple_of(base + part * count, SUB), count)

    def half_of(part):
        return pl.ds(part * (part_rows // 2), part_rows // 2)

    def x_block(number, half, offset, level, part):
        span = within(number, part)
        chunk = number // PARTS
        if level < 2:
            if half == 0:
                return xbuf.at[chunk, z, span, lanes(hop(x, offset) * QUAD, QUAD)]
            return xbuf.at[chunk, hop(z, offset), span, lanes(WIDE + x * QUAD, QUAD)]
        if half == 0:
            return xbuf.at[chunk, hop(z, offset), span, pl.ds(0, WIDE)]
        return xbuf.at[chunk, :, span, lanes(WIDE + hop(x, offset) * QUAD, QUAD)]

    def gather_copy(block, sends, recvs, chunk, level, half, way, arriving):
        step = WAYS[way]
        axis = half if level < 2 else 1 - half
        if level % 2 == 0:
            ref = block(chunk, half, -step if arriving else 0, level, None)
        else:
            ref = block(chunk, half, -2 * step if arriving else -step, level, way)
        index = level * 4 + half * 2 + way
        return remote(
            ref, ref, sends.at[chunk, index], recvs.at[chunk, index], neighbour(axis, step)
        )

    def each(make):
        for half in (0, 1):
            for way in (0, 1):
                make(half, way)

    def gather_start(args, chunk, level):
        each(lambda half, way: gather_copy(*args, chunk, level, half, way, False).start())

    def gather_step(args, chunk, level):
        each(lambda half, way: gather_copy(*args, chunk, level, half, way, True).wait_recv())
        if level < 3:
            gather_start(args, chunk, level + 1)

    def gather_sent(args, chunk, level):
        each(lambda half, way: gather_copy(*args, chunk, level, half, way, False).wait_send())

    k_args = (k_block, k_send, k_recv)
    x_args = (x_block, x_send, x_recv)

    def a_copy(piece, level, way, arriving):
        step = WAYS[way]
        offset = -step * (level + 1) if arriving else -step * level
        base = hop(x, offset) * rows
        count = rows
        if level == 1:
            base = base + way * (rows // 2)
            count = rows // 2
        cols = pl.ds(piece * (D // PIECES), D // PIECES)
        ref = abuf.at[pl.ds(pl.multiple_of(base, SUB), count), cols]
        index = level * 2 + way
        return remote(
            ref, ref, a_send.at[piece, index], a_recv.at[piece, index], neighbour(0, step)
        )

    def slab_rows(offset, part=None):
        base = (hop(y, offset) * CORES + core) * slab
        if part is None:
            return pl.ds(pl.multiple_of(base, slab // 2), slab)
        return pl.ds(pl.multiple_of(base + part * (slab // 2), slab // 2), slab // 2)

    def wz_copy(level, way, arriving):
        step = WAYS[way]
        offset = -step * (level + 1) if arriving else -step * level
        span = slab_rows(0, way if level == 1 else None)
        dst = wbuf.at[hop(z, offset), span, :]
        src = wo_hbm.at[span, :] if level == 0 and not arriving else dst
        index = level * 2 + way
        return remote(src, dst, wz_send.at[index], wz_recv.at[index], neighbour(1, step))

    def wy_copy(other, level, way, arriving):
        step = WAYS[way]
        offset = -step * (level + 1) if arriving else -step * level
        span = slab_rows(offset, way if level == 1 else None)
        ref = wbuf.at[hop(z, other), span, :]
        index = (other - 1) * 4 + level * 2 + way
        return remote(ref, ref, wy_send.at[index], wy_recv.at[index], neighbour(2, step))

    def wc_copy(other, offset, arriving):
        base = hop(y, offset) * CORES + (1 - core if arriving else core)
        ref = wbuf.at[hop(z, other), pl.ds(pl.multiple_of(base * slab, slab), slab), :]
        index = (other - 1) * 4 + offset + 1
        peer = {"grp": y * CORES + 1 - core}
        return remote(ref, ref, wc_send.at[index], wc_recv.at[index], peer)

    def group_copy(k, arriving):
        source = lax.rem(grp - k + groups, groups) if arriving else grp
        peer = {"grp": lax.rem(grp + k, groups)}
        return remote(column.at[grp], column.at[source], g_send.at[k], g_recv.at[k], peer)

    def ahead(k):
        return lax.rem(me + k, PEERS)

    def behind(k):
        return lax.rem(me - k + PEERS, PEERS)

    def query_copy(k, arriving):
        dst = incoming.at[behind(k) if arriving else me]
        return remote(outgoing.at[ahead(k)], dst, q_send.at[k], q_recv.at[k], {"tok": ahead(k)})

    def dec_copy(k, arriving):
        dst = dbuf.at[behind(k) if arriving else me]
        return remote(own, dst, d_send.at[k], d_recv.at[k], {"tok": ahead(k)})

    def fdec_copy(k, arriving):
        dst = rdec.at[behind(k) if arriving else me]
        return remote(pdec.at[ahead(k)], dst, f_send.at[k], f_recv.at[k], {"tok": ahead(k)})

    def base_copies(k, arriving):
        to = hop(z, k)
        slot = hop(z, -k) if arriving else z
        start = pl.ds(pl.multiple_of(to * tall, tall), tall)
        peer = {"tok": to * SIDE + x}
        last = pl.ds(PEERS * rows, PEERS)
        return (
            remote(
                resid_hbm.at[start, :],
                rbuf.at[slot, pl.ds(0, tall), :],
                b_send.at[2 * k],
                b_recv.at[2 * k],
                peer,
            ),
            remote(
                resid_hbm.at[last, :],
                rbuf.at[slot, pl.ds(tall, PEERS), :],
                b_send.at[2 * k + 1],
                b_recv.at[2 * k + 1],
                peer,
            ),
        )

    def xdec_copies(k, arriving):
        owner = hop(x, -k) if arriving else x
        peer = {"tok": z * SIDE + hop(x, k)}
        copies = []
        for half in (0, 1):
            ref = xdec.at[:, lanes(half * WIDE + owner * QUAD, QUAD)]
            index = 2 * k + half
            copies.append(remote(ref, ref, e_send.at[index], e_recv.at[index], peer))
        return copies

    def near_lanes(half, offset):
        if half == 0:
            return lanes(z * QUAD + hop(x, offset) * HALF, HALF)
        return lanes(WIDE + x * QUAD + hop(z, offset) * HALF, HALF)

    def far_lanes(half, offset):
        if half == 0:
            return lanes(hop(z, offset) * QUAD, QUAD)
        return lanes(WIDE + hop(x, offset) * QUAD, QUAD)

    def scatter_copy(number, level, half, way):
        step = WAYS[way]
        axis = 1 - half if level < 2 else half
        chunk, span = number // PARTS, within(number)
        if level == 0:
            src = pbuf.at[chunk, :, within(number, way), far_lanes(half, 2)]
            dst = r1.at[number, half, :, half_of(way), :]
        elif level == 1:
            src = pbuf.at[chunk, :, span, far_lanes(half, step)]
            dst = r2.at[number, half, way]
        elif level == 2:
            src = pbuf.at[chunk, :, within(number, way), near_lanes(half, 2)]
            dst = r3.at[number, half, :, half_of(way), :]
        else:
            src = pbuf.at[chunk, :, span, near_lanes(half, step)]
            dst = r4.at[number, half, way]
        index = level * 4 + half * 2 + way
        return remote(
            src, dst, p_send.at[number, index], p_recv.at[number, index], neighbour(axis, step)
        )

    def scatter_start(chunk, level):
        each(lambda half, way: scatter_copy(chunk, level, half, way).start())

    def mine(half):
        return lanes(half * WIDE + x * QUAD + z * HALF, HALF)

    def out_copy(number):
        span = pl.ds(pl.multiple_of(number * high, high), high)
        return pltpu.make_async_copy(obuf.at[span, :], out_hbm.at[span, :], o_sem.at[number])

    def scatter_step(number, level):
        chunk, span = number // PARTS, within(number)
        for half in (0, 1):
            for way in (0, 1):
                scatter_copy(number, level, half, way).wait_recv()
            if level % 2 == 0:
                for way in (0, 1):
                    cols = (far_lanes if level == 0 else near_lanes)(half, WAYS[way])
                    some = within(number, way)
                    landed = (r1 if level == 0 else r3)[number, half, :, half_of(way), :]
                    total = wide(pbuf[chunk, :, some, cols]) + wide(landed)
                    pbuf[chunk, :, some, cols] = total.astype(jnp.bfloat16)
                    scatter_copy(number, level + 1, half, way).start()
            elif level == 1:
                cols = far_lanes(half, 0)
                total = (
                    wide(pbuf[chunk, :, span, cols])
                    + wide(r2[number, half, 0])
                    + wide(r2[number, half, 1])
                )
                pbuf[chunk, :, span, cols] = total.astype(jnp.bfloat16)
                for way in (0, 1):
                    scatter_copy(number, 2, half, way).start()
            else:
                total = (
                    wide(pbuf[chunk, :, span, near_lanes(half, 0)])
                    + wide(r4[number, half, 0])
                    + wide(r4[number, half, 1])
                )
                total = wide(xbuf[chunk, :, span, mine(half)]) + total
                to = pl.ds(pl.multiple_of(number * high, high), high)
                obuf[to, half * HALF : (half + 1) * HALF] = total.astype(jnp.bfloat16).reshape(
                    high, HALF
                )
        if level == 3:
            out_copy(number).start()

    def scatter_sent(chunk, level):
        each(lambda half, way: scatter_copy(chunk, level, half, way).wait_send())

    first = 2 * (jnp.maximum(me - 8, 0) // 2)

    def mask():
        span = WINDOW * rows
        near = lanes((me // 2) * (2 * rows), 2 * rows)
        part = segment_ref[:, near].astype(jnp.float32)
        turned = jnp.transpose(jnp.broadcast_to(part, (2 * rows, 2 * rows)))
        query_seg = jnp.where(me % 2 == 1, turned[rows:], turned[:rows])[:, :1]
        key_seg = segment_ref[:, lanes(first * rows, span)].astype(jnp.float32)
        query_pos = me * rows + lax.broadcasted_iota(jnp.int32, (rows, span), 0)
        key_pos = first * rows + lax.broadcasted_iota(jnp.int32, (rows, span), 1)
        allowed = (key_pos <= query_pos) & (query_seg == key_seg)
        bias[...] = jnp.where(allowed, 0.0, -jnp.inf)

    def prefill(piece):
        @pl.loop(0, heads)
        def _(i):
            head = piece * heads + i

            def joined(base):
                cols = lanes(base + head * HD, HD)
                return jnp.concatenate(
                    [
                        pbuf[(first + b) // SIDE, (first + b) % SIDE, :, cols]
                        for b in range(WINDOW)
                    ],
                    axis=0,
                )

            keys, values = joined(0), joined(width)
            for j in range(group):
                cols = lanes((head * group + j) * HD, HD)
                scores = lax.dot_general(
                    qbuf[:, cols],
                    keys,
                    (((1,), (1,)), ((), ())),
                    preferred_element_type=jnp.float32,
                )
                scores = scores * scale + bias[...]
                top = jnp.max(scores, axis=-1, keepdims=True)
                weights = jnp.exp(scores - top).astype(jnp.bfloat16)
                total = jnp.sum(wide(weights), axis=-1, keepdims=True)
                summed = jnp.dot(weights, values, preferred_element_type=jnp.float32)
                to = pl.ds(pl.multiple_of(x * rows, rows), rows)
                abuf[to, cols] = (summed / total).astype(jnp.bfloat16)

    def decode():
        query = wide(incoming[0])
        for t in range(1, PEERS):
            query = query + wide(incoming[t])
        query = query.astype(jnp.bfloat16)
        count = 2 * tall

        def cached(base):
            return pbuf[0:2, :, :, WIDE + base : WIDE + base + HD].reshape(count, HD)

        owner = lax.broadcasted_iota(jnp.int32, (H, count), 0) // group
        scores = jnp.zeros((H, count), jnp.float32)
        for head in range(KVH):
            part = lax.dot_general(
                query,
                cached(head * HD),
                (((1,), (1,)), ((), ())),
                preferred_element_type=jnp.float32,
            )
            scores = jnp.where(owner == head, part, scores)
        visible = lax.broadcasted_iota(jnp.int32, (H, count), 1) < length_ref[0]
        scores = jnp.where(visible, scores * scale, -jnp.inf)
        top = jnp.max(scores, axis=-1, keepdims=True)
        weights = jnp.exp(scores - top).astype(jnp.bfloat16)
        total = jnp.sum(wide(weights), axis=-1, keepdims=True)
        owner = lax.broadcasted_iota(jnp.int32, (H, HD), 0) // group
        summed = jnp.zeros((H, HD), jnp.float32)
        for head in range(KVH):
            part = jnp.dot(
                weights, cached(width + head * HD), preferred_element_type=jnp.float32
            )
            summed = jnp.where(owner == head, part, summed)
        own[...] = summed / total

    def project(other):
        total = wide(rbuf[other]) + jnp.dot(
            abuf[...], wbuf[other], preferred_element_type=jnp.float32
        )
        value = total.astype(jnp.bfloat16)
        for half in (0, 1):
            to = lanes(half * WIDE + x * QUAD + other * HALF, HALF)
            part = value[:, half * HALF : (half + 1) * HALF]
            for chunk in range(SIDE):
                xbuf[chunk, z, :, to] = part[chunk * rows : (chunk + 1) * rows]
            xdec[:, to] = part[tall:]

    def scaled(read, owner, write):
        total = jnp.zeros((SUB, HALF), jnp.float32)
        for block in range(D // HALF):
            value = wide(read(slice(block * HALF, (block + 1) * HALF)))
            total = total + value * value
        inverse = lax.rsqrt(jnp.sum(total, axis=-1, keepdims=True) / D + epsilon)
        for block in range(D // HALF):
            cols = slice(block * HALF, (block + 1) * HALF)
            gain = gbuf[3:4, cols]
            for k in (2, 1, 0):
                gain = jnp.where(owner == k, gbuf[k : k + 1, cols], gain)
            write(cols, (wide(read(cols)) * inverse * gain).astype(jnp.bfloat16))

    def owners(base):
        part = tenant_ref[:, lanes(base, HALF)].astype(jnp.float32)
        return jnp.transpose(jnp.broadcast_to(part, (HALF, HALF)))

    def normalize(number):
        chunk = number // PARTS
        for q in range(high // HALF):
            tbuf[q * HALF : (q + 1) * HALF, :] = owners(number * high + q * HALF)

        @pl.loop(0, high // SUB)
        def _(t):
            per = part_rows // SUB
            base = (number % PARTS) * part_rows + (t % per) * SUB
            span = pl.ds(pl.multiple_of(base, SUB), SUB)
            to = pl.ds(pl.multiple_of(t * SUB, SUB), SUB)

            def write(cols, value):
                normed[to, cols] = value

            scaled(lambda cols: xbuf[chunk, t // per, span, cols], tbuf[to, :], write)

    def normalize_dec():
        def write(cols, value):
            normed[high : high + SUB, cols] = value

        scaled(lambda cols: xdec[:, cols], owners(PEERS * rows)[:SUB], write)

    def lift(tile, size):
        cols = slice(tile * size, (tile + 1) * size)
        gate = jnp.dot(normed[...], wg_ref[:, cols], preferred_element_type=jnp.float32)
        up = jnp.dot(normed[...], wu_ref[:, cols], preferred_element_type=jnp.float32)
        hidden[:, cols] = (gate / (1.0 + jnp.exp(-gate)) * up).astype(jnp.bfloat16)

    def lower(number):
        @pl.loop(0, D // QUAD)
        def _(tile):
            cols = lanes(tile * QUAD, QUAD)
            part = jnp.dot(hidden[...], wd_ref[:, cols], preferred_element_type=jnp.float32)
            part = part.astype(jnp.bfloat16)
            pbuf[number // PARTS, :, within(number), cols] = part[:high].reshape(
                SIDE, part_rows, QUAD
            )

            @pl.when(number == 0)
            def _():
                for i in range(SIDE):
                    piece = part[high:, i * HALF : (i + 1) * HALF]

                    @pl.when(tile < SIDE)
                    def _():
                        pdec[tile * SIDE + i, :, :HALF] = piece

                    @pl.when(tile >= SIDE)
                    def _():
                        pdec[i * SIDE + tile - SIDE, :, HALF:] = piece

    barrier = pltpu.get_barrier_semaphore()

    @pl.loop(1, PEERS)
    def _(k):
        pl.semaphore_signal(barrier, inc=1, device_id={"tok": ahead(k)}, device_id_type=MESH)

    @pl.loop(1, groups)
    def _(k):
        pl.semaphore_signal(
            barrier, inc=1, device_id={"grp": lax.rem(grp + k, groups)}, device_id_type=MESH
        )

    def local(src, dst, index):
        copy = pltpu.make_async_copy(src, dst, w_sem.at[index])
        copy.start()
        return copy

    fetch_pair = local(pair_hbm, pbuf.at[z, x, :, pl.ds(0, WIDE)], 5)
    fetch_query = local(query_hbm, qbuf, 6)
    fetch = local(cache_hbm, pbuf.at[0:2, :, :, pl.ds(WIDE, WIDE)], 0)
    for head in range(H):
        own[head : head + 1, :] = wide(dec_ref[:, head * HD : (head + 1) * HD])
    column[grp] = own[...].astype(jnp.bfloat16)
    fetch_pair.wait()
    pl.semaphore_wait(barrier, PEERS + groups - 2)

    @pl.loop(1, groups)
    def _(k):
        group_copy(k, False).start()

    for piece in range(PIECES):
        gather_start(k_args, piece, 0)
    for way in (0, 1):
        wz_copy(0, way, False).start()
    fetch_wo = local(wo_hbm, wbuf.at[z], 4)
    fetch_gain = local(gain_hbm, gbuf, 7)
    tall_at = pl.ds(pl.multiple_of(z * tall, tall), tall)
    last_at = pl.ds(PEERS * rows, PEERS)
    fetch_base = local(resid_hbm.at[tall_at, :], rbuf.at[z, pl.ds(0, tall), :], 8)
    fetch_last = local(resid_hbm.at[last_at, :], rbuf.at[z, pl.ds(tall, PEERS), :], 9)
    mask()
    near_order = ((0, 0), (1, 0), (0, 1), (2, 0), (1, 1), (3, 0), (2, 1), (3, 1))
    for piece, level in near_order:
        gather_step(k_args, piece, level)

    @pl.loop(1, groups)
    def _(k):
        group_copy(k, True).wait_recv()

    @pl.loop(0, PEERS)
    def _(t):
        request = request_ref[grp * PEERS + t]
        row = column[request // PEERS]
        held = request % PEERS == me
        outgoing[t] = jnp.where(held, wide(row), 0.0).astype(jnp.bfloat16)

    @pl.loop(1, PEERS)
    def _(k):
        query_copy(k, False).start()

    incoming[me] = outgoing[me]
    fetch_query.wait()

    def attend(piece):
        gather_step(k_args, piece, 3)
        prefill(piece)
        for way in (0, 1):
            a_copy(piece, 0, way, False).start()

    def pass_on(piece):
        for way in (0, 1):
            a_copy(piece, 0, way, True).wait_recv()
            a_copy(piece, 1, way, False).start()

    gather_step(k_args, 0, 2)
    for way in (0, 1):
        wz_copy(0, way, True).wait_recv()
    for way in (0, 1):
        wz_copy(1, way, False).start()
    for other in (1, 3):
        for way in (0, 1):
            wy_copy(other, 0, way, False).start()
        wc_copy(other, 0, False).start()
    gather_step(k_args, 1, 2)
    attend(0)
    for way in (0, 1):
        wz_copy(1, way, True).wait_recv()
    for way in (0, 1):
        wy_copy(2, 0, way, False).start()
    wc_copy(2, 0, False).start()
    gather_step(k_args, 2, 2)
    attend(1)
    pass_on(0)
    gather_step(k_args, 3, 2)
    for k in (1, 2, 3):
        for copy in base_copies(k, False):
            copy.start()
    attend(2)
    pass_on(1)
    fetch.wait()

    @pl.loop(1, PEERS)
    def _(k):
        query_copy(k, True).wait_recv()

    decode()

    @pl.loop(1, PEERS)
    def _(k):
        dec_copy(k, False).start()

    dbuf[me] = own[...]
    attend(3)
    pass_on(2)

    @pl.loop(0, PEERS)
    def _(t):
        tz, tx = t // SIDE, t % SIDE
        for half in (0, 1):
            source = lanes(t * BLOCK + half * HALF, HALF)
            inside = lanes(half * WIDE + tx * QUAD + tz * HALF, HALF)
            place = t * HALF if half == 0 else WIDE + tx * QUAD + tz * HALF
            target = lanes(place, HALF)
            pltpu.make_async_copy(wg_hbm.at[source, :], wg_ref.at[inside, :], w_sem.at[1]).start()
            pltpu.make_async_copy(wu_hbm.at[source, :], wu_ref.at[inside, :], w_sem.at[2]).start()
            pltpu.make_async_copy(wd_hbm.at[:, source], wd_ref.at[:, target], w_sem.at[3]).start()

    pass_on(3)
    for other in (1, 3, 2):
        for way in (0, 1):
            wy_copy(other, 0, way, True).wait_recv()
            wy_copy(other, 1, way, False).start()
            wc_copy(other, -WAYS[way], False).start()

    @pl.loop(1, PEERS)
    def _(k):
        dec_copy(k, True).wait_recv()

    for head in range(H):
        abuf[tall : tall + SUB, head * HD : (head + 1) * HD] = dbuf[:, head, :].astype(
            jnp.bfloat16
        )
    for other in (1, 3, 2):
        for way in (0, 1):
            wy_copy(other, 1, way, True).wait_recv()
        wc_copy(other, 2, False).start()
    for k in (1, 2, 3):
        for copy in base_copies(k, True):
            copy.wait_recv()
    for piece in range(PIECES):
        for way in (0, 1):
            a_copy(piece, 1, way, True).wait_recv()
    for other in (1, 2, 3):
        for offset in (-1, 0, 1, 2):
            wc_copy(other, offset, True).wait_recv()
    fetch_wo.wait()
    fetch_base.wait()
    fetch_last.wait()
    fetch_gain.wait()

    @pl.loop(0, SIDE)
    def _(other):
        project(other)

    for k in (1, 2, 3):
        for copy in xdec_copies(k, False):
            copy.start()

    @pl.loop(0, CHUNKS)
    def _(number):
        gather_start(x_args, number, 0)

    @pl.loop(0, PIECES)
    def _(piece):
        for level in range(4):
            gather_sent(k_args, piece, level)

    size = 256

    @pl.loop(0, CHUNKS + 8)
    def _(turn):
        s = turn - 3
        f_on = jnp.logical_and(s >= 1, s < CHUNKS + 1)

        def guarded(number, step, level, args=()):
            @pl.when(jnp.logical_and(number >= 0, number < CHUNKS))
            def _():
                step(*args, number, level)

        def gather(number, level):
            guarded(number, gather_step, level, (x_args,))

        def scatter(number, level):
            guarded(number, scatter_step, level)

        @pl.when(s == 1)
        def _():
            pltpu.make_async_copy(wg_ref, wg_ref, w_sem.at[1]).wait()
            pltpu.make_async_copy(wu_ref, wu_ref, w_sem.at[2]).wait()
            pltpu.make_async_copy(wd_ref, wd_ref, w_sem.at[3]).wait()
            for k in (1, 2, 3):
                for copy in xdec_copies(k, True):
                    copy.wait_recv()
            normalize_dec()

        @pl.when(f_on)
        def _():
            normalize(s - 1)

        gather(s + 3, 0)
        gather(s + 2, 1)
        gather(s + 1, 2)

        @pl.when(f_on)
        def _():
            lift(0, size)

        scatter(s - 5, 3)
        scatter(s - 4, 2)

        @pl.when(f_on)
        def _():
            lift(1, size)

        scatter(s - 3, 1)
        scatter(s - 2, 0)

        @pl.when(f_on)
        def _():
            for tile in range(2, ffw // size):
                lift(tile, size)
            lower(s - 1)
            scatter_start(s - 1, 0)

        @pl.when(s == 1)
        def _():
            @pl.loop(1, PEERS)
            def _(k):
                fdec_copy(k, False).start()

        gather(s, 3)

    @pl.loop(1, PEERS)
    def _(k):
        fdec_copy(k, True).wait_recv()

    rdec[me] = pdec[me]
    total = wide(rdec[0])
    for t in range(1, PEERS):
        total = total + wide(rdec[t])
    for half in (0, 1):
        part = wide(xdec[:, mine(half)]) + total[:, half * HALF : (half + 1) * HALF]
        obuf[PEERS * rows : PEERS * rows + SUB, half * HALF : (half + 1) * HALF] = part.astype(
            jnp.bfloat16
        )
    ending = pl.ds(PEERS * rows, SUB)
    out_last = pltpu.make_async_copy(
        obuf.at[ending, :], out_hbm.at[ending, :], o_sem.at[CHUNKS]
    )
    out_last.start()

    @pl.loop(1, groups)
    def _(k):
        group_copy(k, False).wait_send()

    @pl.loop(1, PEERS)
    def _(k):
        query_copy(k, False).wait_send()
        dec_copy(k, False).wait_send()
        fdec_copy(k, False).wait_send()

    for way in (0, 1):
        for level in (0, 1):
            wz_copy(level, way, False).wait_send()
            for other in (1, 2, 3):
                wy_copy(other, level, way, False).wait_send()
            for piece in range(PIECES):
                a_copy(piece, level, way, False).wait_send()
    for other in (1, 2, 3):
        for offset in (-1, 0, 1, 2):
            wc_copy(other, offset, False).wait_send()
        for copy in base_copies(other, False) + tuple(xdec_copies(other, False)):
            copy.wait_send()

    @pl.loop(0, CHUNKS)
    def _(number):
        for level in range(4):
            gather_sent(x_args, number, level)
            scatter_sent(number, level)
        out_copy(number).wait()

    out_last.wait()


def layer_call(length, request, queries, pairs, segment, dec, cache, resid, owner, gains, *weights):
    wo, w_gate, w_up, w_down = weights
    rows = queries.shape[0]
    tall = SIDE * rows
    inner = rows // PARTS
    high = SIDE * inner
    ffw = w_gate.shape[1]
    groups = lax.axis_size("grp")
    vmem = pl.BlockSpec(memory_space=pltpu.VMEM)
    smem = pl.BlockSpec(memory_space=pltpu.SMEM)
    hbm = pl.BlockSpec(memory_space=pl.ANY)
    bf16 = jnp.bfloat16
    dma = pltpu.SemaphoreType.DMA
    pairs_of = lambda *shape: [dma(shape), dma(shape)]
    return pl.pallas_call(
        layer_kernel,
        out_shape=jax.ShapeDtypeStruct(resid.shape, bf16),
        in_specs=[smem, smem, hbm, hbm, vmem, vmem, hbm, hbm, vmem] + [hbm] * 5,
        out_specs=hbm,
        scratch_shapes=[
            pltpu.VMEM(queries.shape, bf16),
            pltpu.VMEM(gains.shape, jnp.float32),
            pltpu.VMEM(resid.shape, bf16),
            pltpu.VMEM((tall + SUB, D), bf16),
            pltpu.VMEM((SIDE, D, BLOCK), bf16),
            pltpu.VMEM((SIDE, SIDE, rows, D), bf16),
            pltpu.VMEM((SIDE, SIDE, rows, D), bf16),
            pltpu.VMEM((high + SUB, D), bf16),
            pltpu.VMEM((high + SUB, ffw), bf16),
            pltpu.VMEM((CHUNKS, 2, SIDE, inner, QUAD), bf16),
            pltpu.VMEM((CHUNKS, 2, 2, SIDE, inner, QUAD), bf16),
            pltpu.VMEM((CHUNKS, 2, SIDE, inner, HALF), bf16),
            pltpu.VMEM((CHUNKS, 2, 2, SIDE, inner, HALF), bf16),
            pltpu.VMEM(w_gate.shape, bf16),
            pltpu.VMEM(w_up.shape, bf16),
            pltpu.VMEM(w_down.shape, bf16),
            pltpu.VMEM((rows, WINDOW * rows), jnp.float32),
            pltpu.VMEM((high, HALF), jnp.float32),
            pltpu.VMEM((groups, H, HD), bf16),
            pltpu.VMEM((PEERS, H, HD), bf16),
            pltpu.VMEM((PEERS, H, HD), bf16),
            pltpu.VMEM((H, HD), jnp.float32),
            pltpu.VMEM((PEERS, H, HD), jnp.float32),
            pltpu.VMEM((SIDE, tall + SUB, BLOCK), bf16),
            pltpu.VMEM((SUB, D), bf16),
            pltpu.VMEM((PEERS, SUB, BLOCK), bf16),
            pltpu.VMEM((PEERS, SUB, BLOCK), bf16),
            dma((10,)),
            dma((CHUNKS + 1,)),
            *pairs_of(PIECES, 16),
            *pairs_of(groups),
            *pairs_of(PEERS),
            *pairs_of(PEERS),
            *pairs_of(PIECES, 4),
            *pairs_of(4),
            *pairs_of(12),
            *pairs_of(12),
            *pairs_of(8),
            *pairs_of(8),
            *pairs_of(CHUNKS, 16),
            *pairs_of(CHUNKS, 16),
            *pairs_of(PEERS),
        ],
        compiler_params=pltpu.CompilerParams(
            collective_id=1, has_side_effects=True, vmem_limit_bytes=67043328
        ),
        name="layer",
    )(length, request, queries, pairs, segment, dec, cache, resid, owner, gains, *weights)


def shards(
    pre_q,
    pre_kv,
    pre_segment,
    dec_q,
    cache,
    cache_len,
    slot_request,
    resid,
    wo,
    tenant,
    norm_gain,
    w_gate,
    w_up,
    w_down,
):
    rows = pre_q.shape[0]
    tokens, cols = resid.shape
    split = resid.reshape(PEERS, rows + 1, cols)
    natural = jnp.concatenate([split[:, :rows].reshape(PEERS * rows, cols), split[:, rows]], axis=0)
    owner = tenant[0].reshape(PEERS, rows + 1)
    main = owner[:, :rows].reshape(SIDE, CHUNKS, -1)
    owner = jnp.concatenate([jnp.swapaxes(main, 0, 1).reshape(-1), owner[:, rows]], axis=0)
    owner = jnp.pad(owner, (0, HALF - SUB)).reshape(1, -1)
    gains = norm_gain.reshape(-1, SIDE, SIDE, 2, HALF).transpose(0, 3, 2, 1, 4).reshape(-1, D)
    result = layer_call(
        cache_len,
        slot_request,
        pre_q,
        pre_kv,
        pre_segment,
        dec_q,
        cache.reshape(2, SIDE, -1, cache.shape[2]),
        natural,
        owner,
        gains,
        wo,
        w_gate,
        w_up,
        w_down,
    )
    main = result[: PEERS * rows].reshape(CHUNKS, SIDE, -1, cols)
    main = jnp.swapaxes(main, 0, 1).reshape(PEERS, rows, cols)
    last = result[PEERS * rows :].reshape(PEERS, 1, cols)
    return jnp.concatenate([main, last], axis=1).reshape(tokens, cols)


def solution(mesh):
    in_specs = (
        P(("grp", "tok"), None),
        P(("grp", "tok"), None),
        P("grp", None),
        P(("grp", "tok"), None),
        P(("grp", "tok"), None, None),
        P(("grp", "tok")),
        P(),
        P("grp", "tok"),
        P(None, "tok"),
        P("grp", None),
        P(),
        P(None, "tok"),
        P(None, "tok"),
        P("tok", None),
    )
    out_specs = P("grp", "tok")
    return jax.shard_map(shards, mesh=mesh, in_specs=in_specs, out_specs=out_specs, check_vma=False)
```

```python
import functools
import math

import jax
import jax.numpy as jnp
from jax import lax
from jax.experimental import pallas as pl
from jax.experimental.pallas import tpu as pltpu
from jax.sharding import PartitionSpec as P

D = 4096
H = 32
KVH = 8
HD = 128
SIDE = 4
PEERS = SIDE * SIDE
BLOCK = D // PEERS
HALF = BLOCK // 2
WIDE = D // 2
QUAD = SIDE * HALF
SUB = 16
PIECES = 4
CHUNKS = 4
PARTS = CHUNKS // SIDE
WINDOW = 10
CORES = 2

epsilon = 1e-05
MESH = pl.DeviceIdType.MESH
WAYS = (1, -1)


def layer_kernel(
    length_ref,
    request_ref,
    query_hbm,
    pair_hbm,
    segment_ref,
    dec_ref,
    cache_hbm,
    resid_hbm,
    tenant_ref,
    gain_hbm,
    wo_hbm,
    wg_hbm,
    wu_hbm,
    wd_hbm,
    out_hbm,
    qbuf,
    gbuf,
    obuf,
    nbuf,
    ndec,
    tbase,
    abuf,
    wbuf,
    xbuf,
    pbuf,
    normed,
    hidden,
    r1,
    r2,
    r3,
    r4,
    wg_ref,
    wu_ref,
    wd_ref,
    bias,
    tbuf,
    column,
    outgoing,
    incoming,
    own,
    dbuf,
    rbuf,
    xdec,
    pdec,
    rdec,
    w_sem,
    o_sem,
    k_send,
    k_recv,
    g_send,
    g_recv,
    q_send,
    q_recv,
    d_send,
    d_recv,
    a_send,
    a_recv,
    wz_send,
    wz_recv,
    wy_send,
    wy_recv,
    wc_send,
    wc_recv,
    b_send,
    b_recv,
    e_send,
    e_recv,
    x_send,
    x_recv,
    p_send,
    p_recv,
    f_send,
    f_recv,
):
    me = lax.axis_index("tok")
    grp = lax.axis_index("grp")
    groups = column.shape[0]
    z, x = me // SIDE, me % SIDE
    y, core = grp // CORES, grp % CORES
    rows = query_hbm.shape[0]
    tall = SIDE * rows
    part_rows = rows // PARTS
    high = SIDE * part_rows
    width = KVH * HD
    group = H // KVH
    heads = KVH // PIECES
    ffw = wg_ref.shape[1]
    slab = D // groups
    scale = 1.0 / math.sqrt(HD)

    def hop(value, step):
        return lax.rem(value + step + SIDE, SIDE)

    def neighbour(axis, step):
        if axis == 0:
            return {"tok": z * SIDE + hop(x, step)}
        if axis == 1:
            return {"tok": hop(z, step) * SIDE + x}
        return {"grp": hop(y, step) * CORES + core}

    def remote(src, dst, sent, landed, peer):
        return pltpu.make_async_remote_copy(
            src_ref=src,
            dst_ref=dst,
            send_sem=sent,
            recv_sem=landed,
            device_id=peer,
            device_id_type=MESH,
        )

    def lanes(base, size):
        return pl.ds(pl.multiple_of(base, HALF), size)

    def wide(value):
        return value.astype(jnp.float32)

    def inner(part):
        if part is None:
            return pl.ds(0, rows)
        return pl.ds(part * (rows // 2), rows // 2)

    def k_block(piece, half, offset, level, part):
        cols = pl.ds(half * width + piece * heads * HD, heads * HD)
        span = inner(part)
        if level < 2:
            if half == 0:
                return pbuf.at[z, hop(x, offset), span, cols]
            return pbuf.at[hop(z, offset), x, span, cols]
        if half == 0:
            return pbuf.at[hop(z, offset), :, span, cols]
        return pbuf.at[:, hop(x, offset), span, cols]

    def within(chunk, part=None):
        base = (chunk % PARTS) * part_rows
        if part is None:
            return pl.ds(pl.multiple_of(base, SUB), part_rows)
        count = part_rows // 2
        return pl.ds(pl.multiple_of(base + part * count, SUB), count)

    def half_of(part):
        return pl.ds(part * (part_rows // 2), part_rows // 2)

    def x_block(number, half, offset, level, part):
        span = within(number, part)
        chunk = number // PARTS
        if level < 2:
            if half == 0:
                return xbuf.at[chunk, z, span, lanes(hop(x, offset) * QUAD, QUAD)]
            return xbuf.at[chunk, hop(z, offset), span, lanes(WIDE + x * QUAD, QUAD)]
        if half == 0:
            return xbuf.at[chunk, hop(z, offset), span, pl.ds(0, WIDE)]
        return xbuf.at[chunk, :, span, lanes(WIDE + hop(x, offset) * QUAD, QUAD)]

    def gather_copy(block, sends, recvs, chunk, level, half, way, arriving):
        step = WAYS[way]
        axis = half if level < 2 else 1 - half
        if level % 2 == 0:
            ref = block(chunk, half, -step if arriving else 0, level, None)
        else:
            ref = block(chunk, half, -2 * step if arriving else -step, level, way)
        index = level * 4 + half * 2 + way
        return remote(
            ref, ref, sends.at[chunk, index], recvs.at[chunk, index], neighbour(axis, step)
        )

    def each(make):
        for half in (0, 1):
            for way in (0, 1):
                make(half, way)

    def gather_start(args, chunk, level):
        each(lambda half, way: gather_copy(*args, chunk, level, half, way, False).start())

    def gather_step(args, chunk, level):
        for half in (0, 1):
            for way in (0, 1):
                gather_copy(*args, chunk, level, half, way, True).wait_recv()
                if level % 2 == 0:
                    gather_copy(*args, chunk, level + 1, half, way, False).start()
            if level == 1:
                for way in (0, 1):
                    gather_copy(*args, chunk, 2, half, way, False).start()

    def gather_sent(args, chunk, level):
        each(lambda half, way: gather_copy(*args, chunk, level, half, way, False).wait_send())

    k_args = (k_block, k_send, k_recv)
    x_args = (x_block, x_send, x_recv)

    def a_copy(piece, level, way, arriving):
        step = WAYS[way]
        offset = -step * (level + 1) if arriving else -step * level
        base = hop(x, offset) * rows
        count = rows
        if level == 1:
            base = base + way * (rows // 2)
            count = rows // 2
        cols = pl.ds(piece * (D // PIECES), D // PIECES)
        ref = abuf.at[pl.ds(pl.multiple_of(base, SUB), count), cols]
        index = level * 2 + way
        return remote(
            ref, ref, a_send.at[piece, index], a_recv.at[piece, index], neighbour(0, step)
        )

    def slab_rows(offset, part=None):
        base = (hop(y, offset) * CORES + core) * slab
        if part is None:
            return pl.ds(pl.multiple_of(base, slab // 2), slab)
        return pl.ds(pl.multiple_of(base + part * (slab // 2), slab // 2), slab // 2)

    def wz_copy(level, way, arriving):
        step = WAYS[way]
        offset = -step * (level + 1) if arriving else -step * level
        span = slab_rows(0, way if level == 1 else None)
        dst = wbuf.at[hop(z, offset), span, :]
        src = wo_hbm.at[span, :] if level == 0 and not arriving else dst
        index = level * 2 + way
        return remote(src, dst, wz_send.at[index], wz_recv.at[index], neighbour(1, step))

    def wy_copy(other, level, way, arriving):
        step = WAYS[way]
        offset = -step * (level + 1) if arriving else -step * level
        span = slab_rows(offset, way if level == 1 else None)
        ref = wbuf.at[hop(z, other), span, :]
        index = (other - 1) * 4 + level * 2 + way
        return remote(ref, ref, wy_send.at[index], wy_recv.at[index], neighbour(2, step))

    def wc_copy(other, offset, arriving):
        base = hop(y, offset) * CORES + (1 - core if arriving else core)
        ref = wbuf.at[hop(z, other), pl.ds(pl.multiple_of(base * slab, slab), slab), :]
        index = (other - 1) * 4 + offset + 1
        peer = {"grp": y * CORES + 1 - core}
        return remote(ref, ref, wc_send.at[index], wc_recv.at[index], peer)

    def group_copy(k, arriving):
        source = lax.rem(grp - k + groups, groups) if arriving else grp
        peer = {"grp": lax.rem(grp + k, groups)}
        return remote(column.at[grp], column.at[source], g_send.at[k], g_recv.at[k], peer)

    def ahead(k):
        return lax.rem(me + k, PEERS)

    def behind(k):
        return lax.rem(me - k + PEERS, PEERS)

    def query_copy(k, arriving):
        dst = incoming.at[behind(k) if arriving else me]
        return remote(outgoing.at[ahead(k)], dst, q_send.at[k], q_recv.at[k], {"tok": ahead(k)})

    def dec_copy(k, arriving):
        dst = dbuf.at[behind(k) if arriving else me]
        return remote(own, dst, d_send.at[k], d_recv.at[k], {"tok": ahead(k)})

    def fdec_copy(k, arriving):
        dst = rdec.at[behind(k) if arriving else me]
        return remote(pdec.at[ahead(k)], dst, f_send.at[k], f_recv.at[k], {"tok": ahead(k)})

    def base_copies(k, arriving):
        to = hop(z, k)
        slot = hop(z, -k) if arriving else z
        start = pl.ds(pl.multiple_of(to * tall, tall), tall)
        peer = {"tok": to * SIDE + x}
        last = pl.ds(PEERS * rows, PEERS)
        return (
            remote(
                nbuf.at[start, :],
                rbuf.at[slot, pl.ds(0, tall), :],
                b_send.at[2 * k],
                b_recv.at[2 * k],
                peer,
            ),
            remote(
                nbuf.at[last, :],
                rbuf.at[slot, pl.ds(tall, PEERS), :],
                b_send.at[2 * k + 1],
                b_recv.at[2 * k + 1],
                peer,
            ),
        )

    def xdec_copies(k, arriving):
        owner = hop(x, -k) if arriving else x
        peer = {"tok": z * SIDE + hop(x, k)}
        copies = []
        for half in (0, 1):
            ref = xdec.at[:, lanes(half * WIDE + owner * QUAD, QUAD)]
            index = 2 * k + half
            copies.append(remote(ref, ref, e_send.at[index], e_recv.at[index], peer))
        return copies

    def near_lanes(half, offset):
        if half == 0:
            return lanes(z * QUAD + hop(x, offset) * HALF, HALF)
        return lanes(WIDE + x * QUAD + hop(z, offset) * HALF, HALF)

    def far_lanes(half, offset):
        if half == 0:
            return lanes(hop(z, offset) * QUAD, QUAD)
        return lanes(WIDE + hop(x, offset) * QUAD, QUAD)

    def scatter_copy(number, level, half, way):
        step = WAYS[way]
        axis = 1 - half if level < 2 else half
        chunk, span = number // PARTS, within(number)
        if level == 0:
            src = pbuf.at[chunk, :, within(number, way), far_lanes(half, 2)]
            dst = r1.at[number, half, :, half_of(way), :]
        elif level == 1:
            src = pbuf.at[chunk, :, span, far_lanes(half, step)]
            dst = r2.at[number, half, way]
        elif level == 2:
            src = pbuf.at[chunk, :, within(number, way), near_lanes(half, 2)]
            dst = r3.at[number, half, :, half_of(way), :]
        else:
            src = pbuf.at[chunk, :, span, near_lanes(half, step)]
            dst = r4.at[number, half, way]
        index = level * 4 + half * 2 + way
        return remote(
            src, dst, p_send.at[number, index], p_recv.at[number, index], neighbour(axis, step)
        )

    def scatter_start(chunk, level):
        each(lambda half, way: scatter_copy(chunk, level, half, way).start())

    def mine(half):
        return lanes(half * WIDE + x * QUAD + z * HALF, HALF)

    def out_copy(number):
        span = pl.ds(pl.multiple_of(number * high, high), high)
        return pltpu.make_async_copy(obuf.at[span, :], out_hbm.at[span, :], o_sem.at[number])

    def scatter_step(number, level):
        chunk, span = number // PARTS, within(number)
        for half in (0, 1):
            if level % 2 == 1:
                for way in (0, 1):
                    scatter_copy(number, level, half, way).wait_recv()
            if level % 2 == 0:
                for way in (0, 1):
                    scatter_copy(number, level, half, way).wait_recv()
                    cols = (far_lanes if level == 0 else near_lanes)(half, WAYS[way])
                    some = within(number, way)
                    landed = (r1 if level == 0 else r3)[number, half, :, half_of(way), :]
                    total = wide(pbuf[chunk, :, some, cols]) + wide(landed)
                    pbuf[chunk, :, some, cols] = total.astype(jnp.bfloat16)
                    scatter_copy(number, level + 1, half, way).start()
            elif level == 1:
                cols = far_lanes(half, 0)
                total = (
                    wide(pbuf[chunk, :, span, cols])
                    + wide(r2[number, half, 0])
                    + wide(r2[number, half, 1])
                )
                pbuf[chunk, :, span, cols] = total.astype(jnp.bfloat16)
                for way in (0, 1):
                    scatter_copy(number, 2, half, way).start()
            else:
                total = (
                    wide(pbuf[chunk, :, span, near_lanes(half, 0)])
                    + wide(r4[number, half, 0])
                    + wide(r4[number, half, 1])
                )
                total = wide(xbuf[chunk, :, span, mine(half)]) + total
                to = pl.ds(pl.multiple_of(number * high, high), high)
                obuf[to, half * HALF : (half + 1) * HALF] = total.astype(jnp.bfloat16).reshape(
                    high, HALF
                )
        if level == 3:
            out_copy(number).start()

    def scatter_sent(chunk, level):
        each(lambda half, way: scatter_copy(chunk, level, half, way).wait_send())

    first = 2 * (jnp.maximum(me - 8, 0) // 2)

    def mask():
        span = WINDOW * rows
        near = lanes((me // 2) * (2 * rows), 2 * rows)
        part = segment_ref[:, near].astype(jnp.float32)
        turned = jnp.transpose(jnp.broadcast_to(part, (2 * rows, 2 * rows)))
        query_seg = jnp.where(me % 2 == 1, turned[rows:], turned[:rows])[:, :1]
        key_seg = segment_ref[:, lanes(first * rows, span)].astype(jnp.float32)
        query_pos = me * rows + lax.broadcasted_iota(jnp.int32, (rows, span), 0)
        key_pos = first * rows + lax.broadcasted_iota(jnp.int32, (rows, span), 1)
        allowed = (key_pos <= query_pos) & (query_seg == key_seg)
        bias[...] = jnp.where(allowed, 0.0, -jnp.inf)

    def prefill(piece):
        @pl.loop(0, heads)
        def _(i):
            head = piece * heads + i

            def joined(base):
                cols = lanes(base + head * HD, HD)
                return jnp.concatenate(
                    [
                        pbuf[(first + b) // SIDE, (first + b) % SIDE, :, cols]
                        for b in range(WINDOW)
                    ],
                    axis=0,
                )

            keys, values = joined(0), joined(width)
            for j in range(group):
                cols = lanes((head * group + j) * HD, HD)
                scores = lax.dot_general(
                    qbuf[:, cols],
                    keys,
                    (((1,), (1,)), ((), ())),
                    preferred_element_type=jnp.float32,
                )
                scores = scores * scale + bias[...]
                top = jnp.max(scores, axis=-1, keepdims=True)
                weights = jnp.exp(scores - top).astype(jnp.bfloat16)
                total = jnp.sum(wide(weights), axis=-1, keepdims=True)
                summed = jnp.dot(weights, values, preferred_element_type=jnp.float32)
                to = pl.ds(pl.multiple_of(x * rows, rows), rows)
                abuf[to, cols] = (summed / total).astype(jnp.bfloat16)

    def decode():
        query = wide(incoming[0])
        for t in range(1, PEERS):
            query = query + wide(incoming[t])
        query = query.astype(jnp.bfloat16)
        count = 2 * tall

        def cached(base):
            return pbuf[0:2, :, :, WIDE + base : WIDE + base + HD].reshape(count, HD)

        owner = lax.broadcasted_iota(jnp.int32, (H, count), 0) // group
        scores = jnp.zeros((H, count), jnp.float32)
        for head in range(KVH):
            part = lax.dot_general(
                query,
                cached(head * HD),
                (((1,), (1,)), ((), ())),
                preferred_element_type=jnp.float32,
            )
            scores = jnp.where(owner == head, part, scores)
        visible = lax.broadcasted_iota(jnp.int32, (H, count), 1) < length_ref[0]
        scores = jnp.where(visible, scores * scale, -jnp.inf)
        top = jnp.max(scores, axis=-1, keepdims=True)
        weights = jnp.exp(scores - top).astype(jnp.bfloat16)
        total = jnp.sum(wide(weights), axis=-1, keepdims=True)
        owner = lax.broadcasted_iota(jnp.int32, (H, HD), 0) // group
        summed = jnp.zeros((H, HD), jnp.float32)
        for head in range(KVH):
            part = jnp.dot(
                weights, cached(width + head * HD), preferred_element_type=jnp.float32
            )
            summed = jnp.where(owner == head, part, summed)
        own[...] = summed / total

    def project(other):
        total = wide(rbuf[other]) + jnp.dot(
            abuf[...], wbuf[other], preferred_element_type=jnp.float32
        )
        value = total.astype(jnp.bfloat16)
        for half in (0, 1):
            to = lanes(half * WIDE + x * QUAD + other * HALF, HALF)
            part = value[:, half * HALF : (half + 1) * HALF]
            for chunk in range(SIDE):
                xbuf[chunk, z, :, to] = part[chunk * rows : (chunk + 1) * rows]
            xdec[:, to] = part[tall:]

    def scaled(read, owner, write):
        total = jnp.zeros((SUB, HALF), jnp.float32)
        for block in range(D // HALF):
            value = wide(read(slice(block * HALF, (block + 1) * HALF)))
            total = total + value * value
        inverse = lax.rsqrt(jnp.sum(total, axis=-1, keepdims=True) / D + epsilon)
        for block in range(D // HALF):
            cols = slice(block * HALF, (block + 1) * HALF)
            gain = gbuf[3:4, cols]
            for k in (2, 1, 0):
                gain = jnp.where(owner == k, gbuf[k : k + 1, cols], gain)
            write(cols, (wide(read(cols)) * inverse * gain).astype(jnp.bfloat16))

    def owners(base):
        part = tbase[:, lanes(base, HALF)].astype(jnp.float32)
        return jnp.transpose(jnp.broadcast_to(part, (HALF, HALF)))

    def normalize(number):
        chunk = number // PARTS
        for q in range(high // HALF):
            tbuf[q * HALF : (q + 1) * HALF, :] = owners(number * high + q * HALF)

        @pl.loop(0, high // SUB)
        def _(t):
            per = part_rows // SUB
            base = (number % PARTS) * part_rows + (t % per) * SUB
            span = pl.ds(pl.multiple_of(base, SUB), SUB)
            to = pl.ds(pl.multiple_of(t * SUB, SUB), SUB)

            def write(cols, value):
                normed[to, cols] = value

            scaled(lambda cols: xbuf[chunk, t // per, span, cols], tbuf[to, :], write)

    def normalize_dec():
        def write(cols, value):
            normed[high : high + SUB, cols] = value

        scaled(lambda cols: xdec[:, cols], owners(PEERS * rows)[:SUB], write)

    def lift(tile, size):
        cols = slice(tile * size, (tile + 1) * size)
        gate = jnp.dot(normed[...], wg_ref[:, cols], preferred_element_type=jnp.float32)
        up = jnp.dot(normed[...], wu_ref[:, cols], preferred_element_type=jnp.float32)
        hidden[:, cols] = (gate / (1.0 + jnp.exp(-gate)) * up).astype(jnp.bfloat16)

    def lower(number):
        @pl.loop(0, D // QUAD)
        def _(i):
            base = jnp.where(i % 2 == 0, z, x)
            tile = (i % 2) * SIDE + (base + 2 - i // 2 + SIDE) % SIDE
            cols = lanes(tile * QUAD, QUAD)
            part = jnp.dot(hidden[...], wd_ref[:, cols], preferred_element_type=jnp.float32)
            part = part.astype(jnp.bfloat16)
            pbuf[number // PARTS, :, within(number), cols] = part[:high].reshape(
                SIDE, part_rows, QUAD
            )

            @pl.when(i == 1)
            def _():
                scatter_start(number, 0)

            @pl.when(number == 0)
            def _():
                for i in range(SIDE):
                    piece = part[high:, i * HALF : (i + 1) * HALF]

                    @pl.when(tile < SIDE)
                    def _():
                        pdec[tile * SIDE + i, :, :HALF] = piece

                    @pl.when(tile >= SIDE)
                    def _():
                        pdec[i * SIDE + tile - SIDE, :, HALF:] = piece

    barrier = pltpu.get_barrier_semaphore()

    @pl.loop(1, PEERS)
    def _(k):
        pl.semaphore_signal(barrier, inc=1, device_id={"tok": ahead(k)}, device_id_type=MESH)

    @pl.loop(1, groups)
    def _(k):
        pl.semaphore_signal(
            barrier, inc=1, device_id={"grp": lax.rem(grp + k, groups)}, device_id_type=MESH
        )

    def local(src, dst, index):
        copy = pltpu.make_async_copy(src, dst, w_sem.at[index])
        copy.start()
        return copy

    fetch_pair = local(pair_hbm, pbuf.at[z, x, :, pl.ds(0, WIDE)], 5)
    fetch_query = local(query_hbm, qbuf, 6)
    fetch = local(cache_hbm, pbuf.at[0:2, :, :, pl.ds(WIDE, WIDE)], 0)
    for head in range(H):
        own[head : head + 1, :] = wide(dec_ref[:, head * HD : (head + 1) * HD])
    column[grp] = own[...].astype(jnp.bfloat16)
    fetch_pair.wait()
    pl.semaphore_wait(barrier, PEERS + groups - 2)

    @pl.loop(1, groups)
    def _(k):
        group_copy(k, False).start()

    gather_start(k_args, 0, 0)
    for way in (0, 1):
        wz_copy(0, way, False).start()
    for piece in range(1, PIECES):
        gather_start(k_args, piece, 0)
    fetch_wo = local(wo_hbm, wbuf.at[z], 4)
    fetch_base = local(resid_hbm, obuf, 8)
    mask()
    near_order = ((0, 0), (1, 0), (0, 1), (2, 0), (1, 1), (3, 0), (2, 1), (3, 1))
    for piece, level in near_order:
        gather_step(k_args, piece, level)

    @pl.loop(1, groups)
    def _(k):
        group_copy(k, True).wait_recv()

    @pl.loop(0, PEERS)
    def _(t):
        request = request_ref[grp * PEERS + t]
        row = column[request // PEERS]
        held = request % PEERS == me
        outgoing[t] = jnp.where(held, wide(row), 0.0).astype(jnp.bfloat16)

    @pl.loop(1, PEERS)
    def _(k):
        query_copy(k, False).start()

    incoming[me] = outgoing[me]
    fetch_query.wait()

    def wo_along_y(other):
        for way in (0, 1):
            wy_copy(other, 0, way, True).wait_recv()
            wy_copy(other, 1, way, False).start()
            wc_copy(other, -WAYS[way], False).start()

    def wo_to_core(other):
        for way in (0, 1):
            wy_copy(other, 1, way, True).wait_recv()
        wc_copy(other, 2, False).start()

    def attend(piece):
        gather_step(k_args, piece, 3)
        prefill(piece)
        for way in (0, 1):
            a_copy(piece, 0, way, False).start()

    def pass_on(piece):
        for way in (0, 1):
            a_copy(piece, 0, way, True).wait_recv()
            a_copy(piece, 1, way, False).start()

    gather_step(k_args, 0, 2)
    for way in (0, 1):
        wz_copy(0, way, True).wait_recv()
    for way in (0, 1):
        wz_copy(1, way, False).start()
    for other in (1, 3):
        for way in (0, 1):
            wy_copy(other, 0, way, False).start()
        wc_copy(other, 0, False).start()
    gather_step(k_args, 1, 2)
    attend(0)
    for way in (0, 1):
        wz_copy(1, way, True).wait_recv()
    for way in (0, 1):
        wy_copy(2, 0, way, False).start()
    wc_copy(2, 0, False).start()
    gather_step(k_args, 2, 2)
    attend(1)
    pass_on(0)
    gather_step(k_args, 3, 2)
    fetch_base.wait()
    tbase[...] = jnp.zeros_like(tbase)
    for t in range(PEERS):
        for part in range(PARTS):
            at = ((t % SIDE) * PARTS + part) * high + (t // SIDE) * part_rows
            of = t * (rows + 1) + part * part_rows
            tbase[:, at : at + part_rows] = tenant_ref[:, of : of + part_rows]
        at, of = PEERS * rows + t, t * (rows + 1) + rows
        tbase[:, at : at + 1] = tenant_ref[:, of : of + 1]
        first_row = t * (rows + 1)
        nbuf[t * rows : (t + 1) * rows, :] = obuf[first_row : first_row + rows, :]
        own_row = wide(obuf[first_row + rows : first_row + rows + 1, :])
        ndec[t : t + 1, :] = own_row
    nbuf[PEERS * rows :, :] = ndec[...].astype(jnp.bfloat16)
    rbuf[z, 0:tall, :] = nbuf[pl.ds(pl.multiple_of(z * tall, tall), tall), :]
    rbuf[z, tall:, :] = nbuf[PEERS * rows :, :]
    for k in (1, 2, 3):
        for copy in base_copies(k, False):
            copy.start()
    attend(2)
    pass_on(1)
    wo_along_y(1)
    wo_along_y(3)
    attend(3)
    pass_on(2)
    fetch.wait()

    @pl.loop(1, PEERS)
    def _(k):
        query_copy(k, True).wait_recv()

    decode()

    @pl.loop(1, PEERS)
    def _(k):
        dec_copy(k, False).start()

    dbuf[me] = own[...]

    wo_along_y(2)

    @pl.loop(0, PEERS)
    def _(t):
        tz, tx = t // SIDE, t % SIDE
        for half in (0, 1):
            source = lanes(t * BLOCK + half * HALF, HALF)
            inside = lanes(half * WIDE + tx * QUAD + tz * HALF, HALF)
            place = t * HALF if half == 0 else WIDE + tx * QUAD + tz * HALF
            target = lanes(place, HALF)
            pltpu.make_async_copy(wg_hbm.at[source, :], wg_ref.at[inside, :], w_sem.at[1]).start()
            pltpu.make_async_copy(wu_hbm.at[source, :], wu_ref.at[inside, :], w_sem.at[2]).start()
            pltpu.make_async_copy(wd_hbm.at[:, source], wd_ref.at[:, target], w_sem.at[3]).start()
            pltpu.make_async_copy(gain_hbm.at[:, source], gbuf.at[:, inside], w_sem.at[7]).start()

    pass_on(3)
    wo_to_core(1)
    wo_to_core(3)

    @pl.loop(1, PEERS)
    def _(k):
        dec_copy(k, True).wait_recv()

    for head in range(H):
        abuf[tall : tall + SUB, head * HD : (head + 1) * HD] = dbuf[:, head, :].astype(
            jnp.bfloat16
        )
    for k in (1, 2, 3):
        for copy in base_copies(k, True):
            copy.wait_recv()
    for piece in range(PIECES):
        for way in (0, 1):
            a_copy(piece, 1, way, True).wait_recv()
    fetch_wo.wait()
    pltpu.make_async_copy(gbuf, gbuf, w_sem.at[7]).wait()

    for other in (0, 1, 3, 2):
        if other > 0:
            for offset in (-1, 0, 1, 2):
                wc_copy(other, offset, True).wait_recv()
        project(hop(z, other))
        if other == 0:
            wo_to_core(2)

    for k in (1, 2, 3):
        for copy in xdec_copies(k, False):
            copy.start()

    @pl.loop(0, CHUNKS)
    def _(number):
        gather_start(x_args, number, 0)

    @pl.loop(0, PIECES)
    def _(piece):
        for level in range(4):
            gather_sent(k_args, piece, level)

    size = 256

    @pl.loop(0, CHUNKS + 8)
    def _(turn):
        s = turn - 3
        f_on = jnp.logical_and(s >= 1, s < CHUNKS + 1)

        def guarded(number, step, level, args=()):
            @pl.when(jnp.logical_and(number >= 0, number < CHUNKS))
            def _():
                step(*args, number, level)

        def gather(number, level):
            guarded(number, gather_step, level, (x_args,))

        def scatter(number, level):
            guarded(number, scatter_step, level)

        @pl.when(s == 1)
        def _():
            pltpu.make_async_copy(wg_ref, wg_ref, w_sem.at[1]).wait()
            pltpu.make_async_copy(wu_ref, wu_ref, w_sem.at[2]).wait()
            pltpu.make_async_copy(wd_ref, wd_ref, w_sem.at[3]).wait()
            for k in (1, 2, 3):
                for copy in xdec_copies(k, True):
                    copy.wait_recv()
            normalize_dec()

        @pl.when(f_on)
        def _():
            normalize(s - 1)

        gather(s + 3, 0)
        gather(s + 2, 1)
        gather(s + 1, 2)

        @pl.when(f_on)
        def _():
            lift(0, size)

        scatter(s - 5, 3)
        scatter(s - 4, 2)

        @pl.when(f_on)
        def _():
            lift(1, size)

        scatter(s - 3, 1)
        scatter(s - 2, 0)

        @pl.when(f_on)
        def _():
            for tile in range(2, ffw // size):
                lift(tile, size)
            lower(s - 1)

        @pl.when(s == 1)
        def _():
            @pl.loop(1, PEERS)
            def _(k):
                fdec_copy(k, False).start()

        gather(s, 3)

    @pl.loop(1, PEERS)
    def _(k):
        fdec_copy(k, True).wait_recv()

    rdec[me] = pdec[me]
    total = wide(rdec[0])
    for t in range(1, PEERS):
        total = total + wide(rdec[t])
    for half in (0, 1):
        part = wide(xdec[:, mine(half)]) + total[:, half * HALF : (half + 1) * HALF]
        obuf[PEERS * rows : PEERS * rows + SUB, half * HALF : (half + 1) * HALF] = part.astype(
            jnp.bfloat16
        )
    ending = pl.ds(PEERS * rows, SUB)
    out_last = pltpu.make_async_copy(
        obuf.at[ending, :], out_hbm.at[ending, :], o_sem.at[CHUNKS]
    )
    out_last.start()

    @pl.loop(1, groups)
    def _(k):
        group_copy(k, False).wait_send()

    @pl.loop(1, PEERS)
    def _(k):
        query_copy(k, False).wait_send()
        dec_copy(k, False).wait_send()
        fdec_copy(k, False).wait_send()

    for way in (0, 1):
        for level in (0, 1):
            wz_copy(level, way, False).wait_send()
            for other in (1, 2, 3):
                wy_copy(other, level, way, False).wait_send()
            for piece in range(PIECES):
                a_copy(piece, level, way, False).wait_send()
    for other in (1, 2, 3):
        for offset in (-1, 0, 1, 2):
            wc_copy(other, offset, False).wait_send()
        for copy in base_copies(other, False) + tuple(xdec_copies(other, False)):
            copy.wait_send()

    @pl.loop(0, CHUNKS)
    def _(number):
        for level in range(4):
            gather_sent(x_args, number, level)
            scatter_sent(number, level)
        out_copy(number).wait()

    out_last.wait()


def layer_call(length, request, queries, pairs, segment, dec, cache, resid, owner, gains, *weights):
    wo, w_gate, w_up, w_down = weights
    rows = queries.shape[0]
    tall = SIDE * rows
    inner = rows // PARTS
    high = SIDE * inner
    ffw = w_gate.shape[1]
    groups = lax.axis_size("grp")
    vmem = pl.BlockSpec(memory_space=pltpu.VMEM)
    smem = pl.BlockSpec(memory_space=pltpu.SMEM)
    hbm = pl.BlockSpec(memory_space=pl.ANY)
    bf16 = jnp.bfloat16
    dma = pltpu.SemaphoreType.DMA
    pairs_of = lambda *shape: [dma(shape), dma(shape)]
    return pl.pallas_call(
        layer_kernel,
        out_shape=jax.ShapeDtypeStruct(resid.shape, bf16),
        in_specs=[smem, smem, hbm, hbm, vmem, vmem, hbm, hbm, vmem] + [hbm] * 5,
        out_specs=hbm,
        scratch_shapes=[
            pltpu.VMEM(queries.shape, bf16),
            pltpu.VMEM(gains.shape, jnp.float32),
            pltpu.VMEM(resid.shape, bf16),
            pltpu.VMEM(resid.shape, bf16),
            pltpu.VMEM((PEERS, BLOCK), jnp.float32),
            pltpu.VMEM((1, resid.shape[0] + HALF - SUB), jnp.int32),
            pltpu.VMEM((tall + SUB, D), bf16),
            pltpu.VMEM((SIDE, D, BLOCK), bf16),
            pltpu.VMEM((SIDE, SIDE, rows, D), bf16),
            pltpu.VMEM((SIDE, SIDE, rows, D), bf16),
            pltpu.VMEM((high + SUB, D), bf16),
            pltpu.VMEM((high + SUB, ffw), bf16),
            pltpu.VMEM((CHUNKS, 2, SIDE, inner, QUAD), bf16),
            pltpu.VMEM((CHUNKS, 2, 2, SIDE, inner, QUAD), bf16),
            pltpu.VMEM((CHUNKS, 2, SIDE, inner, HALF), bf16),
            pltpu.VMEM((CHUNKS, 2, 2, SIDE, inner, HALF), bf16),
            pltpu.VMEM(w_gate.shape, bf16),
            pltpu.VMEM(w_up.shape, bf16),
            pltpu.VMEM(w_down.shape, bf16),
            pltpu.VMEM((rows, WINDOW * rows), jnp.float32),
            pltpu.VMEM((high, HALF), jnp.float32),
            pltpu.VMEM((groups, H, HD), bf16),
            pltpu.VMEM((PEERS, H, HD), bf16),
            pltpu.VMEM((PEERS, H, HD), bf16),
            pltpu.VMEM((H, HD), jnp.float32),
            pltpu.VMEM((PEERS, H, HD), jnp.float32),
            pltpu.VMEM((SIDE, tall + SUB, BLOCK), bf16),
            pltpu.VMEM((SUB, D), bf16),
            pltpu.VMEM((PEERS, SUB, BLOCK), bf16),
            pltpu.VMEM((PEERS, SUB, BLOCK), bf16),
            dma((10,)),
            dma((CHUNKS + 1,)),
            *pairs_of(PIECES, 16),
            *pairs_of(groups),
            *pairs_of(PEERS),
            *pairs_of(PEERS),
            *pairs_of(PIECES, 4),
            *pairs_of(4),
            *pairs_of(12),
            *pairs_of(12),
            *pairs_of(8),
            *pairs_of(8),
            *pairs_of(CHUNKS, 16),
            *pairs_of(CHUNKS, 16),
            *pairs_of(PEERS),
        ],
        compiler_params=pltpu.CompilerParams(
            collective_id=1, has_side_effects=True, vmem_limit_bytes=67043328
        ),
        name="layer",
    )(length, request, queries, pairs, segment, dec, cache, resid, owner, gains, *weights)


def shards(
    pre_q,
    pre_kv,
    pre_segment,
    dec_q,
    cache,
    cache_len,
    slot_request,
    resid,
    wo,
    tenant,
    norm_gain,
    w_gate,
    w_up,
    w_down,
):
    rows = pre_q.shape[0]
    tokens, cols = resid.shape
    result = layer_call(
        cache_len,
        slot_request,
        pre_q,
        pre_kv,
        pre_segment,
        dec_q,
        cache.reshape(2, SIDE, -1, cache.shape[2]),
        resid,
        tenant,
        norm_gain,
        wo,
        w_gate,
        w_up,
        w_down,
    )
    main = result[: PEERS * rows].reshape(CHUNKS, SIDE, -1, cols)
    main = jnp.swapaxes(main, 0, 1).reshape(PEERS, rows, cols)
    last = result[PEERS * rows :].reshape(PEERS, 1, cols)
    return jnp.concatenate([main, last], axis=1).reshape(tokens, cols)


def solution(mesh):
    in_specs = (
        P(("grp", "tok"), None),
        P(("grp", "tok"), None),
        P("grp", None),
        P(("grp", "tok"), None),
        P(("grp", "tok"), None, None),
        P(("grp", "tok")),
        P(),
        P("grp", "tok"),
        P(None, "tok"),
        P("grp", None),
        P(),
        P(None, "tok"),
        P(None, "tok"),
        P("tok", None),
    )
    out_specs = P("grp", "tok")
    return jax.shard_map(shards, mesh=mesh, in_specs=in_specs, out_specs=out_specs, check_vma=False)
```

```python
import functools
import math

import jax
import jax.numpy as jnp
from jax import lax
from jax.experimental import pallas as pl
from jax.experimental.pallas import tpu as pltpu
from jax.sharding import PartitionSpec as P

D = 4096
H = 32
KVH = 8
HD = 128
SIDE = 4
PEERS = SIDE * SIDE
BLOCK = D // PEERS
HALF = BLOCK // 2
WIDE = D // 2
QUAD = SIDE * HALF
SUB = 16
PIECES = 4
CHUNKS = 4
PARTS = CHUNKS // SIDE
WINDOW = 10
CORES = 2

epsilon = 1e-05
MESH = pl.DeviceIdType.MESH
WAYS = (1, -1)


def layer_kernel(
    length_ref,
    request_ref,
    query_hbm,
    pair_hbm,
    segment_ref,
    dec_ref,
    cache_hbm,
    resid_hbm,
    tenant_ref,
    gain_hbm,
    wo_hbm,
    wg_hbm,
    wu_hbm,
    wd_hbm,
    out_hbm,
    qbuf,
    gbuf,
    obuf,
    nbuf,
    ndec,
    tbase,
    abuf,
    wbuf,
    xbuf,
    pbuf,
    normed,
    hidden,
    r1,
    r2,
    r3,
    r4,
    wg_ref,
    wu_ref,
    wd_ref,
    bias,
    tbuf,
    column,
    outgoing,
    incoming,
    own,
    dbuf,
    rbuf,
    xdec,
    pdec,
    rdec,
    w_sem,
    o_sem,
    k_send,
    k_recv,
    g_send,
    g_recv,
    q_send,
    q_recv,
    d_send,
    d_recv,
    a_send,
    a_recv,
    wz_send,
    wz_recv,
    wy_send,
    wy_recv,
    wc_send,
    wc_recv,
    b_send,
    b_recv,
    e_send,
    e_recv,
    x_send,
    x_recv,
    p_send,
    p_recv,
    f_send,
    f_recv,
):
    me = lax.axis_index("tok")
    grp = lax.axis_index("grp")
    groups = column.shape[0]
    z, x = me // SIDE, me % SIDE
    y, core = grp // CORES, grp % CORES
    rows = query_hbm.shape[0]
    tall = SIDE * rows
    part_rows = rows // PARTS
    high = SIDE * part_rows
    width = KVH * HD
    group = H // KVH
    heads = KVH // PIECES
    ffw = wg_ref.shape[1]
    slab = D // groups
    scale = 1.0 / math.sqrt(HD)

    def hop(value, step):
        return lax.rem(value + step + SIDE, SIDE)

    def neighbour(axis, step):
        if axis == 0:
            return {"tok": z * SIDE + hop(x, step)}
        if axis == 1:
            return {"tok": hop(z, step) * SIDE + x}
        return {"grp": hop(y, step) * CORES + core}

    def remote(src, dst, sent, landed, peer):
        return pltpu.make_async_remote_copy(
            src_ref=src,
            dst_ref=dst,
            send_sem=sent,
            recv_sem=landed,
            device_id=peer,
            device_id_type=MESH,
        )

    def lanes(base, size):
        return pl.ds(pl.multiple_of(base, HALF), size)

    def wide(value):
        return value.astype(jnp.float32)

    def inner(part):
        if part is None:
            return pl.ds(0, rows)
        return pl.ds(part * (rows // 2), rows // 2)

    def k_block(piece, half, offset, level, part):
        cols = pl.ds(half * width + piece * heads * HD, heads * HD)
        span = inner(part)
        if level < 2:
            if half == 0:
                return pbuf.at[z, hop(x, offset), span, cols]
            return pbuf.at[hop(z, offset), x, span, cols]
        if half == 0:
            return pbuf.at[hop(z, offset), :, span, cols]
        return pbuf.at[:, hop(x, offset), span, cols]

    def within(chunk, part=None):
        base = (chunk % PARTS) * part_rows
        if part is None:
            return pl.ds(pl.multiple_of(base, SUB), part_rows)
        count = part_rows // 2
        return pl.ds(pl.multiple_of(base + part * count, SUB), count)

    def half_of(part):
        return pl.ds(part * (part_rows // 2), part_rows // 2)

    def x_block(number, half, offset, level, part):
        span = within(number, part)
        chunk = number // PARTS
        if level < 2:
            if half == 0:
                return xbuf.at[chunk, z, span, lanes(hop(x, offset) * QUAD, QUAD)]
            return xbuf.at[chunk, hop(z, offset), span, lanes(WIDE + x * QUAD, QUAD)]
        if half == 0:
            return xbuf.at[chunk, hop(z, offset), span, pl.ds(0, WIDE)]
        return xbuf.at[chunk, :, span, lanes(WIDE + hop(x, offset) * QUAD, QUAD)]

    def gather_copy(block, sends, recvs, chunk, level, half, way, arriving):
        step = WAYS[way]
        axis = half if level < 2 else 1 - half
        if level % 2 == 0:
            ref = block(chunk, half, -step if arriving else 0, level, None)
        else:
            ref = block(chunk, half, -2 * step if arriving else -step, level, way)
        index = level * 4 + half * 2 + way
        return remote(
            ref, ref, sends.at[chunk, index], recvs.at[chunk, index], neighbour(axis, step)
        )

    def each(make):
        for half in (0, 1):
            for way in (0, 1):
                make(half, way)

    def gather_start(args, chunk, level):
        each(lambda half, way: gather_copy(*args, chunk, level, half, way, False).start())

    def gather_step(args, chunk, level):
        for half in (0, 1):
            for way in (0, 1):
                gather_copy(*args, chunk, level, half, way, True).wait_recv()
                if level % 2 == 0:
                    gather_copy(*args, chunk, level + 1, half, way, False).start()
            if level == 1:
                for way in (0, 1):
                    gather_copy(*args, chunk, 2, half, way, False).start()

    def gather_sent(args, chunk, level):
        each(lambda half, way: gather_copy(*args, chunk, level, half, way, False).wait_send())

    k_args = (k_block, k_send, k_recv)
    x_args = (x_block, x_send, x_recv)

    def a_copy(piece, level, way, arriving):
        step = WAYS[way]
        offset = -step * (level + 1) if arriving else -step * level
        base = hop(x, offset) * rows
        count = rows
        if level == 1:
            base = base + way * (rows // 2)
            count = rows // 2
        cols = pl.ds(piece * (D // PIECES), D // PIECES)
        ref = abuf.at[pl.ds(pl.multiple_of(base, SUB), count), cols]
        index = level * 2 + way
        return remote(
            ref, ref, a_send.at[piece, index], a_recv.at[piece, index], neighbour(0, step)
        )

    def slab_rows(offset, part=None):
        base = (hop(y, offset) * CORES + core) * slab
        if part is None:
            return pl.ds(pl.multiple_of(base, slab // 2), slab)
        return pl.ds(pl.multiple_of(base + part * (slab // 2), slab // 2), slab // 2)

    def wz_copy(level, way, arriving):
        step = WAYS[way]
        offset = -step * (level + 1) if arriving else -step * level
        span = slab_rows(0, way if level == 1 else None)
        dst = wbuf.at[hop(z, offset), span, :]
        src = wo_hbm.at[span, :] if level == 0 and not arriving else dst
        index = level * 2 + way
        return remote(src, dst, wz_send.at[index], wz_recv.at[index], neighbour(1, step))

    def wy_copy(other, level, way, arriving):
        step = WAYS[way]
        offset = -step * (level + 1) if arriving else -step * level
        span = slab_rows(offset, way if level == 1 else None)
        ref = wbuf.at[hop(z, other), span, :]
        index = (other - 1) * 4 + level * 2 + way
        return remote(ref, ref, wy_send.at[index], wy_recv.at[index], neighbour(2, step))

    def wc_copy(other, offset, arriving):
        base = hop(y, offset) * CORES + (1 - core if arriving else core)
        ref = wbuf.at[hop(z, other), pl.ds(pl.multiple_of(base * slab, slab), slab), :]
        index = (other - 1) * 4 + offset + 1
        peer = {"grp": y * CORES + 1 - core}
        return remote(ref, ref, wc_send.at[index], wc_recv.at[index], peer)

    def group_copy(k, arriving):
        source = lax.rem(grp - k + groups, groups) if arriving else grp
        peer = {"grp": lax.rem(grp + k, groups)}
        return remote(column.at[grp], column.at[source], g_send.at[k], g_recv.at[k], peer)

    def ahead(k):
        return lax.rem(me + k, PEERS)

    def behind(k):
        return lax.rem(me - k + PEERS, PEERS)

    def query_copy(k, arriving):
        dst = incoming.at[behind(k) if arriving else me]
        return remote(outgoing.at[ahead(k)], dst, q_send.at[k], q_recv.at[k], {"tok": ahead(k)})

    def dec_copy(k, arriving):
        dst = dbuf.at[behind(k) if arriving else me]
        return remote(own, dst, d_send.at[k], d_recv.at[k], {"tok": ahead(k)})

    def fdec_copy(k, arriving):
        dst = rdec.at[behind(k) if arriving else me]
        return remote(pdec.at[ahead(k)], dst, f_send.at[k], f_recv.at[k], {"tok": ahead(k)})

    def base_copies(k, arriving):
        to = hop(z, k)
        slot = hop(z, -k) if arriving else z
        start = pl.ds(pl.multiple_of(to * tall, tall), tall)
        peer = {"tok": to * SIDE + x}
        last = pl.ds(PEERS * rows, PEERS)
        return (
            remote(
                nbuf.at[start, :],
                rbuf.at[slot, pl.ds(0, tall), :],
                b_send.at[2 * k],
                b_recv.at[2 * k],
                peer,
            ),
            remote(
                nbuf.at[last, :],
                rbuf.at[slot, pl.ds(tall, PEERS), :],
                b_send.at[2 * k + 1],
                b_recv.at[2 * k + 1],
                peer,
            ),
        )

    def xdec_copies(k, arriving):
        owner = hop(x, -k) if arriving else x
        peer = {"tok": z * SIDE + hop(x, k)}
        copies = []
        for half in (0, 1):
            ref = xdec.at[:, lanes(half * WIDE + owner * QUAD, QUAD)]
            index = 2 * k + half
            copies.append(remote(ref, ref, e_send.at[index], e_recv.at[index], peer))
        return copies

    def near_lanes(half, offset):
        if half == 0:
            return lanes(z * QUAD + hop(x, offset) * HALF, HALF)
        return lanes(WIDE + x * QUAD + hop(z, offset) * HALF, HALF)

    def far_lanes(half, offset):
        if half == 0:
            return lanes(hop(z, offset) * QUAD, QUAD)
        return lanes(WIDE + hop(x, offset) * QUAD, QUAD)

    def scatter_copy(number, level, half, way):
        step = WAYS[way]
        axis = 1 - half if level < 2 else half
        chunk, span = number // PARTS, within(number)
        if level == 0:
            src = pbuf.at[chunk, :, within(number, way), far_lanes(half, 2)]
            dst = r1.at[number, half, :, half_of(way), :]
        elif level == 1:
            src = pbuf.at[chunk, :, span, far_lanes(half, step)]
            dst = r2.at[number, half, way]
        elif level == 2:
            src = pbuf.at[chunk, :, within(number, way), near_lanes(half, 2)]
            dst = r3.at[number, half, :, half_of(way), :]
        else:
            src = pbuf.at[chunk, :, span, near_lanes(half, step)]
            dst = r4.at[number, half, way]
        index = level * 4 + half * 2 + way
        return remote(
            src, dst, p_send.at[number, index], p_recv.at[number, index], neighbour(axis, step)
        )

    def scatter_start(chunk, level):
        each(lambda half, way: scatter_copy(chunk, level, half, way).start())

    def mine(half):
        return lanes(half * WIDE + x * QUAD + z * HALF, HALF)

    def scatter_step(number, level):
        chunk, span = number // PARTS, within(number)
        for half in (0, 1):
            if level % 2 == 1:
                for way in (0, 1):
                    scatter_copy(number, level, half, way).wait_recv()
            if level % 2 == 0:
                for way in (0, 1):
                    scatter_copy(number, level, half, way).wait_recv()
                    cols = (far_lanes if level == 0 else near_lanes)(half, WAYS[way])
                    some = within(number, way)
                    landed = (r1 if level == 0 else r3)[number, half, :, half_of(way), :]
                    total = wide(pbuf[chunk, :, some, cols]) + wide(landed)
                    pbuf[chunk, :, some, cols] = total.astype(jnp.bfloat16)
                    scatter_copy(number, level + 1, half, way).start()
            elif level == 1:
                cols = far_lanes(half, 0)
                total = (
                    wide(pbuf[chunk, :, span, cols])
                    + wide(r2[number, half, 0])
                    + wide(r2[number, half, 1])
                )
                pbuf[chunk, :, span, cols] = total.astype(jnp.bfloat16)
                for way in (0, 1):
                    scatter_copy(number, 2, half, way).start()
            else:
                total = (
                    wide(pbuf[chunk, :, span, near_lanes(half, 0)])
                    + wide(r4[number, half, 0])
                    + wide(r4[number, half, 1])
                )
                total = wide(xbuf[chunk, :, span, mine(half)]) + total
                to = pl.ds(pl.multiple_of(number * high, high), high)
                obuf[to, half * HALF : (half + 1) * HALF] = total.astype(jnp.bfloat16).reshape(
                    high, HALF
                )
        if level == 3:
            for k in range(CHUNKS):
                @pl.when(number == k)
                def _():
                    for tz in range(SIDE):
                        at = (tz * SIDE + k // PARTS) * (rows + 1) + (k % PARTS) * part_rows
                        of = k * high + tz * part_rows
                        nbuf[at : at + part_rows, :] = obuf[of : of + part_rows, :]

    def scatter_sent(chunk, level):
        each(lambda half, way: scatter_copy(chunk, level, half, way).wait_send())

    first = 2 * (jnp.maximum(me - 8, 0) // 2)

    def mask():
        span = WINDOW * rows
        near = lanes((me // 2) * (2 * rows), 2 * rows)
        part = segment_ref[:, near].astype(jnp.float32)
        turned = jnp.transpose(jnp.broadcast_to(part, (2 * rows, 2 * rows)))
        query_seg = jnp.where(me % 2 == 1, turned[rows:], turned[:rows])[:, :1]
        key_seg = segment_ref[:, lanes(first * rows, span)].astype(jnp.float32)
        query_pos = me * rows + lax.broadcasted_iota(jnp.int32, (rows, span), 0)
        key_pos = first * rows + lax.broadcasted_iota(jnp.int32, (rows, span), 1)
        allowed = (key_pos <= query_pos) & (query_seg == key_seg)
        bias[...] = jnp.where(allowed, 0.0, -jnp.inf)

    def prefill(piece):
        @pl.loop(0, heads)
        def _(i):
            head = piece * heads + i

            def joined(base):
                cols = lanes(base + head * HD, HD)
                return jnp.concatenate(
                    [
                        pbuf[(first + b) // SIDE, (first + b) % SIDE, :, cols]
                        for b in range(WINDOW)
                    ],
                    axis=0,
                )

            keys, values = joined(0), joined(width)
            for j in range(group):
                cols = lanes((head * group + j) * HD, HD)
                scores = lax.dot_general(
                    qbuf[:, cols],
                    keys,
                    (((1,), (1,)), ((), ())),
                    preferred_element_type=jnp.float32,
                )
                scores = scores * scale + bias[...]
                top = jnp.max(scores, axis=-1, keepdims=True)
                weights = jnp.exp(scores - top).astype(jnp.bfloat16)
                total = jnp.sum(wide(weights), axis=-1, keepdims=True)
                summed = jnp.dot(weights, values, preferred_element_type=jnp.float32)
                to = pl.ds(pl.multiple_of(x * rows, rows), rows)
                abuf[to, cols] = (summed / total).astype(jnp.bfloat16)

    def decode():
        query = wide(incoming[0])
        for t in range(1, PEERS):
            query = query + wide(incoming[t])
        query = query.astype(jnp.bfloat16)
        count = 2 * tall

        def cached(base):
            return pbuf[0:2, :, :, WIDE + base : WIDE + base + HD].reshape(count, HD)

        owner = lax.broadcasted_iota(jnp.int32, (H, count), 0) // group
        scores = jnp.zeros((H, count), jnp.float32)
        for head in range(KVH):
            part = lax.dot_general(
                query,
                cached(head * HD),
                (((1,), (1,)), ((), ())),
                preferred_element_type=jnp.float32,
            )
            scores = jnp.where(owner == head, part, scores)
        visible = lax.broadcasted_iota(jnp.int32, (H, count), 1) < length_ref[0]
        scores = jnp.where(visible, scores * scale, -jnp.inf)
        top = jnp.max(scores, axis=-1, keepdims=True)
        weights = jnp.exp(scores - top).astype(jnp.bfloat16)
        total = jnp.sum(wide(weights), axis=-1, keepdims=True)
        owner = lax.broadcasted_iota(jnp.int32, (H, HD), 0) // group
        summed = jnp.zeros((H, HD), jnp.float32)
        for head in range(KVH):
            part = jnp.dot(
                weights, cached(width + head * HD), preferred_element_type=jnp.float32
            )
            summed = jnp.where(owner == head, part, summed)
        own[...] = summed / total

    def project(other):
        total = wide(rbuf[other]) + jnp.dot(
            abuf[...], wbuf[other], preferred_element_type=jnp.float32
        )
        value = total.astype(jnp.bfloat16)
        for half in (0, 1):
            to = lanes(half * WIDE + x * QUAD + other * HALF, HALF)
            part = value[:, half * HALF : (half + 1) * HALF]
            for chunk in range(SIDE):
                xbuf[chunk, z, :, to] = part[chunk * rows : (chunk + 1) * rows]
            xdec[:, to] = part[tall:]

    def scaled(read, owner, write):
        total = jnp.zeros((SUB, HALF), jnp.float32)
        for block in range(D // HALF):
            value = wide(read(slice(block * HALF, (block + 1) * HALF)))
            total = total + value * value
        inverse = lax.rsqrt(jnp.sum(total, axis=-1, keepdims=True) / D + epsilon)
        for block in range(D // HALF):
            cols = slice(block * HALF, (block + 1) * HALF)
            gain = gbuf[3:4, cols]
            for k in (2, 1, 0):
                gain = jnp.where(owner == k, gbuf[k : k + 1, cols], gain)
            write(cols, (wide(read(cols)) * inverse * gain).astype(jnp.bfloat16))

    def owners(base):
        part = tbase[:, lanes(base, HALF)].astype(jnp.float32)
        return jnp.transpose(jnp.broadcast_to(part, (HALF, HALF)))

    def normalize(number):
        chunk = number // PARTS
        for q in range(high // HALF):
            tbuf[q * HALF : (q + 1) * HALF, :] = owners(number * high + q * HALF)

        @pl.loop(0, high // SUB)
        def _(t):
            per = part_rows // SUB
            base = (number % PARTS) * part_rows + (t % per) * SUB
            span = pl.ds(pl.multiple_of(base, SUB), SUB)
            to = pl.ds(pl.multiple_of(t * SUB, SUB), SUB)

            def write(cols, value):
                normed[to, cols] = value

            scaled(lambda cols: xbuf[chunk, t // per, span, cols], tbuf[to, :], write)

    def normalize_dec():
        def write(cols, value):
            normed[high : high + SUB, cols] = value

        scaled(lambda cols: xdec[:, cols], owners(PEERS * rows)[:SUB], write)

    def lift(tile, size):
        cols = slice(tile * size, (tile + 1) * size)
        gate = jnp.dot(normed[...], wg_ref[:, cols], preferred_element_type=jnp.float32)
        up = jnp.dot(normed[...], wu_ref[:, cols], preferred_element_type=jnp.float32)
        hidden[:, cols] = (gate / (1.0 + jnp.exp(-gate)) * up).astype(jnp.bfloat16)

    def lower(number):
        @pl.loop(0, D // QUAD)
        def _(i):
            base = jnp.where(i % 2 == 0, z, x)
            tile = (i % 2) * SIDE + (base + 2 - i // 2 + SIDE) % SIDE
            cols = lanes(tile * QUAD, QUAD)
            part = jnp.dot(hidden[...], wd_ref[:, cols], preferred_element_type=jnp.float32)
            part = part.astype(jnp.bfloat16)
            pbuf[number // PARTS, :, within(number), cols] = part[:high].reshape(
                SIDE, part_rows, QUAD
            )

            @pl.when(i == 1)
            def _():
                scatter_start(number, 0)

            @pl.when(number == 0)
            def _():
                for i in range(SIDE):
                    piece = part[high:, i * HALF : (i + 1) * HALF]

                    @pl.when(tile < SIDE)
                    def _():
                        pdec[tile * SIDE + i, :, :HALF] = piece

                    @pl.when(tile >= SIDE)
                    def _():
                        pdec[i * SIDE + tile - SIDE, :, HALF:] = piece

    barrier = pltpu.get_barrier_semaphore()

    @pl.loop(1, PEERS)
    def _(k):
        pl.semaphore_signal(barrier, inc=1, device_id={"tok": ahead(k)}, device_id_type=MESH)

    @pl.loop(1, groups)
    def _(k):
        pl.semaphore_signal(
            barrier, inc=1, device_id={"grp": lax.rem(grp + k, groups)}, device_id_type=MESH
        )

    def local(src, dst, index):
        copy = pltpu.make_async_copy(src, dst, w_sem.at[index])
        copy.start()
        return copy

    fetch_pair = local(pair_hbm, pbuf.at[z, x, :, pl.ds(0, WIDE)], 5)
    fetch_query = local(query_hbm, qbuf, 6)
    fetch = local(cache_hbm, pbuf.at[0:2, :, :, pl.ds(WIDE, WIDE)], 0)
    for head in range(H):
        own[head : head + 1, :] = wide(dec_ref[:, head * HD : (head + 1) * HD])
    column[grp] = own[...].astype(jnp.bfloat16)
    fetch_pair.wait()
    pl.semaphore_wait(barrier, PEERS + groups - 2)

    @pl.loop(1, groups)
    def _(k):
        group_copy(k, False).start()

    gather_start(k_args, 0, 0)
    for way in (0, 1):
        wz_copy(0, way, False).start()
    for piece in range(1, PIECES):
        gather_start(k_args, piece, 0)
    fetch_wo = local(wo_hbm, wbuf.at[z], 4)
    fetch_base = local(resid_hbm, obuf, 8)
    mask()
    near_order = ((0, 0), (1, 0), (0, 1), (2, 0), (1, 1), (3, 0), (2, 1), (3, 1))
    for piece, level in near_order:
        gather_step(k_args, piece, level)

    @pl.loop(1, groups)
    def _(k):
        group_copy(k, True).wait_recv()

    @pl.loop(0, PEERS)
    def _(t):
        request = request_ref[grp * PEERS + t]
        row = column[request // PEERS]
        held = request % PEERS == me
        outgoing[t] = jnp.where(held, wide(row), 0.0).astype(jnp.bfloat16)

    @pl.loop(1, PEERS)
    def _(k):
        query_copy(k, False).start()

    incoming[me] = outgoing[me]
    fetch_query.wait()

    def wo_along_y(other):
        for way in (0, 1):
            wy_copy(other, 0, way, True).wait_recv()
            wy_copy(other, 1, way, False).start()
            wc_copy(other, -WAYS[way], False).start()

    def wo_to_core(other):
        for way in (0, 1):
            wy_copy(other, 1, way, True).wait_recv()
        wc_copy(other, 2, False).start()

    def attend(piece):
        gather_step(k_args, piece, 3)
        prefill(piece)
        for way in (0, 1):
            a_copy(piece, 0, way, False).start()

    def pass_on(piece):
        for way in (0, 1):
            a_copy(piece, 0, way, True).wait_recv()
            a_copy(piece, 1, way, False).start()

    gather_step(k_args, 0, 2)
    for way in (0, 1):
        wz_copy(0, way, True).wait_recv()
    for way in (0, 1):
        wz_copy(1, way, False).start()
    for other in (1, 3):
        for way in (0, 1):
            wy_copy(other, 0, way, False).start()
        wc_copy(other, 0, False).start()
    gather_step(k_args, 1, 2)
    attend(0)
    for way in (0, 1):
        wz_copy(1, way, True).wait_recv()
    for way in (0, 1):
        wy_copy(2, 0, way, False).start()
    wc_copy(2, 0, False).start()
    gather_step(k_args, 2, 2)
    attend(1)
    pass_on(0)
    gather_step(k_args, 3, 2)
    fetch_base.wait()
    tbase[...] = jnp.zeros_like(tbase)
    for t in range(PEERS):
        for part in range(PARTS):
            at = ((t % SIDE) * PARTS + part) * high + (t // SIDE) * part_rows
            of = t * (rows + 1) + part * part_rows
            tbase[:, at : at + part_rows] = tenant_ref[:, of : of + part_rows]
        at, of = PEERS * rows + t, t * (rows + 1) + rows
        tbase[:, at : at + 1] = tenant_ref[:, of : of + 1]
        first_row = t * (rows + 1)
        nbuf[t * rows : (t + 1) * rows, :] = obuf[first_row : first_row + rows, :]
        own_row = wide(obuf[first_row + rows : first_row + rows + 1, :])
        ndec[t : t + 1, :] = own_row
    nbuf[PEERS * rows :, :] = ndec[...].astype(jnp.bfloat16)
    rbuf[z, 0:tall, :] = nbuf[pl.ds(pl.multiple_of(z * tall, tall), tall), :]
    rbuf[z, tall:, :] = nbuf[PEERS * rows :, :]
    for k in (1, 2, 3):
        for copy in base_copies(k, False):
            copy.start()
    attend(2)
    pass_on(1)
    wo_along_y(1)
    wo_along_y(3)
    attend(3)
    pass_on(2)
    fetch.wait()

    @pl.loop(1, PEERS)
    def _(k):
        query_copy(k, True).wait_recv()

    decode()

    @pl.loop(1, PEERS)
    def _(k):
        dec_copy(k, False).start()

    dbuf[me] = own[...]

    wo_along_y(2)

    @pl.loop(0, PEERS)
    def _(t):
        tz, tx = t // SIDE, t % SIDE
        for half in (0, 1):
            source = lanes(t * BLOCK + half * HALF, HALF)
            inside = lanes(half * WIDE + tx * QUAD + tz * HALF, HALF)
            place = t * HALF if half == 0 else WIDE + tx * QUAD + tz * HALF
            target = lanes(place, HALF)
            pltpu.make_async_copy(wg_hbm.at[source, :], wg_ref.at[inside, :], w_sem.at[1]).start()
            pltpu.make_async_copy(wu_hbm.at[source, :], wu_ref.at[inside, :], w_sem.at[2]).start()
            pltpu.make_async_copy(wd_hbm.at[:, source], wd_ref.at[:, target], w_sem.at[3]).start()
            pltpu.make_async_copy(gain_hbm.at[:, source], gbuf.at[:, inside], w_sem.at[7]).start()

    pass_on(3)
    wo_to_core(1)
    wo_to_core(3)

    @pl.loop(1, PEERS)
    def _(k):
        dec_copy(k, True).wait_recv()

    for head in range(H):
        abuf[tall : tall + SUB, head * HD : (head + 1) * HD] = dbuf[:, head, :].astype(
            jnp.bfloat16
        )
    for k in (1, 2, 3):
        for copy in base_copies(k, True):
            copy.wait_recv()
    for piece in range(PIECES):
        for way in (0, 1):
            a_copy(piece, 1, way, True).wait_recv()
    fetch_wo.wait()
    pltpu.make_async_copy(gbuf, gbuf, w_sem.at[7]).wait()

    for other in (0, 1, 3, 2):
        if other > 0:
            for offset in (-1, 0, 1, 2):
                wc_copy(other, offset, True).wait_recv()
        project(hop(z, other))
        if other == 0:
            wo_to_core(2)

    for k in (1, 2, 3):
        for copy in xdec_copies(k, False):
            copy.start()

    @pl.loop(0, CHUNKS)
    def _(number):
        gather_start(x_args, number, 0)

    @pl.loop(0, PIECES)
    def _(piece):
        for level in range(4):
            gather_sent(k_args, piece, level)

    for k in (1, 2, 3):
        for copy in base_copies(k, False):
            copy.wait_send()
    size = 256

    @pl.loop(0, CHUNKS + 8)
    def _(turn):
        s = turn - 3
        f_on = jnp.logical_and(s >= 1, s < CHUNKS + 1)

        def guarded(number, step, level, args=()):
            @pl.when(jnp.logical_and(number >= 0, number < CHUNKS))
            def _():
                step(*args, number, level)

        def gather(number, level):
            guarded(number, gather_step, level, (x_args,))

        def scatter(number, level):
            guarded(number, scatter_step, level)

        @pl.when(s == 1)
        def _():
            pltpu.make_async_copy(wg_ref, wg_ref, w_sem.at[1]).wait()
            pltpu.make_async_copy(wu_ref, wu_ref, w_sem.at[2]).wait()
            pltpu.make_async_copy(wd_ref, wd_ref, w_sem.at[3]).wait()
            for k in (1, 2, 3):
                for copy in xdec_copies(k, True):
                    copy.wait_recv()
            normalize_dec()

        @pl.when(f_on)
        def _():
            normalize(s - 1)

        gather(s + 3, 0)
        gather(s + 2, 1)
        gather(s + 1, 2)

        @pl.when(f_on)
        def _():
            lift(0, size)

        scatter(s - 5, 3)
        scatter(s - 4, 2)

        @pl.when(f_on)
        def _():
            lift(1, size)

        scatter(s - 3, 1)
        scatter(s - 2, 0)

        @pl.when(f_on)
        def _():
            for tile in range(2, ffw // size):
                lift(tile, size)
            lower(s - 1)

        @pl.when(s == 1)
        def _():
            @pl.loop(1, PEERS)
            def _(k):
                fdec_copy(k, False).start()

        gather(s, 3)

    @pl.loop(1, PEERS)
    def _(k):
        fdec_copy(k, True).wait_recv()

    rdec[me] = pdec[me]
    total = wide(rdec[0])
    for t in range(1, PEERS):
        total = total + wide(rdec[t])
    for half in (0, 1):
        part = wide(xdec[:, mine(half)]) + total[:, half * HALF : (half + 1) * HALF]
        obuf[PEERS * rows : PEERS * rows + SUB, half * HALF : (half + 1) * HALF] = part.astype(
            jnp.bfloat16
        )
    ndec[...] = wide(obuf[PEERS * rows : PEERS * rows + SUB, :])
    for k in range(PEERS):
        at = k * (rows + 1) + rows
        nbuf[at : at + 1, :] = ndec[k : k + 1, :].astype(jnp.bfloat16)
    out_last = pltpu.make_async_copy(nbuf, out_hbm, o_sem.at[0])
    out_last.start()

    @pl.loop(1, groups)
    def _(k):
        group_copy(k, False).wait_send()

    @pl.loop(1, PEERS)
    def _(k):
        query_copy(k, False).wait_send()
        dec_copy(k, False).wait_send()
        fdec_copy(k, False).wait_send()

    for way in (0, 1):
        for level in (0, 1):
            wz_copy(level, way, False).wait_send()
            for other in (1, 2, 3):
                wy_copy(other, level, way, False).wait_send()
            for piece in range(PIECES):
                a_copy(piece, level, way, False).wait_send()
    for other in (1, 2, 3):
        for offset in (-1, 0, 1, 2):
            wc_copy(other, offset, False).wait_send()
        for copy in xdec_copies(other, False):
            copy.wait_send()

    @pl.loop(0, CHUNKS)
    def _(number):
        for level in range(4):
            gather_sent(x_args, number, level)
            scatter_sent(number, level)

    out_last.wait()


def layer_call(length, request, queries, pairs, segment, dec, cache, resid, owner, gains, *weights):
    wo, w_gate, w_up, w_down = weights
    rows = queries.shape[0]
    tall = SIDE * rows
    inner = rows // PARTS
    high = SIDE * inner
    ffw = w_gate.shape[1]
    groups = lax.axis_size("grp")
    vmem = pl.BlockSpec(memory_space=pltpu.VMEM)
    smem = pl.BlockSpec(memory_space=pltpu.SMEM)
    hbm = pl.BlockSpec(memory_space=pl.ANY)
    bf16 = jnp.bfloat16
    dma = pltpu.SemaphoreType.DMA
    pairs_of = lambda *shape: [dma(shape), dma(shape)]
    return pl.pallas_call(
        layer_kernel,
        out_shape=jax.ShapeDtypeStruct(resid.shape, bf16),
        in_specs=[smem, smem, hbm, hbm, vmem, vmem, hbm, hbm, vmem] + [hbm] * 5,
        out_specs=hbm,
        scratch_shapes=[
            pltpu.VMEM(queries.shape, bf16),
            pltpu.VMEM(gains.shape, jnp.float32),
            pltpu.VMEM(resid.shape, bf16),
            pltpu.VMEM(resid.shape, bf16),
            pltpu.VMEM((PEERS, BLOCK), jnp.float32),
            pltpu.VMEM((1, resid.shape[0] + HALF - SUB), jnp.int32),
            pltpu.VMEM((tall + SUB, D), bf16),
            pltpu.VMEM((SIDE, D, BLOCK), bf16),
            pltpu.VMEM((SIDE, SIDE, rows, D), bf16),
            pltpu.VMEM((SIDE, SIDE, rows, D), bf16),
            pltpu.VMEM((high + SUB, D), bf16),
            pltpu.VMEM((high + SUB, ffw), bf16),
            pltpu.VMEM((CHUNKS, 2, SIDE, inner, QUAD), bf16),
            pltpu.VMEM((CHUNKS, 2, 2, SIDE, inner, QUAD), bf16),
            pltpu.VMEM((CHUNKS, 2, SIDE, inner, HALF), bf16),
            pltpu.VMEM((CHUNKS, 2, 2, SIDE, inner, HALF), bf16),
            pltpu.VMEM(w_gate.shape, bf16),
            pltpu.VMEM(w_up.shape, bf16),
            pltpu.VMEM(w_down.shape, bf16),
            pltpu.VMEM((rows, WINDOW * rows), jnp.float32),
            pltpu.VMEM((high, HALF), jnp.float32),
            pltpu.VMEM((groups, H, HD), bf16),
            pltpu.VMEM((PEERS, H, HD), bf16),
            pltpu.VMEM((PEERS, H, HD), bf16),
            pltpu.VMEM((H, HD), jnp.float32),
            pltpu.VMEM((PEERS, H, HD), jnp.float32),
            pltpu.VMEM((SIDE, tall + SUB, BLOCK), bf16),
            pltpu.VMEM((SUB, D), bf16),
            pltpu.VMEM((PEERS, SUB, BLOCK), bf16),
            pltpu.VMEM((PEERS, SUB, BLOCK), bf16),
            dma((10,)),
            dma((CHUNKS + 1,)),
            *pairs_of(PIECES, 16),
            *pairs_of(groups),
            *pairs_of(PEERS),
            *pairs_of(PEERS),
            *pairs_of(PIECES, 4),
            *pairs_of(4),
            *pairs_of(12),
            *pairs_of(12),
            *pairs_of(8),
            *pairs_of(8),
            *pairs_of(CHUNKS, 16),
            *pairs_of(CHUNKS, 16),
            *pairs_of(PEERS),
        ],
        compiler_params=pltpu.CompilerParams(
            collective_id=1, has_side_effects=True, vmem_limit_bytes=67043328
        ),
        name="layer",
    )(length, request, queries, pairs, segment, dec, cache, resid, owner, gains, *weights)


def shards(
    pre_q,
    pre_kv,
    pre_segment,
    dec_q,
    cache,
    cache_len,
    slot_request,
    resid,
    wo,
    tenant,
    norm_gain,
    w_gate,
    w_up,
    w_down,
):
    return layer_call(
        cache_len,
        slot_request,
        pre_q,
        pre_kv,
        pre_segment,
        dec_q,
        cache.reshape(2, SIDE, -1, cache.shape[2]),
        resid,
        tenant,
        norm_gain,
        wo,
        w_gate,
        w_up,
        w_down,
    )


def solution(mesh):
    in_specs = (
        P(("grp", "tok"), None),
        P(("grp", "tok"), None),
        P("grp", None),
        P(("grp", "tok"), None),
        P(("grp", "tok"), None, None),
        P(("grp", "tok")),
        P(),
        P("grp", "tok"),
        P(None, "tok"),
        P("grp", None),
        P(),
        P(None, "tok"),
        P(None, "tok"),
        P("tok", None),
    )
    out_specs = P("grp", "tok")
    return jax.shard_map(shards, mesh=mesh, in_specs=in_specs, out_specs=out_specs, check_vma=False)
```
